32 devices in a mesh: dp: 8 (over y, x, core), mp: 4 (over z).
Axes of the slice: x: 2, y: 2, z: 4, core: 2. Of those that a mesh axis runs over, the one named last changes fastest.
Arguments:
- decoder_in: bfloat16 [8192, 768], P(('dp', 'mp')), may hold values from -6 to 6
- encoder_out: bfloat16 [4096, 768], P(('dp', 'mp')), may hold values from -6 to 6
- seq_lengths: int32 [8], P('dp'), may hold values from 1 to 1024, 6144 in all
- rel_buckets: int32 [1024], replicated, may hold values from 0 to 31, as said below
- norm_gains: bfloat16 [3, 768], replicated, may hold values from 0.5 to 1.5
- rel_bias: bfloat16 [32, 12], P(None, 'mp'), may hold values from -4 to 4
- self_query: bfloat16 [768, 768], P('dp', 'mp'), may hold values from -0.0546875 to 0.0546875
- self_key: bfloat16 [768, 768], P('dp', 'mp'), may hold values from -0.21875 to 0.21875
- self_value: bfloat16 [768, 768], P('dp', 'mp'), may hold values from -0.21875 to 0.21875
- self_out: bfloat16 [768, 768], P('mp', 'dp'), may hold values from -0.875 to 0.875
- cross_query: bfloat16 [768, 768], P('dp', 'mp'), may hold values from -0.0546875 to 0.0546875
- cross_key: bfloat16 [768, 768], P('dp', 'mp'), may hold values from -0.21875 to 0.21875
- cross_value: bfloat16 [768, 768], P('dp', 'mp'), may hold values from -0.21875 to 0.21875
- cross_out: bfloat16 [768, 768], P('mp', 'dp'), may hold values from -0.875 to 0.875
- gate_weight: bfloat16 [768, 2048], P('dp', 'mp'), may hold values from -0.21875 to 0.21875
- up_weight: bfloat16 [768, 2048], P('dp', 'mp'), may hold values from -0.21875 to 0.21875
- down_weight: bfloat16 [2048, 768], P('mp', 'dp'), may hold values from -0.125 to 0.125
- out_grad: bfloat16 [8192, 768], P(('dp', 'mp')), may hold values from -6 to 6
Outputs:
- layer_out: bfloat16 [8192, 768], P(('dp', 'mp'))
- decoder_grad: float32 [8192, 768], P(('dp', 'mp'))
- encoder_grad: float32 [4096, 768], P(('dp', 'mp'))
- gains_grad: float32 [3, 768], replicated
- bias_grad: float32 [32, 12], replicated
- self_query_grad: float32 [768, 768], P('dp', 'mp')
- self_key_grad: float32 [768, 768], P('dp', 'mp')
- self_value_grad: float32 [768, 768], P('dp', 'mp')
- self_out_grad: float32 [768, 768], P('mp', 'dp')
- cross_query_grad: float32 [768, 768], P('dp', 'mp')
- cross_key_grad: float32 [768, 768], P('dp', 'mp')
- cross_value_grad: float32 [768, 768], P('dp', 'mp')
- cross_out_grad: float32 [768, 768], P('mp', 'dp')
- gate_grad: float32 [768, 2048], P('dp', 'mp')
- up_grad: float32 [768, 2048], P('dp', 'mp')
- down_grad: float32 [2048, 768], P('mp', 'dp')
The draws below stay inside these ranges and needn't reach their ends.
Inputs may be any that keep to these rules, and one draw needn't show every extreme that they name: `seq_lengths`: the largest length is exactly 1024; the lengths sum to 6144. `rel_buckets`: Non-decreasing in the distance; equal to the distance below 16; equal to 31 from distance 128 on.
All inputs are finite; a program needn't handle non-finite values. No bound on the sum of `seq_lengths` on one device may be relied on, other than what follows from the above.
Results may differ from the reference program's by a relative error of at most 0.04.
Values may be sent and summed in bfloat16 or wider, within the bound.
A program may use at most 576 MiB of HBM per device.

```python
import math
import jax
import jax.numpy as jnp
import numpy as np
from jax import lax

D = 768
H = 12
HD = 64
FF = 2048
NB = 32
MAX_DIST = 128
SLOT = 1024
ENC_LEN = 512
SEQS = 8
TOKENS = 8192
ENC_TOKENS = 4096


def draw_rel_buckets(key, part):
    half = NB // 2
    picks = jax.random.permutation(key, MAX_DIST - half)[:half - 1] + half + 1
    bounds = jnp.sort(picks.astype(jnp.int32))
    distance = jnp.arange(SLOT, dtype=jnp.int32)
    far = half + jnp.sum((bounds[None, :] <= distance[:, None]).astype(jnp.int32), axis=1)
    return jnp.where(distance < half, distance, far).astype(jnp.int32)


def block_levels(key, shape, split, low, high):
    def one(axis_at, shards_of):
        heights = jax.random.uniform(jax.random.fold_in(jax.random.fold_in(key, 6), axis_at), (shards_of,), jnp.float32, low / len(split), high / len(split))
        return jnp.repeat(jnp.exp(heights), shape[axis_at] // shards_of).reshape((-1,) + (1,) * (len(shape) - axis_at - 1))

    loudness = one(*split[0])
    for cut in split[1:]:
        loudness = loudness * one(*cut)
    return loudness


def split_up(number_of, total, limit, lean):
    portions = [(1 << 20) // math.isqrt(standing ** lean) + 1 for standing in range(2, number_of + 1)]
    spare, given = total - limit - (number_of - 1), [1] * (number_of - 1)
    while spare > 0:
        movable = [i for i in range(number_of - 1) if given[i] < limit]
        mass, remaining = sum([portions[i] for i in movable]), spare
        for i in movable:
            addition = min(limit - given[i], max(1, remaining * portions[i] // mass), spare)
            given[i] = given[i] + addition
            spare = spare - addition
    return np.array([limit] + given)


def uneven_parts(stream_key, number_of, total, reach, slope):
    if number_of == 2:
        one = jax.random.randint(stream_key, (), max(1, total - reach), min(reach, total - 1) + 1)
        return jnp.stack([one, total - one])
    sizes = jnp.asarray(split_up(number_of, total, reach, slope), jnp.int32)
    pairs = (number_of - 1) // 2
    donor, sink = sizes[1:1 + 2 * pairs:2], sizes[2:2 + 2 * pairs:2]
    margin = jnp.minimum(donor - 1, reach - sink)
    shifted = jax.random.randint(jax.random.fold_in(stream_key, 1), (pairs,), 0, 1 << 20) % (margin + 1)
    sizes = sizes.at[1:1 + 2 * pairs:2].set(donor - shifted).at[2:2 + 2 * pairs:2].set(sink + shifted)
    return sizes[jax.random.permutation(jax.random.fold_in(stream_key, 2), number_of)]


def centred(rng, extent, scale, reach, cuts=(), kind=jnp.bfloat16):
    array = jax.random.normal(rng, extent, jnp.float32) * scale
    if len(cuts) > 0:
        array = block_levels(rng, extent, cuts, -0.22, 0.18) * array
    return jnp.clip(array, min=-reach, max=reach).astype(kind)


def setup_inputs(seed: int = 0) -> dict:
    streams_of = jax.random.split(jax.random.key(seed), 19)
    return {
        "decoder_in": centred(streams_of[0], (TOKENS, D), 1.0, 6.0, ((0, 32),)),
        "encoder_out": centred(streams_of[1], (ENC_TOKENS, D), 1.0, 6.0, ((0, 32),)),
        "seq_lengths": uneven_parts(streams_of[2], SEQS, SEQS * SLOT * 3 // 4, SLOT, 1).astype(jnp.int32),
        "rel_buckets": draw_rel_buckets(jax.random.fold_in(streams_of[18], 71), 0),
        "norm_gains": jnp.clip(1.0 + 0.1 * jax.random.normal(streams_of[4], (3, D), jnp.float32), 0.5, 1.5).astype(jnp.bfloat16),
        "rel_bias": centred(streams_of[5], (NB, H), 1.0, 4.0, ((1, 4),)),
        "self_query": centred(streams_of[6], (D, H * HD), (16 * D) ** -0.5, 0.0546875, ((0, 8), (1, 4))),
        "self_key": centred(streams_of[7], (D, H * HD), D ** -0.5, 0.21875, ((0, 8), (1, 4))),
        "self_value": centred(streams_of[8], (D, H * HD), D ** -0.5, 0.21875, ((0, 8), (1, 4))),
        "self_out": centred(streams_of[9], (H * HD, D), (H * HD // 16) ** -0.5, 0.875, ((0, 4), (1, 8))),
        "cross_query": centred(streams_of[10], (D, H * HD), (16 * D) ** -0.5, 0.0546875, ((0, 8), (1, 4))),
        "cross_key": centred(streams_of[11], (D, H * HD), D ** -0.5, 0.21875, ((0, 8), (1, 4))),
        "cross_value": centred(streams_of[12], (D, H * HD), D ** -0.5, 0.21875, ((0, 8), (1, 4))),
        "cross_out": centred(streams_of[13], (H * HD, D), (H * HD // 16) ** -0.5, 0.875, ((0, 4), (1, 8))),
        "gate_weight": centred(streams_of[14], (D, FF), D ** -0.5, 0.21875, ((0, 8), (1, 4))),
        "up_weight": centred(streams_of[15], (D, FF), D ** -0.5, 0.21875, ((0, 8), (1, 4))),
        "down_weight": centred(streams_of[16], (FF, D), FF ** -0.5, 0.125, ((0, 4), (1, 8))),
        "out_grad": centred(streams_of[17], (TOKENS, D), 1.0, 6.0, ((0, 32),)),
    }


@jax.custom_vjp
def low(v):
    return lax.optimization_barrier(v.astype(jnp.bfloat16)).astype(jnp.float32)

@jax.custom_vjp
def low_back(v):
    return v

def low_keep(v):
    return (low(v), None)

def low_pass(kept, grad):
    return (grad,)

def back_keep(v):
    return (v, None)

def back_low(kept, grad):
    return (low(grad),)
low.defvjp(low_keep, low_pass)
low_back.defvjp(back_keep, back_low)
epsilon = 1e-06
masked_score = -1e+30
highest = lax.Precision.HIGHEST

def both_ways(value):
    return low_back(low(value))

def rms_norm(value, gain):
    inverse = lax.rsqrt(lax.optimization_barrier(jnp.mean(value * value, axis=-1, keepdims=True)) + epsilon)
    return value * inverse * gain

def heads_first(value):
    return value.reshape(value.shape[0], H, HD).transpose(1, 0, 2)

def attention(query, keys, values, extra, allowed):
    scores = jnp.einsum('hqd,hkd->hqk', heads_first(query), heads_first(keys), precision=highest)
    if extra is not None:
        scores = scores + extra
    scores = low_back(scores)
    if allowed is not None:
        scores = jnp.where(allowed[None], scores, masked_score)
    probs = low(jax.nn.softmax(scores, axis=-1))
    mixed = jnp.einsum('hqk,hkd->hqd', probs, heads_first(values), precision=highest)
    return both_ways(mixed.transpose(1, 0, 2).reshape(query.shape[0], H * HD))

def decoder_layer(params, decoder, encoder, bucket_grid, allowed):
    gain_all, bias_table, s_query, s_key, s_value, s_out, c_query, c_key, c_value, c_out, w_gate, w_up, w_down = params
    first = low(rms_norm(decoder, gain_all[0]))
    query = both_ways(jnp.dot(first, s_query, precision=highest))
    keys = both_ways(jnp.dot(first, s_key, precision=highest))
    values = both_ways(jnp.dot(first, s_value, precision=highest))
    extra = bias_table[bucket_grid].transpose(2, 0, 1)
    mixed = attention(query, keys, values, extra, allowed)
    middle = decoder + low_back(jnp.dot(mixed, s_out, precision=highest))
    second = low(rms_norm(middle, gain_all[1]))
    cross_q = both_ways(jnp.dot(second, c_query, precision=highest))
    cross_k = both_ways(jnp.dot(encoder, c_key, precision=highest))
    cross_v = both_ways(jnp.dot(encoder, c_value, precision=highest))
    mixed_two = attention(cross_q, cross_k, cross_v, None, None)
    later = middle + low_back(jnp.dot(mixed_two, c_out, precision=highest))
    third = low(rms_norm(later, gain_all[2]))
    gate = low_back(jnp.dot(third, w_gate, precision=highest))
    upper = low_back(jnp.dot(third, w_up, precision=highest))
    hidden = low(jax.nn.gelu(gate, approximate=True) * upper)
    return later + low_back(jnp.dot(hidden, w_down, precision=highest))

def reference(decoder_in, encoder_out, seq_lengths, rel_buckets, norm_gains, rel_bias, self_query, self_key, self_value, self_out, cross_query, cross_key, cross_value, cross_out, gate_weight, up_weight, down_weight, out_grad):
    params = tuple((w.astype(jnp.float32) for w in (norm_gains, rel_bias, self_query, self_key, self_value, self_out, cross_query, cross_key, cross_value, cross_out, gate_weight, up_weight, down_weight)))
    decoder = decoder_in.astype(jnp.float32).reshape(SEQS, SLOT, D)
    encoder = encoder_out.astype(jnp.float32).reshape(SEQS, ENC_LEN, D)
    cotangent = out_grad.astype(jnp.float32).reshape(SEQS, SLOT, D)
    position = jnp.arange(SLOT, dtype=jnp.int32)
    distance = jnp.maximum(position[:, None] - position[None, :], 0).astype(jnp.int32)
    bucket_grid = rel_buckets[distance]

    def one_sequence(carry, item):
        dec_seq, enc_seq, length, cot_seq = item
        allowed = (position[None, :] <= position[:, None]) & (position[None, :] < length)
        valid = (position < length).astype(jnp.float32)[:, None]

        def forward(p, d, e):
            return decoder_layer(p, d, e, bucket_grid, allowed)
        result, pullback = jax.vjp(forward, params, dec_seq, enc_seq)
        grads, dec_grad, enc_grad = pullback(cot_seq * valid)
        carry = jax.tree.map(jnp.add, carry, grads)
        return (carry, (result.astype(jnp.bfloat16), dec_grad, enc_grad))
    zeros = jax.tree.map(jnp.zeros_like, params)
    totals, stacked = lax.scan(one_sequence, zeros, (decoder, encoder, seq_lengths, cotangent))
    outputs, dec_grads, enc_grads = stacked
    return (outputs.reshape(TOKENS, D), dec_grads.reshape(TOKENS, D), enc_grads.reshape(ENC_TOKENS, D), totals[0], totals[1], totals[2], totals[3], totals[4], totals[5], totals[6], totals[7], totals[8], totals[9], totals[10], totals[11], totals[12])
```

```python
import functools

import jax
import jax.numpy as jnp
from jax import lax
from jax.experimental import pallas as pl
from jax.experimental.pallas import tpu as pltpu
from jax.sharding import PartitionSpec as P

NB = 32
EPS = 1e-06

F32=jnp.float32; BF16=jnp.bfloat16
NEG=-1e30
NN=(((1,),(0,)),((),())); NT=(((1,),(1,)),((),())); TN=(((0,),(0,)),((),()))
def mm(a,b,dims=NN): return lax.dot_general(a,b,dims,preferred_element_type=F32)
TILE=256

def rows_of(i): return pl.ds(pl.multiple_of(i*TILE,TILE),TILE)

def split_heads(src, dst, heads):
    hd=dst.shape[2]
    for h in range(heads): dst[h]=src[:, h*hd:(h+1)*hd]

def bias_tiles(vecs, tiles, heads):
    key=lax.broadcasted_iota(jnp.int32,(TILE,TILE),0); qry=lax.broadcasted_iota(jnp.int32,(TILE,TILE),1)
    for h in range(heads):
        for d in range(3):
            wide=jnp.broadcast_to(vecs[h*3+d:h*3+d+1,:],(TILE,2*TILE))
            t=pltpu.roll(wide,0,1,stride=1,stride_axis=0)[:,:TILE]
            if d==0: t=jnp.where(qry>=key,t,NEG)
            tiles[h,d]=t

def fwd_attention(q3,k3,v3,vt3,out_t,lse,heads,nq,nk,tiles,kmask):
    hd=q3.shape[2]
    causal=tiles is not None
    def qblock(I,_):
        ri=rows_of(I)
        def kblock(J,carry):
            rj=rows_of(J)
            new=[]
            for h in range(heads):
                m,l,acc=carry[h]
                s=mm(k3[h,rj,:],q3[h,ri,:],NT)
                if causal:
                    s=s+tiles[h,jnp.minimum(I-J,2)]+kmask[rj,:1]
                m2=jnp.maximum(m,jnp.max(s,axis=0,keepdims=True))
                a=jnp.exp(m-m2); p=jnp.exp(s-m2)
                l2=l*a+jnp.sum(p,axis=0,keepdims=True)
                acc2=acc*a+mm(vt3[h,:,rj],p.astype(BF16))
                new.append((m2,l2,acc2))
            return tuple(new)
        init=tuple((jnp.full((1,TILE),NEG,F32),jnp.zeros((1,TILE),F32),jnp.zeros((hd,TILE),F32)) for _ in range(heads))
        res=lax.fori_loop(0,(I+1) if causal else nk//TILE,kblock,init)
        for h in range(heads):
            m,l,acc=res[h]
            out_t[h*hd:(h+1)*hd,ri]=acc/l
            lse[h:h+1,ri]=m+jnp.log(l)
        return 0
    lax.fori_loop(0,nq//TILE,qblock,0)

def bwd_attention(q3,k3,v3,kt3,do3,lse,delta,dqt,dk,dv,heads,nq,nk,tiles,kmask,dtile):
    hd=q3.shape[2]
    causal=tiles is not None
    dqt[...]=jnp.zeros_like(dqt)
    dk[...]=jnp.zeros_like(dk); dv[...]=jnp.zeros_like(dv)
    if causal: dtile[...]=jnp.zeros_like(dtile)
    def kblock(J,_):
        rj=rows_of(J)
        def qblock(I,_):
            ri=rows_of(I)
            for h in range(heads):
                s=mm(k3[h,rj,:],q3[h,ri,:],NT)
                if causal:
                    d=jnp.minimum(I-J,2)
                    s=s+tiles[h,d]+kmask[rj,:1]
                p=jnp.exp(s-lse[h:h+1,ri])
                dp=mm(v3[h,rj,:],do3[h,ri,:],NT)
                ds=(p*(dp-delta[h:h+1,ri])).astype(BF16)
                dv[h,rj,:]+=mm(p.astype(BF16),do3[h,ri,:])
                dk[h,rj,:]+=mm(ds,q3[h,ri,:])
                dqt[h*hd:(h+1)*hd,ri]+=mm(kt3[h,:,rj],ds)
                if causal: dtile[h,d]+=ds.astype(F32)
            return 0
        lax.fori_loop(J if causal else 0,nq//TILE,qblock,0)
        return 0
    lax.fori_loop(0,nk//TILE,kblock,0)

def bias_diag(dtile,out,heads):
    r=lax.broadcasted_iota(jnp.int32,(TILE,TILE),0); c=lax.broadcasted_iota(jnp.int32,(TILE,TILE),1)
    flip=(r+c==TILE-1).astype(F32)
    z=jnp.zeros((TILE,TILE),F32)
    for h in range(heads):
        for d in range(3):
            rev=lax.dot_general(flip,dtile[h,d],NN,precision=lax.Precision.HIGHEST,preferred_element_type=F32)
            t=pltpu.roll(jnp.concatenate([rev,z],axis=1),0,1,stride=1,stride_axis=0)
            out[h*3+d:h*3+d+1,:]=jnp.sum(t,axis=0,keepdims=True)

def fwd_kernel(heads,nq,nk,causal,*refs):
    if causal:
        length,vecs,q,k,v,out,out_t,lse,q3,k3,v3,vt3,tiles,kmask=refs
    else:
        q,k,v,out,out_t,lse,q3,k3,v3,vt3=refs; tiles=kmask=None
    hd=q3.shape[2]
    split_heads(q,q3,heads);split_heads(k,k3,heads);split_heads(v,v3,heads)
    for h in range(heads): vt3[h]=v3[h].T
    if causal:
        bias_tiles(vecs,tiles,heads)
        kmask[...]=jnp.where(lax.broadcasted_iota(jnp.int32,kmask.shape,0)<length[0],0.0,NEG)
    fwd_attention(q3,k3,v3,vt3,out_t,lse,heads,nq,nk,tiles,kmask)
    out[...]=out_t[...].T.astype(BF16)

def bwd_kernel(heads,nq,nk,causal,*refs):
    if causal:
        length,vecs,q,k,v,do,out_t,lse,dq,dk,dv,dvec,q3,k3,v3,kt3,do3,delta,dqt,dk3,dv3,tiles,kmask,dtile=refs
    else:
        q,k,v,do,out_t,lse,dq,dk,dv,q3,k3,v3,kt3,do3,delta,dqt,dk3,dv3=refs; tiles=kmask=dtile=None
    hd=q3.shape[2]
    for s,d in ((q,q3),(k,k3),(v,v3),(do,do3)): split_heads(s,d,heads)
    for h in range(heads): kt3[h]=k3[h].T
    dot=do[...].astype(F32).T
    for h in range(heads):
        delta[h:h+1,:]=jnp.sum(dot[h*hd:(h+1)*hd,:]*out_t[h*hd:(h+1)*hd,:],axis=0,keepdims=True)
    if causal:
        bias_tiles(vecs,tiles,heads)
        kmask[...]=jnp.where(lax.broadcasted_iota(jnp.int32,kmask.shape,0)<length[0],0.0,NEG)
    bwd_attention(q3,k3,v3,kt3,do3,lse,delta,dqt,dk3,dv3,heads,nq,nk,tiles,kmask,dtile)
    dq[...]=dqt[...].T.astype(BF16)
    for h in range(heads):
        dk[:,h*hd:(h+1)*hd]=dk3[h].astype(BF16); dv[:,h*hd:(h+1)*hd]=dv3[h].astype(BF16)
    if causal: bias_diag(dtile,dvec,heads)

V=pl.BlockSpec(memory_space=pltpu.VMEM); S=pl.BlockSpec(memory_space=pltpu.SMEM)
def attention_forward(q,k,v,heads,length=None,vecs=None):
    nq,w=q.shape; nk=k.shape[0]; hd=w//heads; causal=length is not None
    sc=[pltpu.VMEM((heads,nq,hd),BF16)]+[pltpu.VMEM((heads,nk,hd),BF16)]*2+[pltpu.VMEM((heads,hd,nk),BF16)]
    if causal: sc+=[pltpu.VMEM((heads,3,TILE,TILE),F32),pltpu.VMEM((nk,128),F32)]
    outs=[jax.ShapeDtypeStruct((nq,w),BF16),jax.ShapeDtypeStruct((w,nq),F32),jax.ShapeDtypeStruct((heads,nq),F32)]
    args=([length,vecs] if causal else [])+[q,k,v]
    return pl.pallas_call(functools.partial(fwd_kernel,heads,nq,nk,causal),out_shape=outs,
        in_specs=([S,V] if causal else [])+[V]*3,out_specs=[V]*3,scratch_shapes=sc,name="attn_fwd")(*args)
def attention_backward(q,k,v,do,out_t,lse,heads,length=None,vecs=None):
    nq,w=q.shape; nk=k.shape[0]; hd=w//heads; causal=length is not None
    sc=[pltpu.VMEM((heads,nq,hd),BF16)]+[pltpu.VMEM((heads,nk,hd),BF16)]*2+[pltpu.VMEM((heads,hd,nk),BF16),pltpu.VMEM((heads,nq,hd),BF16),
        pltpu.VMEM((heads,nq),F32),pltpu.VMEM((w,nq),F32),pltpu.VMEM((heads,nk,hd),F32),pltpu.VMEM((heads,nk,hd),F32)]
    if causal: sc+=[pltpu.VMEM((heads,3,TILE,TILE),F32),pltpu.VMEM((nk,128),F32),pltpu.VMEM((heads,3,TILE,TILE),F32)]
    outs=[jax.ShapeDtypeStruct((nq,w),BF16),jax.ShapeDtypeStruct((nk,w),BF16),jax.ShapeDtypeStruct((nk,w),BF16)]
    if causal: outs.append(jax.ShapeDtypeStruct((heads*3,2*TILE),F32))
    args=([length,vecs] if causal else [])+[q,k,v,do,out_t,lse]
    return pl.pallas_call(functools.partial(bwd_kernel,heads,nq,nk,causal),out_shape=outs,
        in_specs=([S,V] if causal else [])+[V]*6,out_specs=[V]*len(outs),scratch_shapes=sc,name="attn_bwd")(*args)
def bias_vectors(t):
    h=t.shape[0]; far=t[:,TILE:TILE+1]
    z=jnp.broadcast_to(far,(h,TILE))
    v0=jnp.concatenate([t[:,:TILE],z],1)
    v1=jnp.concatenate([t[:,TILE:2*TILE],t[:,:TILE]],1)
    v2=jnp.concatenate([z,z],1)
    return jnp.stack([v0,v1,v2],1).reshape(h*3,2*TILE)


def full_rows(share):
    return lax.all_gather(share, "mp", axis=0, tiled=True)


def share_rows(total):
    return lax.psum_scatter(total.astype(BF16), "mp", scatter_dimension=0, tiled=True).astype(F32)


def norm_forward(stream, gain, width):
    inverse = lax.rsqrt(jnp.sum(stream * stream, axis=1) / width + EPS)
    return (stream * inverse[:, None] * gain[None, :]).astype(BF16), inverse


def norm_backward(stream, gain, inverse, upstream, width):
    scaled = upstream * gain[None, :]
    dotted = jnp.sum(scaled * stream, axis=1)
    back = inverse[:, None] * scaled - stream * (inverse * inverse * inverse * dotted / width)[:, None]
    return back, jnp.sum(upstream * stream * inverse[:, None], axis=0)


def distance_bias(rel_buckets, rel_bias):
    onehot = (rel_buckets[:, None] == jnp.arange(NB, dtype=jnp.int32)[None, :]).astype(BF16)
    return jnp.dot(onehot, rel_bias, preferred_element_type=F32).T


def bucket_sums(diag, rel_buckets, heads):
    d3 = diag.reshape(heads, 3, 2 * TILE)
    n = rel_buckets.shape[0]
    near = jnp.pad(d3[:, 0, TILE - 1 : 2 * TILE - 1], ((0, 0), (0, n - TILE)))
    next_one = jnp.pad(d3[:, 1, : 2 * TILE - 1], ((0, 0), (1, n - 2 * TILE)))
    by_distance = near + next_one
    far = jnp.sum(d3[:, 2], axis=1)
    onehot = (rel_buckets[:, None] == jnp.arange(NB, dtype=jnp.int32)[None, :]).astype(F32)
    total = jnp.einsum("hn,nb->bh", by_distance, onehot, precision=lax.Precision.HIGHEST)
    last = (jnp.arange(NB, dtype=jnp.int32)[:, None] == rel_buckets[n - 1]).astype(F32)
    return total + last * far[None, :]


def per_device(
    decoder_in, encoder_out, seq_lengths, rel_buckets, norm_gains, rel_bias,
    self_query, self_key, self_value, self_out, cross_query, cross_key, cross_value, cross_out,
    gate_weight, up_weight, down_weight, out_grad,
):
    width = decoder_in.shape[1]
    local_rows = decoder_in.shape[0]
    heads = rel_bias.shape[1]
    gains = norm_gains.astype(F32)
    w = self_query.shape[1]
    f = gate_weight.shape[1]
    part_self = jnp.concatenate([self_query, self_key, self_value, self_out.T], axis=1)
    part_cross = jnp.concatenate([cross_query, cross_key, cross_value, cross_out.T], axis=1)
    part_ff = jnp.concatenate([gate_weight, up_weight, down_weight.T], axis=1)
    full_self = lax.all_gather(part_self, "dp", axis=0, tiled=True)
    full_rest = lax.all_gather(jnp.concatenate([part_cross, part_ff], axis=1), "dp", axis=0, tiled=True)
    w_qkv, w_out = full_self[:, : 3 * w], full_self[:, 3 * w :]
    c_query, c_kv, c_out = full_rest[:, :w], full_rest[:, w : 3 * w], full_rest[:, 3 * w : 4 * w]
    w_gate, w_up, w_down = full_rest[:, 4 * w : 4 * w + f], full_rest[:, 4 * w + f : 4 * w + 2 * f], full_rest[:, 4 * w + 2 * f :]
    vecs = bias_vectors(distance_bias(rel_buckets, rel_bias))
    slot = rel_buckets.shape[0]
    position = lax.axis_index("mp") * local_rows + jnp.arange(local_rows, dtype=jnp.int32)
    valid = (position < seq_lengths[0]).astype(F32)[:, None]

    def dot(a, b, dims=NN):
        return lax.dot_general(a, b, dims, preferred_element_type=F32)

    stream = decoder_in.astype(F32)
    grad = out_grad.astype(F32) * valid
    grad_one = full_rows(grad.astype(BF16))
    enc_full = full_rows(encoder_out)
    first, inverse_one = norm_forward(stream, gains[0], width)
    first = full_rows(first)
    qkv = dot(first, w_qkv).astype(BF16)
    query, keys, values = qkv[:, :w], qkv[:, w : 2 * w], qkv[:, 2 * w :]
    mixed, mixed_t, lse = attention_forward(query, keys, values, heads, seq_lengths, vecs)
    middle = stream + share_rows(dot(mixed, w_out, NT))
    second, inverse_two = norm_forward(middle, gains[1], width)
    second = full_rows(second)
    cross_q = dot(second, c_query).astype(BF16)
    cross_kv = dot(enc_full, c_kv).astype(BF16)
    cross_k, cross_v = cross_kv[:, :w], cross_kv[:, w:]
    mixed_two, mixed_two_t, lse_two = attention_forward(cross_q, cross_k, cross_v, heads)
    later = middle + share_rows(dot(mixed_two, c_out, NT))
    third, inverse_three = norm_forward(later, gains[2], width)
    third = full_rows(third)
    gate = dot(third, w_gate)
    upper = dot(third, w_up)

    def gated(gate_in, up_in):
        return jax.nn.gelu(gate_in, approximate=True) * up_in

    product, gated_back = jax.vjp(gated, gate, upper)
    hidden = product.astype(BF16)
    layer_out = (later + share_rows(dot(hidden, w_down, NT))).astype(BF16)
    d_gate, d_up = gated_back(dot(grad_one, w_down))
    d_gate, d_up = d_gate.astype(BF16), d_up.astype(BF16)
    g_down = dot(grad_one, hidden, TN)
    g_gate = dot(third, d_gate, TN)
    g_up = dot(third, d_up, TN)
    d_third = share_rows(dot(d_gate, w_gate, NT) + dot(d_up, w_up, NT))
    back_three, gain_three = norm_backward(later, gains[2], inverse_three, d_third, width)
    grad = grad + back_three
    grad_two = full_rows(grad.astype(BF16))
    d_mixed_two = dot(grad_two, c_out).astype(BF16)
    g_cout = dot(grad_two, mixed_two, TN)
    d_cq, d_ck, d_cv = attention_backward(cross_q, cross_k, cross_v, d_mixed_two, mixed_two_t, lse_two, heads)
    d_second = share_rows(dot(d_cq, c_query, NT))
    d_ckv = jnp.concatenate([d_ck, d_cv], axis=1)
    encoder_grad = share_rows(dot(d_ckv, c_kv, NT))
    g_cq = dot(second, d_cq, TN)
    g_ckv = dot(enc_full, d_ckv, TN)
    rest = jnp.concatenate([g.astype(BF16) for g in (g_cq, g_ckv, g_cout, g_gate, g_up, g_down)], axis=1)
    rest = lax.psum_scatter(rest, "dp", scatter_dimension=0, tiled=True)
    back_two, gain_two = norm_backward(middle, gains[1], inverse_two, d_second, width)
    grad = grad + back_two
    grad_three = full_rows(grad.astype(BF16))
    d_mixed = dot(grad_three, w_out).astype(BF16)
    g_out = dot(grad_three, mixed, TN)
    d_query, d_keys, d_values, diag = attention_backward(
        query, keys, values, d_mixed, mixed_t, lse, heads, seq_lengths, vecs
    )
    d_qkv = jnp.concatenate([d_query, d_keys, d_values], axis=1)
    d_first = share_rows(dot(d_qkv, w_qkv, NT))
    g_qkv = dot(first, d_qkv, TN)
    own = jnp.concatenate([g_qkv.astype(BF16), g_out.astype(BF16)], axis=1)
    own = lax.psum_scatter(own, "dp", scatter_dimension=0, tiled=True)
    back_one, gain_one = norm_backward(stream, gains[0], inverse_one, d_first, width)
    decoder_grad = grad + back_one
    bias_table = jnp.zeros((NB, heads * lax.axis_size("mp")), F32)
    bias_table = lax.dynamic_update_slice_in_dim(
        bias_table, bucket_sums(diag, rel_buckets, heads), lax.axis_index("mp") * heads, 1
    )
    gains_grad, bias_grad = lax.psum((jnp.stack([gain_one, gain_two, gain_three]), bias_table), ("dp", "mp"))
    own = own.astype(F32)
    rest = rest.astype(F32)
    return (
        layer_out, decoder_grad, encoder_grad, gains_grad, bias_grad,
        own[:, :w], own[:, w : 2 * w], own[:, 2 * w : 3 * w], own[:, 3 * w :].T,
        rest[:, :w], rest[:, w : 2 * w], rest[:, 2 * w : 3 * w], rest[:, 3 * w : 4 * w].T,
        rest[:, 4 * w : 4 * w + f], rest[:, 4 * w + f : 4 * w + 2 * f], rest[:, 4 * w + 2 * f :].T,
    )


def solution(mesh):
    return jax.shard_map(
        per_device,
        mesh=mesh,
        in_specs=(
            P(("dp", "mp"), None),
            P(("dp", "mp"), None),
            P("dp"),
            P(),
            P(),
            P(None, "mp"),
            P("dp", "mp"),
            P("dp", "mp"),
            P("dp", "mp"),
            P("mp", "dp"),
            P("dp", "mp"),
            P("dp", "mp"),
            P("dp", "mp"),
            P("mp", "dp"),
            P("dp", "mp"),
            P("dp", "mp"),
            P("mp", "dp"),
            P(("dp", "mp"), None),
        ),
        out_specs=(
            P(("dp", "mp"), None),
            P(("dp", "mp"), None),
            P(("dp", "mp"), None),
            P(),
            P(),
            P("dp", "mp"),
            P("dp", "mp"),
            P("dp", "mp"),
            P("mp", "dp"),
            P("dp", "mp"),
            P("dp", "mp"),
            P("dp", "mp"),
            P("mp", "dp"),
            P("dp", "mp"),
            P("dp", "mp"),
            P("mp", "dp"),
        ),
        check_vma=False,
    )
```

```python
import functools

import jax
import jax.numpy as jnp
from jax import lax
from jax.experimental import pallas as pl
from jax.experimental.pallas import tpu as pltpu
from jax.sharding import PartitionSpec as P

NB = 32
EPS = 1e-06

F32=jnp.float32; BF16=jnp.bfloat16
NEG=-1e30
NN=(((1,),(0,)),((),())); NT=(((1,),(1,)),((),())); TN=(((0,),(0,)),((),()))
def mm(a,b,dims=NN): return lax.dot_general(a,b,dims,preferred_element_type=F32)
TILE=256

def rows_of(i): return pl.ds(pl.multiple_of(i*TILE,TILE),TILE)

def split_heads(src, dst, heads):
    hd=dst.shape[2]
    for h in range(heads): dst[h]=src[:, h*hd:(h+1)*hd]

def bias_tiles(vecs, tiles, heads):
    key=lax.broadcasted_iota(jnp.int32,(TILE,TILE),0); qry=lax.broadcasted_iota(jnp.int32,(TILE,TILE),1)
    for h in range(heads):
        for d in range(3):
            wide=jnp.broadcast_to(vecs[h*3+d:h*3+d+1,:],(TILE,2*TILE))
            t=pltpu.roll(wide,0,1,stride=1,stride_axis=0)[:,:TILE]
            if d==0: t=jnp.where(qry>=key,t,NEG)
            tiles[h,d]=t

def fwd_attention(q3,k3,v3,vt3,out_t,lse,heads,nq,nk,tiles,kmask):
    hd=q3.shape[2]
    causal=tiles is not None
    def qblock(I,_):
        ri=rows_of(I)
        def kblock(J,carry):
            rj=rows_of(J)
            new=[]
            for h in range(heads):
                m,l,acc=carry[h]
                s=mm(k3[h,rj,:],q3[h,ri,:],NT)
                if causal:
                    s=s+tiles[h,jnp.minimum(I-J,2)]+kmask[rj,:1]
                m2=jnp.maximum(m,jnp.max(s,axis=0,keepdims=True))
                a=jnp.exp(m-m2); p=jnp.exp(s-m2)
                l2=l*a+jnp.sum(p,axis=0,keepdims=True)
                acc2=acc*a+mm(vt3[h,:,rj],p.astype(BF16))
                new.append((m2,l2,acc2))
            return tuple(new)
        init=tuple((jnp.full((1,TILE),NEG,F32),jnp.zeros((1,TILE),F32),jnp.zeros((hd,TILE),F32)) for _ in range(heads))
        res=lax.fori_loop(0,(I+1) if causal else nk//TILE,kblock,init)
        for h in range(heads):
            m,l,acc=res[h]
            out_t[h*hd:(h+1)*hd,ri]=acc/l
            lse[h:h+1,ri]=m+jnp.log(l)
        return 0
    lax.fori_loop(0,nq//TILE,qblock,0)

def bwd_attention(q3,k3,v3,kt3,do3,lse,delta,dqt,dk,dv,heads,nq,nk,tiles,kmask,dtile):
    hd=q3.shape[2]
    causal=tiles is not None
    dqt[...]=jnp.zeros_like(dqt)
    dk[...]=jnp.zeros_like(dk); dv[...]=jnp.zeros_like(dv)
    if causal: dtile[...]=jnp.zeros_like(dtile)
    def kblock(J,_):
        rj=rows_of(J)
        def qblock(I,_):
            ri=rows_of(I)
            for h in range(heads):
                s=mm(k3[h,rj,:],q3[h,ri,:],NT)
                if causal:
                    d=jnp.minimum(I-J,2)
                    s=s+tiles[h,d]+kmask[rj,:1]
                p=jnp.exp(s-lse[h:h+1,ri])
                dp=mm(v3[h,rj,:],do3[h,ri,:],NT)
                ds=(p*(dp-delta[h:h+1,ri])).astype(BF16)
                dv[h,rj,:]+=mm(p.astype(BF16),do3[h,ri,:])
                dk[h,rj,:]+=mm(ds,q3[h,ri,:])
                dqt[h*hd:(h+1)*hd,ri]+=mm(kt3[h,:,rj],ds)
                if causal: dtile[h,d]+=ds.astype(F32)
            return 0
        lax.fori_loop(J if causal else 0,nq//TILE,qblock,0)
        return 0
    lax.fori_loop(0,nk//TILE,kblock,0)

def bias_diag(dtile,out,heads):
    r=lax.broadcasted_iota(jnp.int32,(TILE,TILE),0); c=lax.broadcasted_iota(jnp.int32,(TILE,TILE),1)
    flip=(r+c==TILE-1).astype(F32)
    z=jnp.zeros((TILE,TILE),F32)
    for h in range(heads):
        for d in range(3):
            rev=lax.dot_general(flip,dtile[h,d],NN,precision=lax.Precision.HIGHEST,preferred_element_type=F32)
            t=pltpu.roll(jnp.concatenate([rev,z],axis=1),0,1,stride=1,stride_axis=0)
            out[h*3+d:h*3+d+1,:]=jnp.sum(t,axis=0,keepdims=True)

def fwd_kernel(heads,nq,nk,causal,*refs):
    if causal:
        length,vecs,q,k,v,out,out_t,lse,q3,k3,v3,vt3,tiles,kmask=refs
    else:
        q,k,v,out,out_t,lse,q3,k3,v3,vt3=refs; tiles=kmask=None
    hd=q3.shape[2]
    split_heads(q,q3,heads);split_heads(k,k3,heads);split_heads(v,v3,heads)
    for h in range(heads): vt3[h]=v3[h].T
    if causal:
        bias_tiles(vecs,tiles,heads)
        kmask[...]=jnp.where(lax.broadcasted_iota(jnp.int32,kmask.shape,0)<length[0],0.0,NEG)
    fwd_attention(q3,k3,v3,vt3,out_t,lse,heads,nq,nk,tiles,kmask)
    out[...]=out_t[...].T.astype(BF16)

def bwd_kernel(heads,nq,nk,causal,*refs):
    if causal:
        length,vecs,q,k,v,do,out_t,lse,dq,dk,dv,dvec,q3,k3,v3,kt3,do3,delta,dqt,dk3,dv3,tiles,kmask,dtile,land,sems=refs
        other={"mp": lax.axis_index("mp")^1}
        barrier=pltpu.get_barrier_semaphore()
        pl.semaphore_signal(barrier,inc=1,device_id=other,device_id_type=pl.DeviceIdType.MESH)
        pl.semaphore_wait(barrier,1)
        copy=pltpu.make_async_remote_copy(src_ref=do,dst_ref=land,send_sem=sems.at[0],recv_sem=sems.at[1],device_id=other,device_id_type=pl.DeviceIdType.MESH)
        copy.start()
    else:
        q,k,v,do,out_t,lse,dq,dk,dv,q3,k3,v3,kt3,do3,delta,dqt,dk3,dv3=refs; tiles=kmask=dtile=None
    hd=q3.shape[2]
    for s,d in ((q,q3),(k,k3),(v,v3),(do,do3)): split_heads(s,d,heads)
    for h in range(heads): kt3[h]=k3[h].T
    dot=do[...].astype(F32).T
    for h in range(heads):
        delta[h:h+1,:]=jnp.sum(dot[h*hd:(h+1)*hd,:]*out_t[h*hd:(h+1)*hd,:],axis=0,keepdims=True)
    if causal:
        bias_tiles(vecs,tiles,heads)
        kmask[...]=jnp.where(lax.broadcasted_iota(jnp.int32,kmask.shape,0)<length[0],0.0,NEG)
    bwd_attention(q3,k3,v3,kt3,do3,lse,delta,dqt,dk3,dv3,heads,nq,nk,tiles,kmask,dtile)
    dq[...]=dqt[...].T.astype(BF16)
    for h in range(heads):
        dk[:,h*hd:(h+1)*hd]=dk3[h].astype(BF16); dv[:,h*hd:(h+1)*hd]=dv3[h].astype(BF16)
    if causal:
        bias_diag(dtile,dvec,heads)
        copy.wait()

V=pl.BlockSpec(memory_space=pltpu.VMEM); S=pl.BlockSpec(memory_space=pltpu.SMEM)
def attention_forward(q,k,v,heads,length=None,vecs=None):
    nq,w=q.shape; nk=k.shape[0]; hd=w//heads; causal=length is not None
    sc=[pltpu.VMEM((heads,nq,hd),BF16)]+[pltpu.VMEM((heads,nk,hd),BF16)]*2+[pltpu.VMEM((heads,hd,nk),BF16)]
    if causal: sc+=[pltpu.VMEM((heads,3,TILE,TILE),F32),pltpu.VMEM((nk,128),F32)]
    outs=[jax.ShapeDtypeStruct((nq,w),BF16),jax.ShapeDtypeStruct((w,nq),F32),jax.ShapeDtypeStruct((heads,nq),F32)]
    args=([length,vecs] if causal else [])+[q,k,v]
    return pl.pallas_call(functools.partial(fwd_kernel,heads,nq,nk,causal),out_shape=outs,
        in_specs=([S,V] if causal else [])+[V]*3,out_specs=[V]*3,scratch_shapes=sc,name="attn_fwd")(*args)
def attention_backward(q,k,v,do,out_t,lse,heads,length=None,vecs=None):
    nq,w=q.shape; nk=k.shape[0]; hd=w//heads; causal=length is not None
    sc=[pltpu.VMEM((heads,nq,hd),BF16)]+[pltpu.VMEM((heads,nk,hd),BF16)]*2+[pltpu.VMEM((heads,hd,nk),BF16),pltpu.VMEM((heads,nq,hd),BF16),
        pltpu.VMEM((heads,nq),F32),pltpu.VMEM((w,nq),F32),pltpu.VMEM((heads,nk,hd),F32),pltpu.VMEM((heads,nk,hd),F32)]
    if causal: sc+=[pltpu.VMEM((heads,3,TILE,TILE),F32),pltpu.VMEM((nk,128),F32),pltpu.VMEM((heads,3,TILE,TILE),F32),pltpu.VMEM((nq,w),BF16),pltpu.SemaphoreType.DMA((2,))]
    outs=[jax.ShapeDtypeStruct((nq,w),BF16),jax.ShapeDtypeStruct((nk,w),BF16),jax.ShapeDtypeStruct((nk,w),BF16)]
    if causal: outs.append(jax.ShapeDtypeStruct((heads*3,2*TILE),F32))
    args=([length,vecs] if causal else [])+[q,k,v,do,out_t,lse]
    return pl.pallas_call(functools.partial(bwd_kernel,heads,nq,nk,causal),out_shape=outs,
        in_specs=([S,V] if causal else [])+[V]*6,out_specs=[V]*len(outs),scratch_shapes=sc,name="attn_bwd",compiler_params=pltpu.CompilerParams(collective_id=0,has_side_effects=True) if causal else None)(*args)
def bias_vectors(t):
    h=t.shape[0]; far=t[:,TILE:TILE+1]
    z=jnp.broadcast_to(far,(h,TILE))
    v0=jnp.concatenate([t[:,:TILE],z],1)
    v1=jnp.concatenate([t[:,TILE:2*TILE],t[:,:TILE]],1)
    v2=jnp.concatenate([z,z],1)
    return jnp.stack([v0,v1,v2],1).reshape(h*3,2*TILE)


def full_rows(share):
    return lax.all_gather(share, "mp", axis=0, tiled=True)


def share_rows(total):
    return lax.psum_scatter(total.astype(BF16), "mp", scatter_dimension=0, tiled=True).astype(F32)


def norm_forward(stream, gain, width):
    inverse = lax.rsqrt(jnp.sum(stream * stream, axis=1) / width + EPS)
    return (stream * inverse[:, None] * gain[None, :]).astype(BF16), inverse


def norm_backward(stream, gain, inverse, upstream, width):
    scaled = upstream * gain[None, :]
    dotted = jnp.sum(scaled * stream, axis=1)
    back = inverse[:, None] * scaled - stream * (inverse * inverse * inverse * dotted / width)[:, None]
    return back, jnp.sum(upstream * stream * inverse[:, None], axis=0)


def distance_bias(rel_buckets, rel_bias):
    onehot = (rel_buckets[:, None] == jnp.arange(NB, dtype=jnp.int32)[None, :]).astype(BF16)
    return jnp.dot(onehot, rel_bias, preferred_element_type=F32).T


def bucket_sums(diag, rel_buckets, heads):
    d3 = diag.reshape(heads, 3, 2 * TILE)
    n = rel_buckets.shape[0]
    near = jnp.pad(d3[:, 0, TILE - 1 : 2 * TILE - 1], ((0, 0), (0, n - TILE)))
    next_one = jnp.pad(d3[:, 1, : 2 * TILE - 1], ((0, 0), (1, n - 2 * TILE)))
    by_distance = near + next_one
    far = jnp.sum(d3[:, 2], axis=1)
    onehot = (rel_buckets[:, None] == jnp.arange(NB, dtype=jnp.int32)[None, :]).astype(F32)
    total = jnp.einsum("hn,nb->bh", by_distance, onehot, precision=lax.Precision.HIGHEST)
    last = (jnp.arange(NB, dtype=jnp.int32)[:, None] == rel_buckets[n - 1]).astype(F32)
    return total + last * far[None, :]


def per_device(
    decoder_in, encoder_out, seq_lengths, rel_buckets, norm_gains, rel_bias,
    self_query, self_key, self_value, self_out, cross_query, cross_key, cross_value, cross_out,
    gate_weight, up_weight, down_weight, out_grad,
):
    width = decoder_in.shape[1]
    local_rows = decoder_in.shape[0]
    heads = rel_bias.shape[1]
    gains = norm_gains.astype(F32)
    w = self_query.shape[1]
    f = gate_weight.shape[1]
    part_self = jnp.concatenate([self_query, self_key, self_value, self_out.T], axis=1)
    part_cross = jnp.concatenate([cross_query, cross_key, cross_value, cross_out.T], axis=1)
    part_ff = jnp.concatenate([gate_weight, up_weight, down_weight.T], axis=1)
    full_self = lax.all_gather(part_self, "dp", axis=0, tiled=True)
    full_rest = lax.all_gather(jnp.concatenate([part_cross, part_ff], axis=1), "dp", axis=0, tiled=True)
    w_qkv, w_out = full_self[:, : 3 * w], full_self[:, 3 * w :]
    c_query, c_kv, c_out = full_rest[:, :w], full_rest[:, w : 3 * w], full_rest[:, 3 * w : 4 * w]
    w_gate, w_up, w_down = full_rest[:, 4 * w : 4 * w + f], full_rest[:, 4 * w + f : 4 * w + 2 * f], full_rest[:, 4 * w + 2 * f :]
    vecs = bias_vectors(distance_bias(rel_buckets, rel_bias))
    slot = rel_buckets.shape[0]
    position = lax.axis_index("mp") * local_rows + jnp.arange(local_rows, dtype=jnp.int32)
    valid = (position < seq_lengths[0]).astype(F32)[:, None]

    def dot(a, b, dims=NN):
        return lax.dot_general(a, b, dims, preferred_element_type=F32)

    stream = decoder_in.astype(F32)
    grad = out_grad.astype(F32) * valid
    grad_one = full_rows(grad.astype(BF16))
    enc_full = full_rows(encoder_out)
    first, inverse_one = norm_forward(stream, gains[0], width)
    first = full_rows(first)
    qkv = dot(first, w_qkv).astype(BF16)
    query, keys, values = qkv[:, :w], qkv[:, w : 2 * w], qkv[:, 2 * w :]
    mixed, mixed_t, lse = attention_forward(query, keys, values, heads, seq_lengths, vecs)
    middle = stream + share_rows(dot(mixed, w_out, NT))
    second, inverse_two = norm_forward(middle, gains[1], width)
    second = full_rows(second)
    cross_q = dot(second, c_query).astype(BF16)
    cross_kv = dot(enc_full, c_kv).astype(BF16)
    cross_k, cross_v = cross_kv[:, :w], cross_kv[:, w:]
    mixed_two, mixed_two_t, lse_two = attention_forward(cross_q, cross_k, cross_v, heads)
    later = middle + share_rows(dot(mixed_two, c_out, NT))
    third, inverse_three = norm_forward(later, gains[2], width)
    third = full_rows(third)
    gate = dot(third, w_gate)
    upper = dot(third, w_up)

    def gated(gate_in, up_in):
        return jax.nn.gelu(gate_in, approximate=True) * up_in

    product, gated_back = jax.vjp(gated, gate, upper)
    hidden = product.astype(BF16)
    layer_out = (later + share_rows(dot(hidden, w_down, NT))).astype(BF16)
    d_gate, d_up = gated_back(dot(grad_one, w_down))
    d_gate, d_up = d_gate.astype(BF16), d_up.astype(BF16)
    g_down = dot(grad_one, hidden, TN)
    g_gate = dot(third, d_gate, TN)
    g_up = dot(third, d_up, TN)
    d_third = share_rows(dot(d_gate, w_gate, NT) + dot(d_up, w_up, NT))
    back_three, gain_three = norm_backward(later, gains[2], inverse_three, d_third, width)
    grad = grad + back_three
    grad_two = full_rows(grad.astype(BF16))
    d_mixed_two = dot(grad_two, c_out).astype(BF16)
    g_cout = dot(grad_two, mixed_two, TN)
    d_cq, d_ck, d_cv = attention_backward(cross_q, cross_k, cross_v, d_mixed_two, mixed_two_t, lse_two, heads)
    d_second = share_rows(dot(d_cq, c_query, NT))
    d_ckv = jnp.concatenate([d_ck, d_cv], axis=1)
    encoder_grad = share_rows(dot(d_ckv, c_kv, NT))
    g_cq = dot(second, d_cq, TN)
    g_ckv = dot(enc_full, d_ckv, TN)
    rest = jnp.concatenate([g.astype(BF16) for g in (g_cq, g_ckv, g_cout, g_gate, g_up, g_down)], axis=1)
    rest = lax.psum_scatter(rest, "dp", scatter_dimension=0, tiled=True)
    back_two, gain_two = norm_backward(middle, gains[1], inverse_two, d_second, width)
    grad = grad + back_two
    grad_three = full_rows(grad.astype(BF16))
    d_mixed = dot(grad_three, w_out).astype(BF16)
    g_out = dot(grad_three, mixed, TN)
    d_query, d_keys, d_values, diag = attention_backward(
        query, keys, values, d_mixed, mixed_t, lse, heads, seq_lengths, vecs
    )
    d_qkv = jnp.concatenate([d_query, d_keys, d_values], axis=1)
    d_first = share_rows(dot(d_qkv, w_qkv, NT))
    g_qkv = dot(first, d_qkv, TN)
    own = jnp.concatenate([g_qkv.astype(BF16), g_out.astype(BF16)], axis=1)
    own = lax.psum_scatter(own, "dp", scatter_dimension=0, tiled=True)
    back_one, gain_one = norm_backward(stream, gains[0], inverse_one, d_first, width)
    decoder_grad = grad + back_one
    bias_table = jnp.zeros((NB, heads * lax.axis_size("mp")), F32)
    bias_table = lax.dynamic_update_slice_in_dim(
        bias_table, bucket_sums(diag, rel_buckets, heads), lax.axis_index("mp") * heads, 1
    )
    gains_grad, bias_grad = lax.psum((jnp.stack([gain_one, gain_two, gain_three]), bias_table), ("dp", "mp"))
    own = own.astype(F32)
    rest = rest.astype(F32)
    return (
        layer_out, decoder_grad, encoder_grad, gains_grad, bias_grad,
        own[:, :w], own[:, w : 2 * w], own[:, 2 * w : 3 * w], own[:, 3 * w :].T,
        rest[:, :w], rest[:, w : 2 * w], rest[:, 2 * w : 3 * w], rest[:, 3 * w : 4 * w].T,
        rest[:, 4 * w : 4 * w + f], rest[:, 4 * w + f : 4 * w + 2 * f], rest[:, 4 * w + 2 * f :].T,
    )


def solution(mesh):
    return jax.shard_map(
        per_device,
        mesh=mesh,
        in_specs=(
            P(("dp", "mp"), None),
            P(("dp", "mp"), None),
            P("dp"),
            P(),
            P(),
            P(None, "mp"),
            P("dp", "mp"),
            P("dp", "mp"),
            P("dp", "mp"),
            P("mp", "dp"),
            P("dp", "mp"),
            P("dp", "mp"),
            P("dp", "mp"),
            P("mp", "dp"),
            P("dp", "mp"),
            P("dp", "mp"),
            P("mp", "dp"),
            P(("dp", "mp"), None),
        ),
        out_specs=(
            P(("dp", "mp"), None),
            P(("dp", "mp"), None),
            P(("dp", "mp"), None),
            P(),
            P(),
            P("dp", "mp"),
            P("dp", "mp"),
            P("dp", "mp"),
            P("mp", "dp"),
            P("dp", "mp"),
            P("dp", "mp"),
            P("dp", "mp"),
            P("mp", "dp"),
            P("dp", "mp"),
            P("dp", "mp"),
            P("mp", "dp"),
        ),
        check_vma=False,
    )
```

```python
import functools
import types

import jax
import jax.numpy as jnp
from jax import lax
from jax.experimental import pallas as pl
from jax.experimental.pallas import tpu as pltpu
from jax.sharding import PartitionSpec as P

NB = 32
EPS = 1e-06

F32=jnp.float32; BF16=jnp.bfloat16
NEG=-1e30
NN=(((1,),(0,)),((),())); NT=(((1,),(1,)),((),())); TN=(((0,),(0,)),((),()))
def mm(a,b,dims=NN): return lax.dot_general(a,b,dims,preferred_element_type=F32)
TILE=256

def rows_of(i): return pl.ds(pl.multiple_of(i*TILE,TILE),TILE)

def split_heads(src, dst, heads):
    hd=dst.shape[2]
    for h in range(heads): dst[h]=src[:, h*hd:(h+1)*hd]

def bias_tiles(vecs, tiles, heads):
    key=lax.broadcasted_iota(jnp.int32,(TILE,TILE),0); qry=lax.broadcasted_iota(jnp.int32,(TILE,TILE),1)
    for h in range(heads):
        for d in range(3):
            wide=jnp.broadcast_to(vecs[h*3+d:h*3+d+1,:],(TILE,2*TILE))
            t=pltpu.roll(wide,0,1,stride=1,stride_axis=0)[:,:TILE]
            if d==0: t=jnp.where(qry>=key,t,NEG)
            tiles[h,d]=t

def fwd_attention(q3,k3,v3,vt3,out_t,lse,heads,nq,nk,tiles,kmask):
    hd=q3.shape[2]
    causal=tiles is not None
    def qblock(I,_):
        ri=rows_of(I)
        def kblock(J,carry):
            rj=rows_of(J)
            new=[]
            for h in range(heads):
                m,l,acc=carry[h]
                s=mm(k3[h,rj,:],q3[h,ri,:],NT)
                if causal:
                    s=s+tiles[h,jnp.minimum(I-J,2)]+kmask[rj,:1]
                m2=jnp.maximum(m,jnp.max(s,axis=0,keepdims=True))
                a=jnp.exp(m-m2); p=jnp.exp(s-m2)
                l2=l*a+jnp.sum(p,axis=0,keepdims=True)
                acc2=acc*a+mm(vt3[h,:,rj],p.astype(BF16))
                new.append((m2,l2,acc2))
            return tuple(new)
        init=tuple((jnp.full((1,TILE),NEG,F32),jnp.zeros((1,TILE),F32),jnp.zeros((hd,TILE),F32)) for _ in range(heads))
        res=lax.fori_loop(0,(I+1) if causal else nk//TILE,kblock,init)
        for h in range(heads):
            m,l,acc=res[h]
            out_t[h*hd:(h+1)*hd,ri]=acc/l
            lse[h:h+1,ri]=m+jnp.log(l)
        return 0
    lax.fori_loop(0,nq//TILE,qblock,0)

def bwd_attention(q3,k3,v3,kt3,do3,lse,delta,dqt,dk,dv,heads,nq,nk,tiles,kmask,dtile):
    hd=q3.shape[2]
    causal=tiles is not None
    dqt[...]=jnp.zeros_like(dqt)
    dk[...]=jnp.zeros_like(dk); dv[...]=jnp.zeros_like(dv)
    if causal: dtile[...]=jnp.zeros_like(dtile)
    def kblock(J,_):
        rj=rows_of(J)
        def qblock(I,_):
            ri=rows_of(I)
            for h in range(heads):
                s=mm(k3[h,rj,:],q3[h,ri,:],NT)
                if causal:
                    d=jnp.minimum(I-J,2)
                    s=s+tiles[h,d]+kmask[rj,:1]
                p=jnp.exp(s-lse[h:h+1,ri])
                dp=mm(v3[h,rj,:],do3[h,ri,:],NT)
                ds=(p*(dp-delta[h:h+1,ri])).astype(BF16)
                dv[h,rj,:]+=mm(p.astype(BF16),do3[h,ri,:])
                dk[h,rj,:]+=mm(ds,q3[h,ri,:])
                dqt[h*hd:(h+1)*hd,ri]+=mm(kt3[h,:,rj],ds)
                if causal: dtile[h,d]+=ds.astype(F32)
            return 0
        lax.fori_loop(J if causal else 0,nq//TILE,qblock,0)
        return 0
    lax.fori_loop(0,nk//TILE,kblock,0)

MESH_ID = pl.DeviceIdType.MESH


def layer_kernel(dims, names, *refs):
    D, Hn, hd, FFL, N, NE, NQ, NK, g, part = dims
    s = types.SimpleNamespace(**dict(zip(names, refs)))
    hw = Hn * hd
    o_qkv, o_out, o_cq, o_co, o_ckv, o_ff, o_up, o_down = (
        0, 3 * hw, 4 * hw, 5 * hw, 6 * hw, 8 * hw, 8 * hw + FFL, 8 * hw + 2 * FFL,
    )
    dp, z = lax.axis_index("dp"), lax.axis_index("mp")
    a, low = dp // g, dp % g
    c, r = a % 2, a // 2
    p, zb = z // 2, z % 2
    j = 2 * c + zb
    rx, ry = r + 1 - 2 * (r % 2), (r + 2) % 4
    rd = 3 - r
    z1, z2 = z + 1 - 2 * zb, (z + 2) % 4
    stay = c == p
    moved = c != p

    def device(r_, c_, z_):
        return {"dp": (2 * r_ + c_) * g + low, "mp": z_}

    sibling, across = device(r, 1 - c, z), device(r, c, z1)
    home = device(r, p, j)
    x_chip, y_chip = device(rx, c, z), device(ry, c, z)
    counter = [0]

    def slots(k):
        counter[0] += k
        return counter[0] - k

    def remote(src, dst, dev, send=None, recv=None):
        send = slots(1) if send is None else send
        recv = slots(1) if recv is None else recv
        return pltpu.make_async_remote_copy(
            src_ref=src, dst_ref=dst, send_sem=s.sems.at[send], recv_sem=s.sems.at[recv],
            device_id=dev, device_id_type=MESH_ID,
        )

    def local(src, dst):
        return pltpu.make_async_copy(src, dst, s.sems.at[slots(1)])

    unsent = []

    def go(copy):
        copy.start()
        unsent.append(copy)
        return copy

    def block(i, n):
        return pl.ds(pl.multiple_of(i * n, n), n)

    def order(k):
        return 2 * ((c + k % 2) % 2) + (zb + k // 2) % 2

    barrier = pltpu.get_barrier_semaphore()
    peers = [device(r, (c + dc) % 2, (z + dz) % 4) for dz in range(4) for dc in range(2) if dz or dc] + [x_chip, y_chip]
    for peer in peers:
        pl.semaphore_signal(barrier, inc=1, device_id=peer, device_id_type=MESH_ID)
    pl.semaphore_wait(barrier, len(peers))

    def swap(src, dst):
        far, near = remote(src, dst, home), local(src, dst)

        @pl.when(moved)
        def _():
            far.start()

        @pl.when(stay)
        def _():
            near.start()

        def wait():
            @pl.when(moved)
            def _():
                far.wait()

            @pl.when(stay)
            def _():
                near.wait()

        return wait

    rows_a = D // 8

    def weights_start(col, wide):
        src = s.wpack.at[:, pl.ds(col, wide)]
        near = local(src, s.W.at[block(a, rows_a), pl.ds(col, wide)])
        beside = remote(src, s.W.at[block(a, rows_a), pl.ds(col, wide)], sibling)
        base = slots(2)
        far = remote(src, s.W.at[block(a, rows_a), pl.ds(col, wide)], device(r, p, z2), recv=base + c)

        @pl.when(stay)
        def _():
            near.start()

        @pl.when(moved)
        def _():
            beside.start()

        go(far)

        def wait():
            @pl.when(stay)
            def _():
                near.wait()
                beside.wait_recv()

            @pl.when(moved)
            def _():
                beside.wait_send()
                for k in range(2):
                    remote(src, s.W.at[block(2 * r + k, rows_a), pl.ds(col, wide)], sibling, 0, base + k).wait_recv()

        half = wide // 2
        A, B = pl.ds(col, half), pl.ds(col + half, half)
        chip = 2 * rows_a

        def first_hop():
            wait()
            hop_a = go(remote(s.W.at[block(r, chip), A], s.W.at[block(r, chip), A], x_chip))
            hop_b = go(remote(s.W.at[block(r, chip), B], s.W.at[block(r, chip), B], y_chip))

            def second_hop():
                hop_a.wait_recv()
                two = block(r // 2, 2 * chip)
                last = [go(remote(s.W.at[two, A], s.W.at[two, A], y_chip))]
                hop_b.wait_recv()
                for q in (r, ry):
                    last.append(go(remote(s.W.at[block(q, chip), B], s.W.at[block(q, chip), B], x_chip)))

                def finish():
                    for copy in last:
                        copy.wait_recv()

                return finish

            return second_hop

        return first_hop

    chip = 2 * rows_a

    def grads_start(col, wide):
        half = wide // 2
        A, B = pl.ds(col, half), pl.ds(col + half, half)
        hA = pl.ds(col // 2, half)
        G = s.dW
        one = [
            go(remote(G.at[block(ry // 2, 2 * chip), A], s.ra1.at[:, hA], y_chip)),
            go(remote(G.at[block(rx, chip), B], s.rb1.at[0, :, hA], x_chip)),
            go(remote(G.at[block(rd, chip), B], s.rb1.at[1, :, hA], x_chip)),
        ]

        def add(dst, src):
            n = 96
            for q in range(dst.shape[0] // n):
                w = pl.ds(q * n, n)
                dst[w, :] = (dst[w, :].astype(F32) + src[w, :].astype(F32)).astype(BF16)

        def second():
            one[0].wait_recv()
            add(G.at[block(r // 2, 2 * chip), A], s.ra1.at[:, hA])
            two = [go(remote(G.at[block(rx, chip), A], s.ra2.at[:, hA], x_chip))]
            one[1].wait_recv()
            add(G.at[block(r, chip), B], s.rb1.at[0, :, hA])
            one[2].wait_recv()
            add(G.at[block(ry, chip), B], s.rb1.at[1, :, hA])
            two.append(go(remote(G.at[block(ry, chip), B], s.rb2.at[:, hA], y_chip)))

            def third():
                C = pl.ds(col, wide)
                two[0].wait_recv()
                add(G.at[block(r, chip), A], s.ra2.at[:, hA])
                two[1].wait_recv()
                add(G.at[block(r, chip), B], s.rb2.at[:, hA])
                near = remote(G.at[block(2 * r + 1 - c, rows_a), C], s.rzs.at[:, C], sibling)
                recv = slots(1)
                got = remote(G.at[block(2 * r, rows_a), C], s.rzz.at[:, C], device(r, 0, z2), 0, recv)
                far = [
                    remote(G.at[block(2 * r + k, rows_a), C], s.rzz.at[:, C], device(r, k, z2), None, recv)
                    for k in range(2)
                ]

                @pl.when(stay)
                def _():
                    near.start()
                    s.rzs[:, C] = G[block(a, rows_a), C]

                @pl.when(moved)
                def _():
                    for copy in far:
                        copy.start()

                def finish():
                    @pl.when(stay)
                    def _():
                        near.wait_send()

                    @pl.when(moved)
                    def _():
                        near.wait_recv()
                        for copy in far:
                            copy.wait_send()

                    got.wait_recv()
                    s.gw[:, C] = s.rzs[:, C].astype(F32) + s.rzz[:, C].astype(F32)

                return finish

            return third

        return second

    def gather(buf, n):
        own = buf.at[block(j, n), :]
        side = remote(own, own, sibling)
        cross = remote(own, own, across)
        there = buf.at[block(2 * c + 1 - zb, n), :]
        fwd = remote(there, there, sibling)
        cross.start()
        side.start()

        def forward():
            cross.wait_recv()
            fwd.start()

        def far():
            fwd.wait_recv()
            for copy in (side, cross, fwd):
                copy.wait_send()

        return types.SimpleNamespace(side=side.wait_recv, forward=forward, far=far)

    def each_block(h, body):
        h.side()
        lax.fori_loop(0, 2, lambda k, _: (body(order(k)), 0)[1], 0)
        h.forward()
        h.far()
        lax.fori_loop(2, 4, lambda k, _: (body(order(k)), 0)[1], 0)

    def scatter(fn, bufs, res):
        s0, s1, zs, r0, r1, rz = bufs
        s0[...] = fn(order(3)).astype(BF16)
        d0 = remote(s0, r0, sibling)
        d0.start()
        res[...] = fn(order(2))
        d0.wait_recv()
        zs[...] = (res[...] + r0[...].astype(F32)).astype(BF16)
        dz = remote(zs, rz, across)
        dz.start()
        s1[...] = fn(order(1)).astype(BF16)
        d1 = remote(s1, r1, sibling)
        d1.start()
        res[...] = fn(order(0))

        def finish():
            d1.wait_recv()
            dz.wait_recv()
            res[...] += r1[...].astype(F32) + rz[...].astype(F32)
            for copy in (d0, d1, dz):
                copy.wait_send()

        return finish

    CH = 64

    def chunks(n, body, init=0):
        return lax.fori_loop(0, n // CH, lambda i, v: body(pl.ds(pl.multiple_of(i * CH, CH), CH), v), init)

    gains = [s.gains[k : k + 1, :] for k in range(3)]

    def norm_rows(v, which, inv_ref, w, dst, dst_at):
        inv = lax.rsqrt(jnp.sum(v * v, axis=1, keepdims=True) / D + EPS)
        inv_ref[w, :] = jnp.broadcast_to(inv, (CH, 128))
        dst[dst_at, :] = (v * inv * gains[which]).astype(BF16)

    def own_rows(w, n):
        return pl.ds(pl.multiple_of(j * n + w.start, CH), CH)

    def norm_back_rows(d, v, which, inv):
        scaled = d * gains[which]
        dotted = jnp.sum(scaled * v, axis=1, keepdims=True)
        back = inv * scaled - v * (inv * inv * inv * dotted / D)
        return back, jnp.sum(d * v * inv, axis=0, keepdims=True)

    zero_gain = jnp.zeros((1, D), F32)

    wait_x = swap(s.x, s.XN)
    first_hop_s = weights_start(0, 4 * hw)
    tab = go(remote(s.table, s.table_in, device(r, c, z2)))
    lens = go(remote(s.length, s.length_in, sibling))
    lens.wait_recv()
    s.len_row[...] = jnp.where(stay, s.length[...], s.length_in[...])
    tab.wait_recv()
    table = jnp.where(stay, s.table[...], s.table_in[...])
    span = 2 * TILE
    ids = lax.broadcasted_iota(jnp.int32, (128, span), 0)

    def onehot(row):
        return (ids == s.buckets[row : row + 1, :]).astype(F32)

    for k in range(3):
        s.vecs[8 * k : 8 * k + 8, :] = mm(table, onehot(k))
    key_at = lax.broadcasted_iota(jnp.int32, (TILE, TILE), 0)
    query_at = lax.broadcasted_iota(jnp.int32, (TILE, TILE), 1)
    for h in range(Hn):
        for k in range(3):
            wide = jnp.broadcast_to(s.vecs[8 * k + h : 8 * k + h + 1, :], (TILE, span))
            tile = pltpu.roll(wide, 0, 1, stride=1, stride_axis=0)[:, :TILE]
            s.tiles[h, k] = jnp.where(query_at >= key_at, tile, NEG) if k == 0 else tile
    length = s.len_row[0:1, :]
    s.kmask[...] = jnp.where(
        lax.broadcasted_iota(jnp.int32, s.kmask.shape, 0).astype(F32) < length, 0.0, NEG
    )
    wait_x()
    wait_e = swap(s.enc, s.EN)
    first_hop_c = weights_start(4 * hw, 4 * hw)

    def norm_one(w, _):
        norm_rows(s.XN[w, :].astype(F32), 0, s.inv1, w, s.FIRST, own_rows(w, N))
        return 0

    chunks(N, norm_one)
    ga = gather(s.FIRST, N)
    second_hop_s = first_hop_s()
    wait_o = swap(s.og, s.ON)
    wait_e()
    s.ENC[block(j, NE), :] = s.EN[...]
    ge = gather(s.ENC, NE)
    done_s = second_hop_s()
    first_hop_f = weights_start(8 * hw, 3 * FFL)
    done_s()
    s.WO[...] = s.W[:, o_out : o_out + hw]

    def split(dst, value, rows):
        for h in range(Hn):
            dst[h, rows, :] = value[:, h * hd : (h + 1) * hd]

    def project_one(i):
        w = block(i, N)
        y = mm(s.FIRST[w, :], s.W[:, : 3 * hw]).astype(BF16)
        for k, dst in enumerate((s.q3, s.k3, s.v3)):
            split(dst, y[:, k * hw : (k + 1) * hw], w)

    each_block(ga, project_one)
    second_hop_c = first_hop_c()
    for h in range(Hn):
        s.t3[h] = s.v3[h].T
    fwd_attention(s.q3, s.k3, s.v3, s.t3, s.out_t, s.lse, Hn, NQ, NQ, s.tiles, s.kmask)
    done_c = second_hop_c()
    s.MIX[...] = s.out_t[...].T.astype(BF16)
    end = scatter(lambda i: mm(s.MIX[block(i, N), :], s.WO[...], NT), (s.s0, s.s1, s.zs, s.a0, s.a1, s.az), s.res)
    wait_o()
    own_pos = lax.broadcasted_iota(jnp.int32, (N, 128), 0) + j * N
    s.ok[...] = (own_pos.astype(F32) < length).astype(F32)

    def mask_rows(w, _):
        s.GF[own_rows(w, N), :] = (s.ON[w, :].astype(F32) * s.ok[w, :1]).astype(BF16)
        return 0

    chunks(N, mask_rows)
    done_c()
    s.WCO[...] = s.W[:, o_co : o_co + hw]

    def project_enc(i):
        w = block(i, NE)
        y = mm(s.ENC[w, :], s.W[:, o_ckv : o_ckv + 2 * hw]).astype(BF16)
        split(s.ck3, y[:, :hw], w)
        split(s.cv3, y[:, hw:], w)

    each_block(ge, project_enc)
    end()

    def norm_two(w, _):
        v = s.XN[w, :].astype(F32) + s.res[w, :]
        s.MID[w, :] = v
        norm_rows(v, 1, s.inv2, w, s.SECOND, own_rows(w, N))
        return 0

    chunks(N, norm_two)
    gs = gather(s.SECOND, N)
    second_hop_f = first_hop_f()
    gg = gather(s.GF, N)
    for h in range(Hn):
        s.ct3[h] = s.cv3[h].T

    def project_two(i):
        w = block(i, N)
        split(s.cq3, mm(s.SECOND[w, :], s.W[:, o_cq : o_cq + hw]).astype(BF16), w)

    each_block(gs, project_two)
    fwd_attention(s.cq3, s.ck3, s.cv3, s.ct3, s.out_t2, s.lse2, Hn, NQ, NK, None, None)
    done_f = second_hop_f()
    s.MIX2[...] = s.out_t2[...].T.astype(BF16)
    end = scatter(lambda i: mm(s.MIX2[block(i, N), :], s.WCO[...], NT), (s.s0, s.s1, s.zs, s.b0, s.b1, s.bz), s.res)
    gg.side()
    gg.forward()
    end()

    def norm_three(w, _):
        v = s.MID[w, :] + s.res[w, :]
        s.LAT[w, :] = v
        norm_rows(v, 2, s.inv3, w, s.THIRD, own_rows(w, N))
        return 0

    chunks(N, norm_three)
    gt = gather(s.THIRD, N)
    gg.far()
    done_f()
    root = 0.7978845608028654
    SUB = 128

    def feed(i):
        def sub(u, _):
            w = pl.ds(pl.multiple_of(i * N + u * SUB, SUB), SUB)
            t = s.THIRD[w, :]
            gate = mm(t, s.W[:, o_ff : o_ff + FFL])
            up = mm(t, s.W[:, o_up : o_up + FFL])
            dh = mm(s.GF[w, :], s.W[:, o_down : o_down + FFL])
            sq = gate * gate
            th = jnp.tanh(root * gate * (1.0 + 0.044715 * sq))
            half = 0.5 * (1.0 + th)
            act = gate * half
            slope = half + 0.5 * gate * (1.0 - th * th) * root * (1.0 + 3 * 0.044715 * sq)
            s.HID[w, :] = (act * up).astype(BF16)
            s.DGU[w, :FFL] = (dh * up * slope).astype(BF16)
            s.DGU[w, FFL:] = (dh * act).astype(BF16)
            return 0

        lax.fori_loop(0, N // SUB, sub, 0)

    each_block(gt, feed)
    end = scatter(
        lambda i: mm(s.DGU[block(i, N), :], s.W[:, o_ff : o_ff + 2 * FFL], NT), (s.s0, s.s1, s.zs, s.a0, s.a1, s.az), s.res
    )
    end_out = scatter(
        lambda i: mm(s.HID[block(i, N), :], s.W[:, o_down : o_down + FFL], NT),
        (s.t0, s.t1, s.ts, s.b0, s.b1, s.bz), s.res2,
    )

    def weight_grad(left, right, col, n):
        def step(q, _):
            m = pl.ds(pl.multiple_of(q * 256, 256), 256)
            s.dW[m, pl.ds(col, n)] = mm(left[:, m], right, TN).astype(BF16)
            return 0

        lax.fori_loop(0, D // 256, step, 0)

    weight_grad(s.GF, s.HID[...], o_down, FFL)
    weight_grad(s.THIRD, s.DGU[...], o_ff, 2 * FFL)
    grad_f = grads_start(8 * hw, 3 * FFL)
    end()

    def back_three(w, acc):
        back, part_gain = norm_back_rows(s.res[w, :], s.LAT[w, :], 2, s.inv3[w, :1])
        d = s.GF[own_rows(w, N), :].astype(F32) + back
        s.GR[w, :] = d
        s.DL[own_rows(w, N), :] = d.astype(BF16)
        return acc + part_gain

    gain_three = chunks(N, back_three, zero_gain)
    gd = gather(s.DL, N)
    end_out()

    def put_out(w, _):
        s.LO[w, :] = (s.LAT[w, :] + s.res2[w, :]).astype(BF16)
        return 0

    chunks(N, put_out)
    wait_lo = swap(s.LO, s.lo)

    for h in range(Hn):
        s.ct3[h] = s.ck3[h].T

    def back_heads(src, weight, out_t):
        def body(i):
            w = block(i, N)
            y = mm(src[w, :], weight[...]).astype(BF16)
            split(s.do3, y, w)
            yt = y.astype(F32).T
            for h in range(Hn):
                hh = slice(h * hd, (h + 1) * hd)
                s.delta[h : h + 1, w] = jnp.sum(yt[hh, :] * out_t[hh, w], axis=0, keepdims=True)

        return body

    each_block(gd, back_heads(s.DL, s.WCO, s.out_t2))
    grad_f = grad_f()
    bwd_attention(
        s.cq3, s.ck3, s.cv3, s.ct3, s.do3, s.lse2, s.delta, s.dqt, s.dk3, s.dv3, Hn, NQ, NK, None, None, None
    )
    grad_f = grad_f()
    s.DCQ[...] = s.dqt[...].T.astype(BF16)
    end = scatter(
        lambda i: mm(s.DCQ[block(i, N), :], s.W[:, o_cq : o_cq + hw], NT), (s.s0, s.s1, s.zs, s.a0, s.a1, s.az), s.res
    )
    for h in range(Hn):
        s.DCKV[:, h * hd : (h + 1) * hd] = s.dk3[h, :NK, :].astype(BF16)
        s.DCKV[:, hw + h * hd : hw + (h + 1) * hd] = s.dv3[h, :NK, :].astype(BF16)
    end_enc = scatter(
        lambda i: mm(s.DCKV[block(i, NE), :], s.W[:, o_ckv : o_ckv + 2 * hw], NT),
        (s.e0, s.e1, s.es, s.f0, s.f1, s.fz), s.rese,
    )
    weight_grad(s.SECOND, s.DCQ[...], o_cq, hw)
    weight_grad(s.DL, s.MIX2[...], o_co, hw)
    weight_grad(s.ENC, s.DCKV[...], o_ckv, 2 * hw)
    grad_c = grads_start(4 * hw, 4 * hw)
    end()

    def back_two(w, acc):
        back, part_gain = norm_back_rows(s.res[w, :], s.MID[w, :], 1, s.inv2[w, :1])
        d = s.GR[w, :] + back
        s.GR[w, :] = d
        s.GF[own_rows(w, N), :] = d.astype(BF16)
        return acc + part_gain

    gain_two = chunks(N, back_two, zero_gain)
    gm = gather(s.GF, N)
    end_enc()
    s.EO[...] = s.rese[...].astype(BF16)
    wait_eo = swap(s.EO, s.EO_in)
    for h in range(Hn):
        s.t3[h] = s.k3[h].T
    grad_f()

    each_block(gm, back_heads(s.GF, s.WO, s.out_t))
    grad_c = grad_c()
    bwd_attention(
        s.q3, s.k3, s.v3, s.t3, s.do3, s.lse, s.delta, s.dqt, s.dk3, s.dv3, Hn, NQ, NQ, s.tiles, s.kmask, s.dtile
    )
    grad_c = grad_c()
    s.DQKV[:, :hw] = s.dqt[...].T.astype(BF16)
    for h in range(Hn):
        s.DQKV[:, hw + h * hd : hw + (h + 1) * hd] = s.dk3[h].astype(BF16)
        s.DQKV[:, 2 * hw + h * hd : 2 * hw + (h + 1) * hd] = s.dv3[h].astype(BF16)
    end = scatter(
        lambda i: mm(s.DQKV[block(i, N), :], s.W[:, : 3 * hw], NT), (s.s0, s.s1, s.zs, s.a0, s.a1, s.az), s.res
    )
    weight_grad(s.FIRST, s.DQKV[...], o_qkv, 3 * hw)
    weight_grad(s.GF, s.MIX[...], o_out, hw)
    grad_s = grads_start(0, 4 * hw)
    end()

    def back_one(w, acc):
        back, part_gain = norm_back_rows(s.res[w, :], s.XN[w, :].astype(F32), 0, s.inv1[w, :1])
        s.LO2[w, :] = (s.GR[w, :] + back).astype(BF16)
        return acc + part_gain

    gain_one = chunks(N, back_one, zero_gain)
    wait_dg = swap(s.LO2, s.LO2_in)
    grad_c()

    s.small[...] = jnp.zeros_like(s.small)
    s.small[0:1, :D] = gain_one
    s.small[1:2, :D] = gain_two
    s.small[2:3, :D] = gain_three
    flip = (key_at + query_at == TILE - 1).astype(F32)
    blank = jnp.zeros((TILE, TILE), F32)
    head_row = lax.broadcasted_iota(jnp.int32, (16, span), 0)
    bias_rows = jnp.zeros((16, 128), F32)
    for k in range(3):
        diag = jnp.zeros((16, span), F32)
        for h in range(Hn):
            turned = lax.dot_general(
                flip, s.dtile[h, k], NN, precision=lax.Precision.HIGHEST, preferred_element_type=F32
            )
            lined = pltpu.roll(jnp.concatenate([turned, blank], axis=1), 0, 1, stride=1, stride_axis=0)
            diag = jnp.where(head_row == Hn * j + h, jnp.sum(lined, axis=0, keepdims=True), diag)
        bias_rows = bias_rows + lax.dot_general(
            diag, onehot(3 + k), NT, precision=lax.Precision.HIGHEST, preferred_element_type=F32
        )
    s.small[:, D:] = bias_rows
    for k, peer in enumerate((sibling, across, device(r, c, z2), x_chip, y_chip)):
        s.small_out[k] = s.small[...]
        hop = remote(s.small_out.at[k], s.small_in.at[k], peer)
        hop.start()
        if k == 0:
            grad_s = grad_s()
        hop.wait()
        s.small[...] += s.small_in[k]
    s.sm[...] = s.small[...]
    grad_s = grad_s()
    wait_eo()
    s.eg[...] = s.EO_in[...].astype(F32)
    wait_dg()
    s.dg[...] = s.LO2_in[...].astype(F32)
    grad_s()
    wait_lo()
    for copy in unsent:
        copy.wait_send()
    assert counter[0] <= part, counter[0]


def layer_call(wpack, x, enc, og, gains, table, length, buckets, dims):
    D, Hn, hd, FFL, N, NE, NQ, NK, g, part = dims
    hw = Hn * hd
    cols = wpack.shape[1]
    vm, any_ = pl.BlockSpec(memory_space=pltpu.VMEM), pl.BlockSpec(memory_space=pl.ANY)
    ins = dict(wpack=any_, x=any_, enc=any_, og=any_, gains=vm, table=vm, length=vm, buckets=vm)
    outs = dict(
        lo=((N, D), BF16, any_), dg=((N, D), F32, vm), eg=((NE, D), F32, vm),
        gw=((wpack.shape[0], cols), F32, vm), sm=((16, D + 128), F32, vm),
    )
    sc = {}

    def add(dtype, **shapes):
        for name, shape in shapes.items():
            sc[name] = pltpu.VMEM(shape, dtype)

    add(BF16, W=(D, cols), dW=(D, cols), WO=(D, hw), WCO=(D, hw))
    half = cols // 2
    add(BF16, ra1=(D // 2, half), rb1=(2, D // 4, half), ra2=(D // 4, half), rb2=(D // 4, half))
    add(BF16, rzs=(D // 8, cols), rzz=(D // 8, cols))
    add(BF16, **{k: (NQ, D) for k in ("FIRST", "SECOND", "THIRD", "GF", "DL")}, ENC=(NK, D))
    add(BF16, **{k: (N, D) for k in ("s0", "s1", "zs", "t0", "t1", "ts", "a0", "a1", "az", "b0", "b1", "bz")})
    add(BF16, **{k: (NE, D) for k in ("e0", "e1", "es", "f0", "f1", "fz", "EN", "EO", "EO_in")})
    add(BF16, **{k: (N, D) for k in ("XN", "ON", "LO", "LO2", "LO2_in")})
    add(F32, **{k: (N, D) for k in ("MID", "LAT", "GR", "res", "res2")}, rese=(NE, D))
    add(F32, inv1=(N, 128), inv2=(N, 128), inv3=(N, 128), ok=(N, 128))
    add(BF16, q3=(Hn, NQ, hd), k3=(Hn, NQ, hd), v3=(Hn, NQ, hd), cq3=(Hn, NQ, hd), ck3=(Hn, NK, hd), cv3=(Hn, NK, hd))
    add(BF16, do3=(Hn, NQ, hd), t3=(Hn, hd, NQ), ct3=(Hn, hd, NK))
    add(F32, out_t=(hw, NQ), out_t2=(hw, NQ), dqt=(hw, NQ), lse=(8, NQ), lse2=(8, NQ), delta=(8, NQ))
    add(F32, dk3=(Hn, NQ, hd), dv3=(Hn, NQ, hd))
    add(BF16, MIX=(NQ, hw), MIX2=(NQ, hw), HID=(NQ, FFL), DGU=(NQ, 2 * FFL), DCQ=(NQ, hw), DCKV=(NK, 2 * hw), DQKV=(NQ, 3 * hw))
    add(F32, tiles=(Hn, 3, TILE, TILE), dtile=(Hn, 3, TILE, TILE), kmask=(NQ, 128), vecs=(24, 2 * TILE))
    add(F32, table_in=(8, 128), length_in=(8, 128), len_row=(8, 128))
    add(F32, small=(16, D + 128), small_out=(5, 16, D + 128), small_in=(5, 16, D + 128))
    names = list(ins) + list(outs) + list(sc) + ["sems"]
    return pl.pallas_call(
        functools.partial(layer_kernel, dims, names),
        out_shape=[jax.ShapeDtypeStruct(o[0], o[1]) for o in outs.values()],
        in_specs=list(ins.values()),
        out_specs=[o[2] for o in outs.values()],
        scratch_shapes=list(sc.values()) + [pltpu.SemaphoreType.DMA((part,))],
        compiler_params=pltpu.CompilerParams(collective_id=0, has_side_effects=True, vmem_limit_bytes=67043328),
        name="layer",
    )(wpack, x, enc, og, gains, table, length, buckets)


def exchange(value, step, size):
    return lax.ppermute(value, "dp", [(i, i ^ step) for i in range(size)])


def per_device_fast(
    decoder_in, encoder_out, seq_lengths, rel_buckets, norm_gains, rel_bias,
    self_query, self_key, self_value, self_out, cross_query, cross_key, cross_value, cross_out,
    gate_weight, up_weight, down_weight, out_grad,
):
    width = decoder_in.shape[1]
    heads, w, f = rel_bias.shape[1], self_query.shape[1], gate_weight.shape[1]
    size = lax.axis_size("dp")
    g = size // 8
    rows, erows = decoder_in.shape[0], encoder_out.shape[0]
    slot = rel_buckets.shape[0]
    wpack = jnp.concatenate(
        [self_query, self_key, self_value, self_out.T, cross_query, cross_out.T, cross_key, cross_value,
         gate_weight, up_weight, down_weight.T], axis=1,
    )
    step = 1
    while step < g:
        other = exchange(wpack, step, size)
        upper = (lax.axis_index("dp") // step) % 2
        wpack = jnp.where(upper == 1, jnp.concatenate([other, wpack], 0), jnp.concatenate([wpack, other], 0))
        step *= 2
    far = rel_buckets[TILE : 2 * TILE]
    none = jnp.full((TILE,), -1, jnp.int32)
    near, after = rel_buckets[:TILE], rel_buckets[TILE : 2 * TILE]
    last = jnp.broadcast_to(rel_buckets[slot - 1 :], (TILE,))
    buckets = jnp.stack(
        [jnp.concatenate(v) for v in (
            (near, far), (after, near), (last, last),
            (none[1:], near, none[:1]), (rel_buckets[1 : 2 * TILE], none[:1]), (last, last), (none, none), (none, none),
        )]
    )
    table = jnp.pad(rel_bias.astype(F32).T, ((0, 8 - heads), (0, 128 - NB)))
    length = jnp.broadcast_to(seq_lengths.astype(F32)[:, None], (8, 128))
    gains = jnp.pad(norm_gains.astype(F32), ((0, 5), (0, 0)))
    dims = (width, heads, w // heads, f, rows, erows, 4 * rows, 4 * erows, g, 256)
    lo, dg, eg, gw, sm = layer_call(wpack, decoder_in, encoder_out, out_grad, gains, table, length, buckets, dims)
    step = g // 2
    while step >= 1:
        upper = (lax.axis_index("dp") // step) % 2
        n = gw.shape[0] // 2
        keep = jnp.where(upper == 1, gw[n:], gw[:n])
        give = jnp.where(upper == 1, gw[:n], gw[n:])
        gw = keep + exchange(give, step, size)
        sm = sm + exchange(sm, step, size)
        step //= 2
    hw = w
    return (
        lo, dg, eg, sm[:3, :width], sm[: 4 * heads, width : width + NB].T,
        gw[:, :hw], gw[:, hw : 2 * hw], gw[:, 2 * hw : 3 * hw], gw[:, 3 * hw : 4 * hw].T,
        gw[:, 4 * hw : 5 * hw], gw[:, 6 * hw : 7 * hw], gw[:, 7 * hw : 8 * hw], gw[:, 5 * hw : 6 * hw].T,
        gw[:, 8 * hw : 8 * hw + f], gw[:, 8 * hw + f : 8 * hw + 2 * f], gw[:, 8 * hw + 2 * f :].T,
    )


def solution(mesh):
    return jax.shard_map(
        per_device_fast,
        mesh=mesh,
        in_specs=(
            P(("dp", "mp"), None),
            P(("dp", "mp"), None),
            P("dp"),
            P(),
            P(),
            P(None, "mp"),
            P("dp", "mp"),
            P("dp", "mp"),
            P("dp", "mp"),
            P("mp", "dp"),
            P("dp", "mp"),
            P("dp", "mp"),
            P("dp", "mp"),
            P("mp", "dp"),
            P("dp", "mp"),
            P("dp", "mp"),
            P("mp", "dp"),
            P(("dp", "mp"), None),
        ),
        out_specs=(
            P(("dp", "mp"), None),
            P(("dp", "mp"), None),
            P(("dp", "mp"), None),
            P(),
            P(),
            P("dp", "mp"),
            P("dp", "mp"),
            P("dp", "mp"),
            P("mp", "dp"),
            P("dp", "mp"),
            P("dp", "mp"),
            P("dp", "mp"),
            P("mp", "dp"),
            P("dp", "mp"),
            P("dp", "mp"),
            P("mp", "dp"),
        ),
        check_vma=False,
    )
```

```python
import functools
import types

import jax
import jax.numpy as jnp
from jax import lax
from jax.experimental import pallas as pl
from jax.experimental.pallas import tpu as pltpu
from jax.sharding import PartitionSpec as P

NB = 32
EPS = 1e-06
F32 = jnp.float32
BF16 = jnp.bfloat16
NEG = -1e30
TILE = 256
NN = (((1,), (0,)), ((), ()))
NT = (((1,), (1,)), ((), ()))
TN = (((0,), (0,)), ((), ()))
MESH_ID = pl.DeviceIdType.MESH


def mm(a, b, dims=NN):
    return lax.dot_general(a, b, dims, preferred_element_type=F32)


def tile_rows(i):
    return pl.ds(pl.multiple_of(i * TILE, TILE), TILE)


def fwd_attention(q3, k3, vt3, out_t, lse, heads, query_block, key_blocks, tiles, kmask, between):
    hd = q3.shape[2]

    def qblock(u, _):
        ri = tile_rows(u)
        I = query_block(u)

        def kblock(J, carry):
            rj = tile_rows(J)
            new = []
            for h in range(heads):
                m, l, acc = carry[h]
                s = mm(k3[h, rj, :], q3[h, ri, :], NT)
                if tiles is not None:
                    s = s + tiles[h, jnp.minimum(I - J, 2)].astype(F32) + kmask[rj, :1]
                m2 = jnp.maximum(m, jnp.max(s, axis=0, keepdims=True))
                a = jnp.exp(m - m2)
                p = jnp.exp(s - m2)
                l2 = l * a + jnp.sum(p, axis=0, keepdims=True)
                new.append((m2, l2, acc * a + mm(vt3[h, :, rj], p.astype(BF16))))
            return tuple(new)

        init = tuple(
            (jnp.full((1, TILE), NEG, F32), jnp.zeros((1, TILE), F32), jnp.zeros((hd, TILE), F32)) for _ in range(heads)
        )
        res = lax.fori_loop(0, key_blocks(I), kblock, init)
        for h in range(heads):
            m, l, acc = res[h]
            out_t[h * hd : (h + 1) * hd, ri] = acc / l
            lse[h : h + 1, ri] = m + jnp.log(l)
        between(u)
        return 0

    lax.fori_loop(0, 2, qblock, 0)


def bwd_attention(
    q3, k3, v3, kt3, do3, lse, delta, dqt, dk, dv, put, heads, query_block, first_query, key_end, tiles, kmask, dtile, dfar, between
):
    hd = q3.shape[2]
    dqt[...] = jnp.zeros_like(dqt)

    def kblock(J, _):
        rj = tile_rows(J)
        dk[...] = jnp.zeros_like(dk)
        dv[...] = jnp.zeros_like(dv)

        def qblock(u, _):
            ri = tile_rows(u)
            apart = query_block(u) - J
            for h in range(heads):
                s = mm(k3[h, rj, :], q3[h, ri, :], NT)
                if tiles is not None:
                    s = s + tiles[h, jnp.minimum(apart, 2)].astype(F32) + kmask[rj, :1]
                p = jnp.exp(s - lse[h : h + 1, ri])
                dp = mm(v3[h, rj, :], do3[h, ri, :], NT)
                ds = (p * (dp - delta[h : h + 1, ri])).astype(BF16)
                dv[h] += mm(p.astype(BF16), do3[h, ri, :])
                dk[h] += mm(ds, q3[h, ri, :])
                dqt[h * hd : (h + 1) * hd, ri] += mm(kt3[h, :, rj], ds)
                if tiles is not None:
                    wide = ds.astype(F32)

                    @pl.when(apart < 2)
                    def _():
                        dtile[h, apart] += wide

                    @pl.when(apart >= 2)
                    def _():
                        dfar[h : h + 1, :] += jnp.sum(wide, axis=0, keepdims=True)

            return 0

        lax.fori_loop(first_query(J), 2, qblock, 0)
        put(J)
        between(J)
        return 0

    lax.fori_loop(0, key_end, kblock, 0)


def layer_kernel(dims, names, *refs):
    D, Hl, hd, FFL, N, NE, g, part = dims
    s = types.SimpleNamespace(**dict(zip(names, refs)))
    hw = Hl * hd
    H2 = 2 * Hl
    NC, NQ, NK = 2 * N, 4 * N, 4 * NE
    dp, z = lax.axis_index("dp"), lax.axis_index("mp")
    a, low = dp // g, dp % g
    c, r = a % 2, a // 2
    p, zb = z // 2, z % 2
    j = 2 * c + zb
    rx, ry, rd = r + 1 - 2 * (r % 2), (r + 2) % 4, 3 - r
    z1, z2 = z + 1 - 2 * zb, (z + 2) % 4
    stay, moved = c == p, c != p
    own = jnp.where(stay, z, 3 - z)
    beyond = jnp.where(stay, z1, 3 - z1)
    u_own = own // 2
    lo_block = jnp.minimum(own, 3 - own)
    hi_block = 3 - lo_block

    def device(r_, c_, z_):
        return {"dp": (2 * r_ + c_) * g + low, "mp": z_}

    sibling, across = device(r, 1 - c, z), device(r, c, z1)
    home = device(r, p, 3 - z)
    x_chip, y_chip = device(rx, c, z), device(ry, c, z)
    counter = [0]

    def slots(k):
        counter[0] += k
        return counter[0] - k

    def remote(src, dst, dev, send=None, recv=None):
        send = slots(1) if send is None else send
        recv = slots(1) if recv is None else recv
        return pltpu.make_async_remote_copy(
            src_ref=src, dst_ref=dst, send_sem=s.sems.at[send], recv_sem=s.sems.at[recv],
            device_id=dev, device_id_type=MESH_ID,
        )

    def local(src, dst, sem=None):
        return pltpu.make_async_copy(src, dst, s.sems.at[slots(1) if sem is None else sem])

    def either(cond, yes, no):
        @pl.when(cond)
        def _():
            yes()

        @pl.when(jnp.logical_not(cond))
        def _():
            no()

    unsent = []

    def go(copy):
        copy.start()
        unsent.append(copy)
        return copy

    def block(i, n):
        return pl.ds(pl.multiple_of(i * n, n), n)

    def order(k):
        first = jnp.where(k < 2, own, beyond)
        return jnp.where(k % 2 == 0, first, 3 - first)

    def query_block(u):
        return jnp.where(u == 0, lo_block, hi_block)

    barrier = pltpu.get_barrier_semaphore()
    peers = [device(r, (c + dc) % 2, (z + dz) % 4) for dz in range(4) for dc in range(2) if dz or dc] + [x_chip, y_chip]
    for peer in peers:
        pl.semaphore_signal(barrier, inc=1, device_id=peer, device_id_type=MESH_ID)
    pl.semaphore_wait(barrier, len(peers))

    def swap(src, dst):
        far, near = remote(src, dst, home), local(src, dst)
        either(moved, far.start, near.start)
        return lambda: either(moved, far.wait, near.wait)

    rows_a = D // 8
    chip = 2 * rows_a

    def spread(A, B):
        def at(ref, w):
            buf, slot, cols = ref
            return buf.at[w, cols] if slot is None else buf.at[slot, w, cols]

        def hop(ref, w, dev):
            return remote(at(ref, w), at(ref, w), dev)

        first = [hop(A, block(r, chip), x_chip), hop(B, block(r, chip), y_chip)]
        last = [hop(A, block(r // 2, 2 * chip), y_chip)] + [hop(B, block(q, chip), x_chip) for q in (r, ry)]

        def first_hop():
            go(first[0])
            go(first[1])

        def second_hop():
            first[0].wait_recv()
            go(last[0])
            first[1].wait_recv()
            go(last[1])
            go(last[2])

        def finish():
            for copy in last:
                copy.wait_recv()

        return first_hop, second_hop, finish

    def attn_weights(col, wide):
        C = pl.ds(col, wide)
        src = s.wpack.at[:, C]
        base = slots(4)
        dst = s.W2.at[zb, block(a, rows_a), C]
        for dz in range(1, 4):
            go(remote(src, dst, device(r, p, (z + dz) % 4), None, base + 2 * zb + c))
        near = local(src, dst)
        beside = remote(src, dst, sibling, None, base + 2 * zb + c)
        either(stay, near.start, beside.start)
        got = [
            (jnp.logical_and(z == 2 * c + k, c == c_), remote(src, s.W2.at[k, block(2 * r + c_, rows_a), C], sibling, 0, base + 2 * k + c_))
            for k in range(2)
            for c_ in range(2)
        ]
        first_hop, second_hop, finish = spread((s.W2, 0, C), (s.W2, 1, C))

        def start():
            for mine, copy in got:
                either(mine, near.wait, copy.wait_recv)
            pl.when(moved)(beside.wait_send)
            first_hop()

        return start, second_hop, finish

    def ff_weights(col, wide):
        src = s.wpack.at[:, pl.ds(col, wide)]
        dst = s.WF.at[block(a, rows_a), :]
        near, beside = local(src, dst), remote(src, dst, sibling)
        base = slots(2)
        go(remote(src, dst, device(r, p, z2), None, base + c))
        either(stay, near.start, beside.start)
        got = [remote(src, s.WF.at[block(2 * r + k, rows_a), :], sibling, 0, base + k) for k in range(2)]
        half = wide // 2
        first_hop, second_hop, finish = spread((s.WF, None, pl.ds(0, half)), (s.WF, None, pl.ds(half, half)))

        def start():
            @pl.when(stay)
            def _():
                near.wait()
                beside.wait_recv()

            @pl.when(moved)
            def _():
                beside.wait_send()
                for copy in got:
                    copy.wait_recv()

            first_hop()

        return start, second_hop, finish

    def collect(A, B, bufs, send_home):
        ra1, rb1, ra2, rb2 = bufs

        def at(ref, w):
            buf, slot, cols = ref
            return buf.at[w, cols] if slot is None else buf.at[slot, w, cols]

        one = [
            go(remote(at(A, block(ry // 2, 2 * chip)), ra1, y_chip)),
            go(remote(at(B, block(rx, chip)), rb1.at[0], x_chip)),
            go(remote(at(B, block(rd, chip)), rb1.at[1], x_chip)),
        ]
        two = [remote(at(A, block(rx, chip)), ra2, x_chip), remote(at(B, block(ry, chip)), rb2, y_chip)]
        send, finish = send_home()

        def add(dst, src):
            n = 96
            for q in range(src.shape[0] // n):
                w = pl.ds(q * n, n)
                dst[w, :] = (dst[w, :].astype(F32) + src[w, :].astype(F32)).astype(BF16)

        def second():
            one[0].wait_recv()
            add(at(A, block(r // 2, 2 * chip)), ra1)
            go(two[0])
            one[2].wait_recv()
            add(at(B, block(ry, chip)), rb1.at[1])
            go(two[1])
            one[1].wait_recv()
            add(at(B, block(r, chip)), rb1.at[0])

        def third():
            two[0].wait_recv()
            add(at(A, block(r, chip)), ra2)
            two[1].wait_recv()
            add(at(B, block(r, chip)), rb2)
            send()

        return second, third, finish

    def attn_home(col, wide):
        C = pl.ds(col, wide)

        def build():
            base, near_sem = slots(4), slots(1)
            pending = []
            for k in range(2):
                for c_ in range(2):
                    src = s.dW2.at[k, block(2 * r + c_, rows_a), C]
                    dst = s.gz2.at[z, :, C]
                    mine = jnp.logical_and(2 * c + k == z, c == c_)
                    far = remote(src, dst, device(r, c_, 2 * c + k), None, base + z)
                    pending.append((mine, local(src, dst, near_sem), far))
            src = s.dW2.at[0, block(2 * r, rows_a), C]
            got = [(stay & (z == k), remote(src, s.gz2.at[k, :, C], sibling, 0, base + k)) for k in range(4)]

            def send():
                for mine, near, far in pending:
                    either(mine, near.start, far.start)

            def finish():
                for mine, near, far in pending:
                    either(mine, near.wait, far.wait_send)
                for here, copy in got:
                    pl.when(jnp.logical_not(here))(copy.wait_recv)

            return send, finish

        return build

    def ff_home():
        recv, near_recv, near_sem = slots(1), slots(1), slots(1)
        beside = remote(s.dWF.at[block(2 * r + 1 - c, rows_a), :], s.gzf.at[0], sibling, None, near_recv)
        near = local(s.dWF.at[block(a, rows_a), :], s.gzf.at[0], near_sem)
        far = [
            remote(s.dWF.at[block(2 * r + k, rows_a), :], s.gzf.at[1], device(r, k, z2), None, recv) for k in range(2)
        ]

        def send():
            @pl.when(stay)
            def _():
                beside.start()
                near.start()

            @pl.when(moved)
            def _():
                for copy in far:
                    copy.start()

        def finish():
            @pl.when(stay)
            def _():
                beside.wait_send()
                near.wait()

            @pl.when(moved)
            def _():
                beside.wait_recv()
                for copy in far:
                    copy.wait_send()

            far[0].wait_recv()

        return send, finish

    def gather(buf, n):
        mine = buf.at[block(own, n), :]
        there = buf.at[block(beyond, n), :]
        cross, side, fwd = remote(mine, mine, across), remote(mine, mine, sibling), remote(there, there, sibling)
        cross.start()
        side.start()

        def forward():
            cross.wait_recv()
            fwd.start()

        def far():
            fwd.wait_recv()
            for copy in (side, cross, fwd):
                copy.wait_send()

        return types.SimpleNamespace(side=side.wait_recv, forward=forward, far=far)

    def each_block(h, body):
        h.side()
        lax.fori_loop(0, 2, lambda k, _: (body(order(k)), 0)[1], 0)
        h.forward()
        h.far()
        lax.fori_loop(2, 4, lambda k, _: (body(order(k)), 0)[1], 0)

    def gather_chip(buf):
        mine = buf.at[block(u_own, N), :]
        return go(remote(mine, mine, sibling)).wait_recv

    def scatter(fn, bufs, res):
        s0, s1, zs, r0, r1, rz = bufs
        s0[...] = fn(order(3)).astype(BF16)
        d0 = remote(s0, r0, sibling)
        d0.start()
        res[...] = fn(order(2))
        d0.wait_recv()
        zs[...] = (res[...] + r0[...].astype(F32)).astype(BF16)
        dz = remote(zs, rz, across)
        dz.start()
        s1[...] = fn(order(1)).astype(BF16)
        d1 = remote(s1, r1, sibling)
        d1.start()
        res[...] = fn(order(0))

        def finish():
            d1.wait_recv()
            dz.wait_recv()
            res[...] += r1[...].astype(F32) + rz[...].astype(F32)
            for copy in (d0, d1, dz):
                copy.wait_send()

        return finish

    def scatter_chip(fn, s0, r0, res):
        s0[...] = fn(1 - u_own).astype(BF16)
        d0 = remote(s0, r0, sibling)
        d0.start()
        res[...] = fn(u_own)

        def finish():
            d0.wait()
            res[...] += r0[...].astype(F32)

        return finish

    CH = 64

    def chunks(n, body, init=0):
        return lax.fori_loop(0, n // CH, lambda i, v: body(pl.ds(pl.multiple_of(i * CH, CH), CH), v), init)

    gains = [s.gains[k : k + 1, :].astype(F32) for k in range(3)]

    def norm_rows(v, which, inv_ref, w, dst, dst_at):
        inv = lax.rsqrt(jnp.sum(v * v, axis=1, keepdims=True) / D + EPS)
        inv_ref[w, :] = jnp.broadcast_to(inv, (CH, 128))
        dst[dst_at, :] = (v * inv * gains[which]).astype(BF16)

    def rows_in(i, w):
        return pl.ds(pl.multiple_of(i * N + w.start, CH), CH)

    def norm_back_rows(d, v, which, inv):
        scaled = d * gains[which]
        dotted = jnp.sum(scaled * v, axis=1, keepdims=True)
        back = inv * scaled - v * (inv * inv * inv * dotted / D)
        return back, jnp.sum(d * v * inv, axis=0, keepdims=True)

    zero_gain = jnp.zeros((1, D), F32)
    o_ff = 8 * hw
    c_q, c_o, c_ckv, c_cq, c_co = 2 * hw, 3 * hw, 4 * hw, 6 * hw, 7 * hw

    wait_x = swap(s.x, s.XN)
    w_kv = attn_weights(0, 2 * hw)
    w_qo = attn_weights(2 * hw, 2 * hw)
    s.tab[z] = jnp.zeros_like(s.tab[z])
    s.tab[z, :NB, :Hl] = s.rel_bias[...].astype(F32)
    tab_base = slots(4)
    tab_out = [
        remote(s.tab.at[z], s.tab.at[z], device(r, c, (z + dz) % 4), None, tab_base + z) for dz in range(1, 4)
    ]
    for copy in tab_out:
        go(copy)
    s.len_out[...] = jnp.full(s.len_out.shape, s.seq_lengths[0], jnp.int32).astype(F32)
    lens = go(remote(s.len_out, s.len_in, sibling))
    wait_e = swap(s.enc, s.EN)
    lens.wait_recv()
    s.len_row[...] = jnp.where(stay, s.len_out[...], s.len_in[...])
    for dz in range(1, 4):
        other = s.tab.at[(z + dz) % 4]
        remote(other, other, sibling, 0, tab_base + (z + dz) % 4).wait_recv()
    span = 2 * TILE
    ids = lax.broadcasted_iota(jnp.int32, (NB, span), 0)
    buckets = s.rel_buckets[...]
    last = jnp.broadcast_to(buckets[:, -1:], (1, span))
    near = buckets[:, :span]
    after = jnp.concatenate([buckets[:, TILE:span], buckets[:, :TILE]], axis=1)

    def onehot(row):
        return (ids == row).astype(F32)

    key_at = lax.broadcasted_iota(jnp.int32, (TILE, TILE), 0)
    query_at = lax.broadcasted_iota(jnp.int32, (TILE, TILE), 1)
    for q in range(2):
        table = s.tab[2 * c + q, :NB, :].T[:8, :]
        for k, row in enumerate((near, after, last)):
            s.vecs[8 * k : 8 * k + 8, :] = mm(table, onehot(row))

        def build(h, _):
            for k in range(3):
                wide = jnp.broadcast_to(s.vecs[pl.ds(8 * k + h, 1), :], (TILE, span))
                tile = pltpu.roll(wide, 0, 1, stride=1, stride_axis=0)[:, :TILE]
                s.tiles[Hl * q + h, k] = (jnp.where(query_at >= key_at, tile, NEG) if k == 0 else tile).astype(BF16)
            return 0

        lax.fori_loop(0, Hl, build, 0)
    length = s.len_row[0:1, :]
    s.kmask[...] = jnp.where(
        lax.broadcasted_iota(jnp.int32, s.kmask.shape, 0).astype(F32) < length, 0.0, NEG
    )
    wait_x()
    w_c = attn_weights(4 * hw, 4 * hw)

    def norm_one(w, _):
        norm_rows(s.XN[w, :].astype(F32), 0, s.inv1, w, s.FIRST, rows_in(own, w))
        return 0

    chunks(N, norm_one)
    ga = gather(s.FIRST, N)
    w_kv[0]()
    w_qo[0]()
    w_f = ff_weights(o_ff, 3 * FFL)
    wait_o = swap(s.og, s.ON)
    w_kv[1]()
    ga.side()
    ga.forward()
    w_c[0]()
    w_qo[1]()
    wait_e()
    s.ENC[block(own, NE), :] = s.EN[...]
    ge = gather(s.ENC, NE)
    ga.far()
    w_kv[2]()
    w_qo[2]()

    def split(dst, h0, value, rows):
        for h in range(Hl):
            dst[h0 + h, rows, :] = value[:, h * hd : (h + 1) * hd]

    def project_one(k, _):
        i = order(k)
        w = block(i, N)
        f = s.FIRST[w, :]
        for q in range(2):
            y = mm(f, s.W2[q, :, : 2 * hw]).astype(BF16)
            split(s.k3, Hl * q, y[:, :hw], w)
            split(s.v3, Hl * q, y[:, hw:], w)

        @pl.when(k < 2)
        def _():
            for q in range(2):
                split(s.q3, Hl * q, mm(f, s.W2[q, :, c_q : c_q + hw]).astype(BF16), block(i // 2, N))

        return 0

    lax.fori_loop(0, 4, project_one, 0)

    def turn(dst, src):
        def one(h, _):
            dst[h] = src[h].T
            return 0

        lax.fori_loop(0, H2, one, 0)

    turn(s.t3, s.v3)
    s.WO[...] = s.W2[:, :, c_o : c_o + hw]

    def after_first(u):
        @pl.when(u == 0)
        def _():
            ge.side()
            ge.forward()
            w_c[1]()
            w_f[0]()

    fwd_attention(s.q3, s.k3, s.t3, s.out_t, s.lse, H2, query_block, lambda I: I + 1, s.tiles, s.kmask, after_first)
    s.MIX[...] = s.out_t[...].T.astype(BF16)

    def out_proj(mix, weight):
        def fn(u):
            w = block(u, N)
            return mm(mix[w, :hw], weight[0], NT) + mm(mix[w, hw:], weight[1], NT)

        return fn

    end = scatter_chip(out_proj(s.MIX, s.WO), s.s0, s.i0, s.res)
    wait_o()
    own_pos = lax.broadcasted_iota(jnp.int32, (N, 128), 0) + own * N
    s.ok[...] = (own_pos.astype(F32) < length).astype(F32)

    def mask_rows(w, _):
        s.GF[rows_in(own, w), :] = (s.ON[w, :].astype(F32) * s.ok[w, :1]).astype(BF16)
        return 0

    chunks(N, mask_rows)
    gg = gather(s.GF, N)
    end()

    def norm_two(w, _):
        v = s.XN[w, :].astype(F32) + s.res[w, :]
        s.MID[w, :] = v
        norm_rows(v, 1, s.inv2, w, s.SECOND, rows_in(u_own, w))
        return 0

    chunks(N, norm_two)
    second_ready = gather_chip(s.SECOND)
    ge.far()
    w_c[2]()
    s.WCO[...] = s.W2[:, :, c_co : c_co + hw]

    def project_enc(i, _):
        w = block(i, N)
        e = s.ENC[w, :]
        for q in range(2):
            y = mm(e, s.W2[q, :, c_ckv : c_ckv + 2 * hw]).astype(BF16)
            split(s.ck3, Hl * q, y[:, :hw], w)
            split(s.cv3, Hl * q, y[:, hw:], w)
        return 0

    lax.fori_loop(0, NK // N, project_enc, 0)
    turn(s.ct3, s.cv3)
    second_ready()

    def project_two(u, _):
        w = block(u, N)
        t = s.SECOND[w, :]
        for q in range(2):
            split(s.cq3, Hl * q, mm(t, s.W2[q, :, c_cq : c_cq + hw]).astype(BF16), w)
        return 0

    lax.fori_loop(0, 2, project_two, 0)

    def after_cross(u):
        @pl.when(u == 0)
        def _():
            gg.side()
            gg.forward()
            w_f[1]()

    fwd_attention(
        s.cq3, s.ck3, s.ct3, s.out_t2, s.lse2, H2, query_block, lambda I: NK // TILE, None, None, after_cross
    )
    s.MIX2[...] = s.out_t2[...].T.astype(BF16)
    scatter_chip(out_proj(s.MIX2, s.WCO), s.s0, s.i1, s.res)()

    def norm_three(w, _):
        v = s.MID[w, :] + s.res[w, :]
        s.LAT[w, :] = v
        norm_rows(v, 2, s.inv3, w, s.THIRD, rows_in(own, w))
        return 0

    chunks(N, norm_three)
    gt = gather(s.THIRD, N)
    gg.far()
    w_f[2]()
    root = 0.7978845608028654
    SUB = 128

    def feed(i):
        def sub(u, _):
            w = pl.ds(pl.multiple_of(i * N + u * SUB, SUB), SUB)
            t = s.THIRD[w, :]
            gate = mm(t, s.WF[:, :FFL])
            up = mm(t, s.WF[:, FFL : 2 * FFL])
            dh = mm(s.GF[w, :], s.WF[:, 2 * FFL :])
            sq = gate * gate
            th = jnp.tanh(root * gate * (1.0 + 0.044715 * sq))
            half = 0.5 * (1.0 + th)
            act = gate * half
            slope = half + 0.5 * gate * (1.0 - th * th) * root * (1.0 + 3 * 0.044715 * sq)
            s.HID[w, :] = (act * up).astype(BF16)
            s.DGU[w, :FFL] = (dh * up * slope).astype(BF16)
            s.DGU[w, FFL:] = (dh * act).astype(BF16)
            return 0

        lax.fori_loop(0, N // SUB, sub, 0)

    each_block(gt, feed)
    end = scatter(
        lambda i: mm(s.DGU[block(i, N), :], s.WF[:, : 2 * FFL], NT), (s.s0, s.s1, s.zs, s.a0, s.a1, s.az), s.res
    )

    def weight_grad(put, parts):
        def step(q, _):
            m = pl.ds(pl.multiple_of(q * 256, 256), 256)
            total = None
            for left, right in parts:
                y = mm(left(m), right, TN)
                total = y if total is None else total + y
            put(m, total.astype(BF16))
            return 0

        lax.fori_loop(0, D // 256, step, 0)

    def put_f(col, n):
        def put(m, v):
            s.dWF[m, col : col + n] = v

        return put

    def put_slots(col, n):
        def put(m, v):
            for q in range(2):
                s.dW2[q, m, col : col + n] = v[:, q * n : (q + 1) * n]

        return put

    weight_grad(put_f(2 * FFL, FFL), [(lambda m: s.GF[:, m], s.HID[...])])
    weight_grad(put_f(0, 2 * FFL), [(lambda m: s.THIRD[:, m], s.DGU[...])])
    half_f = 3 * FFL // 2
    grad_f = collect(
        (s.dWF, None, pl.ds(0, half_f)), (s.dWF, None, pl.ds(half_f, half_f)), (s.ra1, s.rb1, s.ra2, s.rb2), ff_home
    )
    end()

    def back_three(w, acc):
        back, part_gain = norm_back_rows(s.res[w, :], s.LAT[w, :], 2, s.inv3[w, :1])
        d = s.GF[rows_in(own, w), :].astype(F32) + back
        s.GR[w, :] = d
        s.DL[rows_in(u_own, w), :] = d.astype(BF16)
        return acc + part_gain

    gain_three = chunks(N, back_three, zero_gain)
    dl_ready = gather_chip(s.DL)
    end_out = scatter(
        lambda i: mm(s.HID[block(i, N), :], s.WF[:, 2 * FFL :], NT), (s.s0, s.s1, s.zs, s.b0, s.b1, s.bz), s.res
    )

    turn(s.ct3, s.ck3)

    def back_heads(src, weight, out_t):
        def body(u, _):
            w = block(u, N)
            for q in range(2):
                y = mm(src[w, :], weight[q]).astype(BF16)
                split(s.do3, Hl * q, y, w)
                yt = y.astype(F32).T
                for h in range(Hl):
                    g_h = Hl * q + h
                    both = yt[h * hd : (h + 1) * hd, :] * out_t[g_h * hd : (g_h + 1) * hd, w]
                    s.delta[g_h : g_h + 1, w] = jnp.sum(both, axis=0, keepdims=True)
            return 0

        lax.fori_loop(0, 2, body, 0)

    dl_ready()
    back_heads(s.DL, s.WCO, s.out_t2)

    def put_cross(J):
        w = tile_rows(J)
        for h in range(H2):
            q, hh = h // Hl, h % Hl
            at = 2 * hw * q + hh * hd
            s.DGU[w, at : at + hd] = s.dk[h].astype(BF16)
            s.DGU[w, at + hw : at + hw + hd] = s.dv[h].astype(BF16)

    def cross_between(J):
        @pl.when(J == 0)
        def _():
            grad_f[0]()

    bwd_attention(
        s.cq3, s.ck3, s.cv3, s.ct3, s.do3, s.lse2, s.delta, s.out_t2, s.dk, s.dv, put_cross, H2, query_block,
        lambda J: 0, NK // TILE, None, None, None, None, cross_between,
    )
    s.DQ[...] = s.out_t2[...].T.astype(BF16)

    def query_grad(col):
        def fn(u):
            w = block(u, N)
            return mm(s.DQ[w, :hw], s.W2[0, :, col : col + hw], NT) + mm(s.DQ[w, hw:], s.W2[1, :, col : col + hw], NT)

        return fn

    def put_out(w, _):
        s.ON[w, :] = (s.LAT[w, :] + s.res[w, :]).astype(BF16)
        return 0

    end_out()
    chunks(N, put_out)
    wait_lo = swap(s.ON, s.lo)
    end = scatter_chip(query_grad(c_cq), s.s0, s.i2, s.res)
    grad_f[1]()

    def kv_grad(n, col):
        def fn(i):
            w = block(i, n)
            return (
                mm(s.DGU[w, : 2 * hw], s.W2[0, :, col : col + 2 * hw], NT)
                + mm(s.DGU[w, 2 * hw : 4 * hw], s.W2[1, :, col : col + 2 * hw], NT)
            )

        return fn

    end()

    def back_two(w, acc):
        back, part_gain = norm_back_rows(s.res[w, :], s.MID[w, :], 1, s.inv2[w, :1])
        d = s.GR[w, :] + back
        s.GR[w, :] = d
        s.DM[rows_in(u_own, w), :] = d.astype(BF16)
        return acc + part_gain

    gain_two = chunks(N, back_two, zero_gain)
    dm_ready = gather_chip(s.DM)
    end_enc = scatter(kv_grad(NE, c_ckv), (s.e0, s.e1, s.es, s.f0, s.f1, s.fz), s.rese)
    weight_grad(put_slots(c_cq, hw), [(lambda m: s.SECOND[:, m], s.DQ[...])])
    weight_grad(put_slots(c_co, hw), [(lambda m: s.DL[:, m], s.MIX2[...])])
    weight_grad(put_slots(c_ckv, 2 * hw), [(lambda m: s.ENC[:, m], s.DGU[:NK, : 4 * hw])])
    C4 = pl.ds(4 * hw, 4 * hw)
    grad_c = collect((s.dW2, 0, C4), (s.dW2, 1, C4), (s.qa1, s.qb1, s.qa2, s.qb2), attn_home(4 * hw, 4 * hw))
    end_enc()
    s.EN[...] = s.rese[...].astype(BF16)
    wait_eo = swap(s.EN, s.eg)
    turn(s.t3, s.k3)

    dm_ready()
    back_heads(s.DM, s.WO, s.out_t)
    s.dtile[...] = jnp.zeros_like(s.dtile)
    s.dfar[...] = jnp.zeros_like(s.dfar)

    def self_between(J):
        @pl.when(J == 0)
        def _():
            grad_c[0]()

    bwd_attention(
        s.q3, s.k3, s.v3, s.t3, s.do3, s.lse, s.delta, s.out_t, s.dk, s.dv, put_cross, H2, query_block,
        lambda J: jnp.where(J <= lo_block, 0, 1), hi_block + 1, s.tiles, s.kmask, s.dtile, s.dfar, self_between,
    )

    def clear(J, _):
        s.DGU[tile_rows(J), :] = jnp.zeros((TILE, s.DGU.shape[1]), BF16)
        return 0

    lax.fori_loop(hi_block + 1, 4, clear, 0)
    s.DQ[...] = s.out_t[...].T.astype(BF16)
    own_part = query_grad(c_q)
    other_part = kv_grad(N, 0)

    def scatter_first(bufs, res):
        s0, s1, zs, r0, r1, rz = bufs
        s0[...] = other_part(order(3)).astype(BF16)
        d0 = remote(s0, r0, sibling)
        d0.start()
        res[...] = other_part(order(2))
        d0.wait_recv()
        zs[...] = (res[...] + r0[...].astype(F32)).astype(BF16)
        dz = remote(zs, rz, across)
        dz.start()
        s1[...] = (other_part(3 - own) + own_part(1 - u_own)).astype(BF16)
        d1 = remote(s1, r1, sibling)
        d1.start()
        res[...] = other_part(own) + own_part(u_own)

        def finish():
            d1.wait_recv()
            dz.wait_recv()
            res[...] += r1[...].astype(F32) + rz[...].astype(F32)
            for copy in (d0, d1, dz):
                copy.wait_send()

        return finish

    end = scatter_first((s.s0, s.s1, s.zs, s.a0, s.a1, s.az), s.res)
    weight_grad(put_slots(0, 2 * hw), [(lambda m: s.FIRST[:, m], s.DGU[:, : 4 * hw])])
    weight_grad(
        put_slots(c_q, hw),
        [(lambda m: s.FIRST[tile_rows(lo_block), m], s.DQ[:N, :]), (lambda m: s.FIRST[tile_rows(hi_block), m], s.DQ[N:, :])],
    )
    weight_grad(put_slots(c_o, hw), [(lambda m: s.DM[:, m], s.MIX[...])])
    S4 = pl.ds(0, 4 * hw)
    grad_s = collect((s.dW2, 0, S4), (s.dW2, 1, S4), (s.ra1, s.rb1, s.ra2, s.rb2), attn_home(0, 4 * hw))
    grad_c[1]()
    s.small[...] = jnp.zeros_like(s.small)
    flip = (key_at + query_at == TILE - 1).astype(F32)
    blank = jnp.zeros((TILE, TILE), F32)
    head_row = lax.broadcasted_iota(jnp.int32, (16, span), 0)
    gap = lax.broadcasted_iota(jnp.int32, (1, span), 1)
    near_back = jnp.where(gap >= TILE - 1, pltpu.roll(near, TILE - 1, 1), -1)
    next_back = jnp.where(gap < span - 1, pltpu.roll(near, span - 1, 1), -1)
    for k, row in enumerate((near_back, next_back)):

        def line_up(h, diag):
            turned = lax.dot_general(
                flip, s.dtile[h, k], NN, precision=lax.Precision.HIGHEST, preferred_element_type=F32
            )
            lined = pltpu.roll(jnp.concatenate([turned, blank], axis=1), 0, 1, stride=1, stride_axis=0)
            return jnp.where(head_row == H2 * c + h, jnp.sum(lined, axis=0, keepdims=True), diag)

        diag = lax.fori_loop(0, H2, line_up, jnp.zeros((16, span), F32))
        s.small[:, D : D + NB] += lax.dot_general(
            diag, onehot(row), NT, precision=lax.Precision.HIGHEST, preferred_element_type=F32
        )
    far_sum = jnp.sum(s.dfar[...], axis=1, keepdims=True)
    bucket_at = lax.broadcasted_iota(jnp.int32, (1, NB), 1)
    is_last = (bucket_at == buckets[:, -1:]).astype(F32)
    bias_row = lax.broadcasted_iota(jnp.int32, (16, NB), 0)
    for h in range(H2):
        s.small[:, D : D + NB] += jnp.where(bias_row == H2 * c + h, far_sum[h : h + 1, :] * is_last, 0.0)
    end()

    def back_one(w, acc):
        back, part_gain = norm_back_rows(s.res[w, :], s.XN[w, :].astype(F32), 0, s.inv1[w, :1])
        s.s0[w, :] = (s.GR[w, :] + back).astype(BF16)
        return acc + part_gain

    gain_one = chunks(N, back_one, zero_gain)
    wait_dg = swap(s.s0, s.dg)
    for k, row in enumerate((gain_one, gain_two, gain_three)):
        s.small[k : k + 1, :D] = row
    for k, peer in enumerate((sibling, across, device(r, c, z2), x_chip, y_chip)):
        s.small_out[k] = s.small[...]
        hop = remote(s.small_out.at[k], s.small_in.at[k], peer)
        hop.start()
        if k == 1:
            grad_s[0]()
        if k == 4:
            grad_s[1]()
        hop.wait()
        s.small[...] += s.small_in[k]
    s.sm[...] = s.small[...]
    wait_lo()
    wait_eo()
    grad_f[2]()
    grad_c[2]()
    wait_dg()
    grad_s[2]()
    for copy in unsent:
        copy.wait_send()
    assert counter[0] <= part, counter[0]


def layer_call(wpack, x, enc, og, gains, rel_bias, seq_lengths, rel_buckets, dims):
    D, Hl, hd, FFL, N, NE, g, part = dims
    hw = Hl * hd
    H2, NC, NQ, NK = 2 * Hl, 2 * N, 4 * N, 4 * NE
    ra = D // 8
    vm, any_ = pl.BlockSpec(memory_space=pltpu.VMEM), pl.BlockSpec(memory_space=pl.ANY)
    sm_ = pl.BlockSpec(memory_space=pltpu.SMEM)
    ins = dict(wpack=any_, x=any_, enc=any_, og=any_, gains=vm, rel_bias=vm, seq_lengths=sm_, rel_buckets=vm)
    outs = dict(
        lo=((N, D), BF16, any_), dg=((N, D), BF16, any_), eg=((NE, D), BF16, any_),
        gz2=((4, ra, 8 * hw), BF16, any_), gzf=((2, ra, 3 * FFL), BF16, any_), sm=((16, D + 128), F32, vm),
    )
    sc = {}

    def add(dtype, **shapes):
        for name, shape in shapes.items():
            sc[name] = pltpu.VMEM(shape, dtype)

    add(BF16, W2=(2, D, 8 * hw), dW2=(2, D, 8 * hw), WF=(D, 3 * FFL), dWF=(D, 3 * FFL), WO=(2, D, hw), WCO=(2, D, hw))
    for k in "rq":
        add(BF16, **{k + "a1": (D // 2, 4 * hw), k + "b1": (2, D // 4, 4 * hw), k + "a2": (D // 4, 4 * hw), k + "b2": (D // 4, 4 * hw)})
    add(BF16, FIRST=(NQ, D), THIRD=(NQ, D), GF=(NQ, D), SECOND=(NC, D), DL=(NC, D), DM=(NC, D), ENC=(NK, D))
    add(BF16, **{k: (N, D) for k in ("s0", "s1", "zs", "a0", "a1", "az", "b0", "b1", "bz", "i0", "i1", "i2", "XN", "ON")})
    add(BF16, **{k: (NE, D) for k in ("e0", "e1", "es", "f0", "f1", "fz", "EN")})
    add(F32, **{k: (N, D) for k in ("MID", "LAT", "GR", "res")}, rese=(NE, D))
    add(F32, inv1=(N, 128), inv2=(N, 128), inv3=(N, 128), ok=(N, 128))
    add(BF16, q3=(H2, NC, hd), k3=(H2, NQ, hd), v3=(H2, NQ, hd), cq3=(H2, NC, hd), ck3=(H2, NK, hd), cv3=(H2, NK, hd))
    add(BF16, do3=(H2, NC, hd), t3=(H2, hd, NQ), ct3=(H2, hd, NK))
    add(F32, out_t=(2 * hw, NC), out_t2=(2 * hw, NC), lse=(8, NC), lse2=(8, NC), delta=(8, NC))
    add(F32, dk=(H2, TILE, hd), dv=(H2, TILE, hd))
    add(BF16, MIX=(NC, 2 * hw), MIX2=(NC, 2 * hw), HID=(NQ, FFL), DGU=(NQ, 2 * FFL), DQ=(NC, 2 * hw))
    add(BF16, tiles=(H2, 3, TILE, TILE))
    add(F32, dtile=(H2, 2, TILE, TILE), dfar=(8, TILE), kmask=(NQ, 128), vecs=(24, 2 * TILE))
    add(F32, tab=(4, NB, 128), len_out=(8, 128), len_in=(8, 128), len_row=(8, 128))
    add(F32, small=(16, D + 128), small_out=(5, 16, D + 128), small_in=(5, 16, D + 128))
    names = list(ins) + list(outs) + list(sc) + ["sems"]
    return pl.pallas_call(
        functools.partial(layer_kernel, dims, names),
        out_shape=[jax.ShapeDtypeStruct(o[0], o[1]) for o in outs.values()],
        in_specs=list(ins.values()),
        out_specs=[o[2] for o in outs.values()],
        scratch_shapes=list(sc.values()) + [pltpu.SemaphoreType.DMA((part,))],
        compiler_params=pltpu.CompilerParams(collective_id=0, has_side_effects=True, vmem_limit_bytes=67043328),
        name="layer",
    )(wpack, x, enc, og, gains, rel_bias, seq_lengths, rel_buckets)


def finish_kernel(dims, lo, dg, eg, gz2, gzf, sm, *outs):
    D, Hl, hd, FFL, N, NE, g, part = dims
    hw = Hl * hd
    o_lo, o_dg, o_eg, o_gains, o_bias, sq, sk, sv, so, cq, ck, cv, co, gg, gu, gd = outs
    o_lo[...] = lo[...]
    o_dg[...] = dg[...].astype(F32)
    o_eg[...] = eg[...].astype(F32)
    o_gains[...] = sm[:3, :D]
    o_bias[...] = sm[:, D:].T[:NB, : 4 * Hl]

    def total(col, n):
        w = pl.ds(col, n)
        return (gz2[0, :, w].astype(F32) + gz2[1, :, w].astype(F32)) + (gz2[2, :, w].astype(F32) + gz2[3, :, w].astype(F32))

    for base, parts in ((0, (sk, sv, sq, so)), (4 * hw, (ck, cv, cq, co))):
        y = total(base, 4 * hw)
        for k, out in enumerate(parts):
            v = y[:, k * hw : (k + 1) * hw]
            out[...] = v if k < 3 else v.T
    f = gzf[0].astype(F32) + gzf[1].astype(F32)
    gg[...] = f[:, :FFL]
    gu[...] = f[:, FFL : 2 * FFL]
    gd[...] = f[:, 2 * FFL :].T


def finish_call(dims, lo, dg, eg, gz2, gzf, sm):
    D, Hl, hd, FFL, N, NE, g, part = dims
    hw, ra = Hl * hd, D // 8
    vm = pl.BlockSpec(memory_space=pltpu.VMEM)
    shapes = [((N, D), BF16), ((N, D), F32), ((NE, D), F32), ((3, D), F32), ((NB, 4 * Hl), F32)]
    shapes += [((ra, hw), F32)] * 3 + [((hw, ra), F32)] + [((ra, hw), F32)] * 3 + [((hw, ra), F32)]
    shapes += [((ra, FFL), F32)] * 2 + [((FFL, ra), F32)]
    return pl.pallas_call(
        functools.partial(finish_kernel, dims),
        out_shape=[jax.ShapeDtypeStruct(*v) for v in shapes],
        in_specs=[vm] * 6,
        out_specs=[vm] * len(shapes),
        name="finish",
    )(lo, dg, eg, gz2, gzf, sm)


def exchange(value, step, size):
    return lax.ppermute(value, "dp", [(i, i ^ step) for i in range(size)])


def per_device(
    decoder_in, encoder_out, seq_lengths, rel_buckets, norm_gains, rel_bias,
    self_query, self_key, self_value, self_out, cross_query, cross_key, cross_value, cross_out,
    gate_weight, up_weight, down_weight, out_grad,
):
    width = decoder_in.shape[1]
    heads, w, f = rel_bias.shape[1], self_query.shape[1], gate_weight.shape[1]
    size = lax.axis_size("dp")
    g = size // 8
    rows, erows = decoder_in.shape[0], encoder_out.shape[0]
    wpack = jnp.concatenate(
        [self_key, self_value, self_query, self_out.T, cross_key, cross_value, cross_query, cross_out.T,
         gate_weight, up_weight, down_weight.T], axis=1,
    )
    step = 1
    while step < g:
        other = exchange(wpack, step, size)
        upper = (lax.axis_index("dp") // step) % 2
        wpack = jnp.where(upper == 1, jnp.concatenate([other, wpack], 0), jnp.concatenate([wpack, other], 0))
        step *= 2
    dims = (width, heads, w // heads, f, rows, erows, g, 320)
    lo, dg, eg, gz2, gzf, sm = layer_call(
        wpack, decoder_in, encoder_out, out_grad, norm_gains, rel_bias, seq_lengths, rel_buckets.reshape(1, -1), dims
    )
    if g == 1:
        return tuple(finish_call(dims, lo, dg, eg, gz2, gzf, sm))
    gw = jnp.concatenate([jnp.sum(gz2.astype(F32), axis=0), jnp.sum(gzf.astype(F32), axis=0)], axis=1)
    step = g // 2
    while step >= 1:
        upper = (lax.axis_index("dp") // step) % 2
        n = gw.shape[0] // 2
        keep = jnp.where(upper == 1, gw[n:], gw[:n])
        give = jnp.where(upper == 1, gw[:n], gw[n:])
        gw = keep + exchange(give, step, size)
        sm = sm + exchange(sm, step, size)
        step //= 2
    col = lambda k: gw[:, k * w : (k + 1) * w]
    return (
        lo, dg.astype(F32), eg.astype(F32), sm[:3, :width], sm[: 4 * heads, width : width + NB].T,
        col(2), col(0), col(1), col(3).T, col(6), col(4), col(5), col(7).T,
        gw[:, 8 * w : 8 * w + f], gw[:, 8 * w + f : 8 * w + 2 * f], gw[:, 8 * w + 2 * f :].T,
    )


def solution(mesh):
    return jax.shard_map(
        per_device,
        mesh=mesh,
        in_specs=(
            P(("dp", "mp"), None),
            P(("dp", "mp"), None),
            P("dp"),
            P(),
            P(),
            P(None, "mp"),
            P("dp", "mp"),
            P("dp", "mp"),
            P("dp", "mp"),
            P("mp", "dp"),
            P("dp", "mp"),
            P("dp", "mp"),
            P("dp", "mp"),
            P("mp", "dp"),
            P("dp", "mp"),
            P("dp", "mp"),
            P("mp", "dp"),
            P(("dp", "mp"), None),
        ),
        out_specs=(
            P(("dp", "mp"), None),
            P(("dp", "mp"), None),
            P(("dp", "mp"), None),
            P(),
            P(),
            P("dp", "mp"),
            P("dp", "mp"),
            P("dp", "mp"),
            P("mp", "dp"),
            P("dp", "mp"),
            P("dp", "mp"),
            P("dp", "mp"),
            P("mp", "dp"),
            P("dp", "mp"),
            P("dp", "mp"),
            P("mp", "dp"),
        ),
        check_vma=False,
    )
```

```python
import functools
import types

import jax
import jax.numpy as jnp
from jax import lax
from jax.experimental import pallas as pl
from jax.experimental.pallas import tpu as pltpu
from jax.sharding import PartitionSpec as P

NB = 32
EPS = 1e-06
F32 = jnp.float32
BF16 = jnp.bfloat16
NEG = -1e30
TILE = 256
NN = (((1,), (0,)), ((), ()))
NT = (((1,), (1,)), ((), ()))
TN = (((0,), (0,)), ((), ()))
MESH_ID = pl.DeviceIdType.MESH


def mm(a, b, dims=NN):
    return lax.dot_general(a, b, dims, preferred_element_type=F32)


def tile_rows(i):
    return pl.ds(pl.multiple_of(i * TILE, TILE), TILE)


def fwd_attention(q3, k3, vt3, out_t, lse, heads, query_block, key_blocks, tiles, between):
    hd = vt3.shape[1]

    def qblock(u, _):
        ri = tile_rows(u)
        I = query_block(u)

        def kblock(J, carry):
            rj = tile_rows(J)
            new = []
            for h in range(heads):
                m, l, acc = carry[h]
                s = mm(k3[h, rj, :], q3[h, ri, :], NT)
                if tiles is not None:
                    s = s + tiles[h, jnp.minimum(I - J, 2)].astype(F32)
                m2 = jnp.maximum(m, jnp.max(s, axis=0, keepdims=True))
                a = jnp.exp(m - m2)
                p = jnp.exp(s - m2)
                l2 = l * a + jnp.sum(p, axis=0, keepdims=True)
                new.append((m2, l2, acc * a + mm(vt3[h, :, rj], p.astype(BF16))))
            return tuple(new)

        init = tuple(
            (jnp.full((1, TILE), NEG, F32), jnp.zeros((1, TILE), F32), jnp.zeros((hd, TILE), F32)) for _ in range(heads)
        )
        res = lax.fori_loop(0, key_blocks(I), kblock, init)
        for h in range(heads):
            m, l, acc = res[h]
            out_t[h * hd : (h + 1) * hd, ri] = acc / l
            lse[h : h + 1, ri] = m + jnp.log(l)
        between(u)
        return 0

    lax.fori_loop(0, 2, qblock, 0)


def bwd_attention(
    q3, k3, v3, kt3, do3, lse, delta, dqt, dk, dv, put, heads, query_block, first_query, key_end, tiles, dtile, between
):
    hd = kt3.shape[1]
    dqt[...] = jnp.zeros_like(dqt)

    def kblock(J, _):
        rj = tile_rows(J)
        dk[...] = jnp.zeros_like(dk)
        dv[...] = jnp.zeros_like(dv)

        def qblock(u, _):
            ri = tile_rows(u)
            apart = query_block(u) - J
            for h in range(heads):
                s = mm(k3[h, rj, :], q3[h, ri, :], NT)
                if tiles is not None:
                    s = s + tiles[h, jnp.minimum(apart, 2)].astype(F32)
                p = jnp.exp(s - lse[h : h + 1, ri])
                dp = mm(v3[h, rj, :], do3[h, ri, :], NT)
                ds = (p * (dp - delta[h : h + 1, ri])).astype(BF16)
                dv[h] += mm(p.astype(BF16), do3[h, ri, :])
                dk[h, :, : q3.shape[2]] += mm(ds, q3[h, ri, :])
                dqt[h * hd : (h + 1) * hd, ri] += mm(kt3[h, :, rj], ds)
                if tiles is not None:
                    dtile[h, jnp.minimum(apart, 2)] += ds.astype(F32)
            return 0

        lax.fori_loop(first_query(J), 2, qblock, 0)
        put(J)
        between(J)
        return 0

    lax.fori_loop(0, key_end, kblock, 0)


def layer_kernel(dims, names, *refs):
    D, Hl, hd, FFL, N, NE, g, part = dims
    s = types.SimpleNamespace(**dict(zip(names, refs)))
    hw = Hl * hd
    H2 = 2 * Hl
    NC, NQ, NK = 2 * N, 4 * N, 4 * NE
    dp, z = lax.axis_index("dp"), lax.axis_index("mp")
    a, low = dp // g, dp % g
    c, r = a % 2, a // 2
    p, zb = z // 2, z % 2
    j = 2 * c + zb
    rx, ry, rd = r + 1 - 2 * (r % 2), (r + 2) % 4, 3 - r
    z1, z2 = z + 1 - 2 * zb, (z + 2) % 4
    stay, moved = c == p, c != p
    own = jnp.where(stay, z, 3 - z)
    beyond = jnp.where(stay, z1, 3 - z1)
    u_own = own // 2
    lo_block = jnp.minimum(own, 3 - own)
    hi_block = 3 - lo_block

    def device(r_, c_, z_):
        return {"dp": (2 * r_ + c_) * g + low, "mp": z_}

    sibling, across = device(r, 1 - c, z), device(r, c, z1)
    home = device(r, p, 3 - z)
    x_chip, y_chip = device(rx, c, z), device(ry, c, z)
    counter = [0]

    def slots(k):
        counter[0] += k
        return counter[0] - k

    def remote(src, dst, dev, send=None, recv=None):
        send = slots(1) if send is None else send
        recv = slots(1) if recv is None else recv
        return pltpu.make_async_remote_copy(
            src_ref=src, dst_ref=dst, send_sem=s.sems.at[send], recv_sem=s.sems.at[recv],
            device_id=dev, device_id_type=MESH_ID,
        )

    def local(src, dst, sem=None):
        return pltpu.make_async_copy(src, dst, s.sems.at[slots(1) if sem is None else sem])

    def either(cond, yes, no):
        @pl.when(cond)
        def _():
            yes()

        @pl.when(jnp.logical_not(cond))
        def _():
            no()

    unsent = []

    def chain(*steps):
        return steps

    def go(copy):
        copy.start()
        unsent.append(copy)
        return copy

    def block(i, n):
        return pl.ds(pl.multiple_of(i * n, n), n)

    def order(k):
        first = jnp.where(k < 2, own, beyond)
        return jnp.where(k % 2 == 0, first, 3 - first)

    def query_block(u):
        return jnp.where(u == 0, lo_block, hi_block)

    pieces = (s.p_sk, s.p_sv, s.p_sq, s.p_so, s.p_ck, s.p_cv, s.p_cq, s.p_co)
    loads = []
    for k, piece in enumerate(pieces):
        loads.append(local(piece, s.raw_t.at[k // 4] if k % 4 == 3 else s.raw.at[k - k // 4]))
    for k, piece in enumerate((s.p_gate, s.p_up, s.p_down)):
        loads.append(local(piece, s.wpack.at[:, pl.ds(8 * hw + k * FFL, FFL)]))
    for copy in loads:
        copy.start()

    barrier = pltpu.get_barrier_semaphore()
    peers = [device(r, (c + dc) % 2, (z + dz) % 4) for dz in range(4) for dc in range(2) if dz or dc] + [x_chip, y_chip, device(rd, c, z)]
    for peer in peers:
        pl.semaphore_signal(barrier, inc=1, device_id=peer, device_id_type=MESH_ID)
    for copy in loads:
        copy.wait()
    for k in range(8):
        piece = s.raw_t[k // 4].T if k % 4 == 3 else s.raw[k - k // 4]
        s.wpack[:, k * hw : (k + 1) * hw] = piece
    pl.semaphore_wait(barrier, len(peers))

    def swap_halves(src, dst):
        n = src.shape[0] // 2
        return [swap_of(src.at[pl.ds(k * n, n), :], dst.at[pl.ds(k * n, n), :]) for k in range(2)]

    def swap(src, dst):
        start, wait = swap_of(src, dst)
        start()
        return wait

    def swap_of(src, dst):
        far, near = remote(src, dst, home), local(src, dst)
        return chain(lambda: either(moved, far.start, near.start), lambda: either(moved, far.wait, near.wait))

    rows_a = D // 8
    chip = 2 * rows_a

    def spread(A, B):
        def at(ref, w):
            buf, slot, cols = ref
            return buf.at[w, cols] if slot is None else buf.at[slot, w, cols]

        def hop(ref, w, dev):
            return remote(at(ref, w), at(ref, w), dev)

        first = [hop(A, block(r, chip), x_chip), hop(B, block(r, chip), y_chip)]
        last = [hop(A, block(r // 2, 2 * chip), y_chip)] + [hop(B, block(q, chip), x_chip) for q in (r, ry)]

        def first_hop():
            go(first[0])
            go(first[1])

        def second_hop():
            first[0].wait_recv()
            go(last[0])
            first[1].wait_recv()
            go(last[1])
            go(last[2])

        def finish():
            for copy in last:
                copy.wait_recv()

        return first_hop, second_hop, finish

    def attn_weights(col, wide):
        C = pl.ds(col, wide)
        src = s.wpack.at[:, C]
        base = slots(4)
        dst = s.W2.at[zb, block(a, rows_a), C]
        out = [remote(src, dst, device(r, p, z_), None, base + 2 * zb + c) for z_ in (z2, z1)]
        near = local(src, dst)
        beside = remote(src, dst, sibling, None, base + 2 * zb + c)
        at = [s.W2.at[zb, block(2 * r + c_, rows_a), C] for c_ in range(2)]
        pass_on = [remote(at[c_], at[c_], across, None, base + 2 * zb + c_) for c_ in range(2)]
        here = [remote(src, at[0], sibling, 0, base + 2 * zb + c_) for c_ in range(2)]
        there = [remote(src, at[0], sibling, 0, base + 2 * (1 - zb) + c_) for c_ in range(2)]
        first_hop, second_hop, finish = spread((s.W2, 0, C), (s.W2, 1, C))

        def start():
            for copy in out:
                go(copy)
            either(stay, near.start, beside.start)

        def relay():
            def forward():
                beside.wait_send()
                for c_ in range(2):
                    here[c_].wait_recv()
                    pass_on[c_].start()

            def settle():
                near.wait()
                remote_side.wait_recv()

            either(moved, forward, settle)

        remote_side = remote(src, at[0], sibling, 0, base + 2 * zb + 1 - c)

        def first():
            for c_ in range(2):
                there[c_].wait_recv()
            pl.when(moved)(lambda: [copy.wait_send() for copy in pass_on] and None)
            first_hop()

        return chain(start, relay, first, second_hop, finish)

    def ff_weights(col, wide):
        src = s.wpack.at[:, pl.ds(col, wide)]
        dst = s.WF.at[block(a, rows_a), :]
        near, beside = local(src, dst), remote(src, dst, sibling)
        base = slots(2)
        out = remote(src, dst, device(r, p, z2), None, base + c)
        got = [remote(src, dst, sibling, 0, base + k) for k in range(2)]
        half = wide // 2
        first_hop, second_hop, finish = spread((s.WF, None, pl.ds(0, half)), (s.WF, None, pl.ds(half, half)))

        def start():
            go(out)
            either(stay, near.start, beside.start)

        def first():
            @pl.when(stay)
            def _():
                near.wait()
                beside.wait_recv()

            @pl.when(moved)
            def _():
                beside.wait_send()
                for copy in got:
                    copy.wait_recv()

            first_hop()

        return chain(start, first, second_hop, finish)

    def collect(A, B, bufs, send_home):
        ra1, rb1, ra2, rb2 = bufs

        def at(ref, w):
            buf, slot, cols = ref
            return buf.at[w, cols] if slot is None else buf.at[slot, w, cols]

        one = [
            go(remote(at(A, block(ry // 2, 2 * chip)), ra1, y_chip)),
            go(remote(at(B, block(rx, chip)), rb1.at[0], x_chip)),
            go(remote(at(B, block(rd, chip)), rb1.at[1], x_chip)),
        ]
        two = [remote(at(A, block(rx, chip)), ra2, x_chip), remote(at(B, block(ry, chip)), rb2, y_chip)]
        home_steps = send_home()

        def add(dst, src):
            n = 96
            for q in range(src.shape[0] // n):
                w = pl.ds(q * n, n)
                dst[w, :] = (dst[w, :].astype(F32) + src[w, :].astype(F32)).astype(BF16)

        def second():
            one[0].wait_recv()
            add(at(A, block(r // 2, 2 * chip)), ra1)
            go(two[0])
            one[2].wait_recv()
            add(at(B, block(ry, chip)), rb1.at[1])
            go(two[1])
            one[1].wait_recv()
            add(at(B, block(r, chip)), rb1.at[0])

        def third():
            two[0].wait_recv()
            add(at(A, block(r, chip)), ra2)
            two[1].wait_recv()
            add(at(B, block(r, chip)), rb2)
            home_steps[0]()

        return chain(second, third, *home_steps[1:])

    def to_home(grad, out):
        recv, near_recv, near_sem = slots(1), slots(1), slots(1)
        beside = remote(grad(2 * r + 1 - c), out(0), sibling, None, near_recv)
        near = local(grad(a), out(0), near_sem)
        far = [remote(grad(2 * r + k), out(1), device(r, k, z2), None, recv) for k in range(2)]

        def send():
            @pl.when(stay)
            def _():
                beside.start()
                near.start()

            @pl.when(moved)
            def _():
                for copy in far:
                    copy.start()

        def finish():
            @pl.when(stay)
            def _():
                beside.wait_send()
                near.wait()

            @pl.when(moved)
            def _():
                beside.wait_recv()
                for copy in far:
                    copy.wait_send()

            far[0].wait_recv()

        return send, finish

    def attn_home(col, wide, buf):
        C = pl.ds(col, wide)

        def build():
            pair = remote(s.dW2.at[1 - zb, block(r, chip), C], buf, across)
            send, finish = to_home(
                lambda i: s.dW2.at[zb, block(i, rows_a), C], lambda k: s.gz2.at[k, :, C]
            )

            def add_pair():
                pair.wait()
                for q in range(2):
                    w = pl.ds(q * rows_a, rows_a)
                    at = s.dW2.at[zb, block(2 * r + q, rows_a), C]
                    at[...] = (at[...].astype(F32) + buf[w, :].astype(F32)).astype(BF16)
                send()

            return pair.start, add_pair, finish

        return build

    def ff_home():
        return to_home(lambda i: s.dWF.at[block(i, rows_a), :], lambda k: s.gzf.at[k])

    def all_sum(buf, in1, in2):
        base1, base2 = slots(8), slots(4)
        me = 4 * c + z
        one, two = [], []
        for dz in range(4):
            for dc in range(2):
                if dz or dc:
                    c_, z_ = (c + dc) % 2, (z + dz) % 4
                    one.append((remote(in1.at[me], in1.at[me], device(r, c_, z_), None, base1 + me), base1 + 4 * c_ + z_))
        for dr in range(1, 4):
            r_ = (r + dr) % 4
            two.append((remote(in2.at[r], in2.at[r], device(r_, c, z), None, base2 + r), base2 + r_))

        def waits(copies, ref):
            for copy, recv in copies:
                copy.wait_send()
                remote(ref, ref, sibling, 0, recv).wait_recv()

        def start():
            in1[me] = buf[...]
            for copy, _ in one:
                copy.start()

        def middle():
            waits(one, in1.at[0])
            in2[r] = jnp.sum(in1[...], axis=0)
            for copy, _ in two:
                copy.start()

        def finish():
            waits(two, in2.at[0])
            buf[...] = jnp.sum(in2[...], axis=0)

        return chain(start, middle, finish)

    def gather(buf, n):
        half = n // 2
        copies = []
        for k in range(2):
            mine = buf.at[block(2 * own + k, half), :]
            there = buf.at[block(2 * beyond + k, half), :]
            copies.append((remote(mine, mine, across), remote(mine, mine, sibling), remote(there, there, sibling)))

        def start(k):
            copies[k][0].start()
            copies[k][1].start()

        def side():
            for copy in copies:
                copy[1].wait_recv()

        def forward():
            for copy in copies:
                copy[0].wait_recv()
                copy[2].start()

        def far():
            for copy in copies:
                copy[2].wait_recv()
                for one in copy:
                    one.wait_send()

        first, second, side, forward, far = chain(lambda: start(0), lambda: start(1), side, forward, far)
        return types.SimpleNamespace(start=lambda k: (first, second)[k](), side=side, forward=forward, far=far)

    def gather_all(buf, n):
        h = gather(buf, n)
        h.start(0)
        h.start(1)
        return h

    def each_block(h, body):
        h.side()
        lax.fori_loop(0, 2, lambda k, _: (body(order(k)), 0)[1], 0)
        h.forward()
        h.far()
        lax.fori_loop(2, 4, lambda k, _: (body(order(k)), 0)[1], 0)

    def gather_chip(buf):
        copies = []
        for k in range(2):
            mine = buf.at[block(2 * u_own + k, N // 2), :]
            copies.append(remote(mine, mine, sibling))

        def ready():
            for copy in copies:
                copy.wait_recv()

        first, second, ready = chain(lambda: go(copies[0]), lambda: go(copies[1]), ready)
        return (lambda k: (first, second)[k]()), ready

    def scatter(fn, bufs, res):
        s0, s1, zs, r0, r1, rz = bufs
        s0[...] = fn(order(3)).astype(BF16)
        d0 = remote(s0, r0, sibling)
        d0.start()
        res[...] = fn(order(2))
        d0.wait_recv()
        zs[...] = (res[...] + r0[...].astype(F32)).astype(BF16)
        n = res.shape[0] // 2
        parts = [pl.ds(k * n, n) for k in range(2)]
        dz = [remote(zs.at[w, :], rz.at[w, :], across) for w in parts]
        for copy in dz:
            copy.start()
        s1[...] = fn(order(1)).astype(BF16)
        d1 = remote(s1, r1, sibling)
        d1.start()
        res[...] = fn(order(0))

        def finish(k=None):
            for q in (0, 1) if k is None else (k,):
                if q == 0:
                    d1.wait_recv()
                w = parts[q]
                dz[q].wait_recv()
                res[w, :] += r1[w, :].astype(F32) + rz[w, :].astype(F32)
                if q == 1:
                    for copy in (d0, d1, *dz):
                        copy.wait_send()

        steps = chain(lambda: finish(0), lambda: finish(1))
        return lambda k=None: [step() for step in (steps if k is None else steps[k : k + 1])]

    def scatter_chip(fn, s0, r0, res):
        s0[...] = fn(1 - u_own).astype(BF16)
        d0 = remote(s0, r0, sibling)
        d0.start()
        res[...] = fn(u_own)

        def finish():
            d0.wait()
            res[...] += r0[...].astype(F32)

        return chain(finish)[0]

    CH = 64

    def chunks(n, body, init=0, half=None):
        lo, hi = (0, n // CH) if half is None else (half * n // (2 * CH), (half + 1) * n // (2 * CH))
        return lax.fori_loop(lo, hi, lambda i, v: body(pl.ds(pl.multiple_of(i * CH, CH), CH), v), init)

    gains = [s.gains[k : k + 1, :].astype(F32) for k in range(3)]

    def norm_rows(v, which, inv_ref, w, dst, dst_at):
        inv = lax.rsqrt(jnp.sum(v * v, axis=1, keepdims=True) / D + EPS)
        inv_ref[w, :] = jnp.broadcast_to(inv, (CH, 128))
        dst[dst_at, :] = (v * inv * gains[which]).astype(BF16)

    def rows_in(i, w):
        return pl.ds(pl.multiple_of(i * N + w.start, CH), CH)

    def norm_back_rows(d, v, which, inv):
        scaled = d * gains[which]
        dotted = jnp.sum(scaled * v, axis=1, keepdims=True)
        back = inv * scaled - v * (inv * inv * inv * dotted / D)
        return back, jnp.sum(d * v * inv, axis=0, keepdims=True)

    zero_gain = jnp.zeros((1, D), F32)
    o_ff = 8 * hw
    c_q, c_o, c_ckv, c_cq, c_co = 2 * hw, 3 * hw, 4 * hw, 6 * hw, 7 * hw

    w_kv = attn_weights(0, 2 * hw)
    w_qo = attn_weights(2 * hw, 2 * hw)
    swap_x = swap_halves(s.x, s.XN)
    w_kv[0]()
    for k in range(2):
        swap_x[k][0]()
    w_qo[0]()
    s.tab[z] = jnp.zeros_like(s.tab[z])
    s.tab[z, :Hl, :NB] = s.rel_bias[...].astype(F32)
    tab_base = slots(4)
    tab_out = [
        remote(s.tab.at[z], s.tab.at[z], device(r, c, (z + dz) % 4), None, tab_base + z) for dz in range(1, 4)
    ]
    for copy in tab_out:
        go(copy)
    s.len_out[...] = jnp.full(s.len_out.shape, s.seq_lengths[0], jnp.int32).astype(F32)
    lens = go(remote(s.len_out, s.len_in, sibling))
    lens.wait_recv()
    s.len_row[...] = jnp.where(stay, s.len_out[...], s.len_in[...])
    for dz in range(1, 4):
        other = s.tab.at[(z + dz) % 4]
        remote(other, other, sibling, 0, tab_base + (z + dz) % 4).wait_recv()
    span = 2 * TILE
    ids = lax.broadcasted_iota(jnp.int32, (NB, span), 0)
    buckets = s.rel_buckets[...]
    last = jnp.broadcast_to(buckets[:, -1:], (1, span))
    near = buckets[:, :span]
    after = jnp.concatenate([buckets[:, TILE:span], buckets[:, :TILE]], axis=1)

    def onehot(row):
        return (ids == row).astype(F32)

    key_at = lax.broadcasted_iota(jnp.int32, (TILE, TILE), 0)
    query_at = lax.broadcasted_iota(jnp.int32, (TILE, TILE), 1)
    w_kv[1]()
    for q in range(2):
        table = s.tab[2 * c + q, :, :NB]
        for k, row in enumerate((near, after, last)):
            s.vecs[8 * k : 8 * k + 8, :] = mm(table, onehot(row))

        def build(h, _):
            for k in range(3):
                wide = jnp.broadcast_to(s.vecs[pl.ds(8 * k + h, 1), :], (TILE, span))
                tile = pltpu.roll(wide, 0, 1, stride=1, stride_axis=0)[:, :TILE]
                s.tiles[Hl * q + h, k] = (jnp.where(query_at >= key_at, tile, NEG) if k == 0 else tile).astype(BF16)
            return 0

        lax.fori_loop(0, Hl, build, 0)
    length = s.len_row[0:1, :]
    lane = lax.broadcasted_iota(jnp.int32, (TILE, 128), 1)

    def extra_lane(i, _):
        w = tile_rows(i)
        at = lax.broadcasted_iota(jnp.int32, (TILE, 128), 0) + i * TILE
        mask = jnp.where((lane == hd) & (at.astype(F32) >= length), NEG, 0.0).astype(BF16)
        for h in range(H2):
            s.k3[h, w, :] = mask

        @pl.when(i < 2)
        def _():
            for h in range(H2):
                s.q3[h, w, :] = jnp.where(lane == hd, 1.0, 0.0).astype(BF16)

        return 0

    lax.fori_loop(0, 4, extra_lane, 0)
    ga = gather(s.FIRST, N)

    def norm_one(w, _):
        norm_rows(s.XN[w, :].astype(F32), 0, s.inv1, w, s.FIRST, rows_in(own, w))
        return 0

    for k in range(2):
        swap_x[k][1]()
        chunks(N, norm_one, 0, k)
        ga.start(k)
    w_kv[2]()
    w_c = attn_weights(4 * hw, 4 * hw)
    w_f = ff_weights(o_ff, 3 * FFL)
    w_c[0]()
    w_qo[1]()
    w_kv[3]()
    w_qo[2]()
    wait_e = swap(s.enc, s.EN)
    ga.side()
    ga.forward()
    w_c[1]()
    w_f[0]()
    w_qo[3]()
    w_c[2]()
    wait_o = swap(s.og, s.ON)
    wait_e()
    s.ENC[block(own, NE), :] = s.EN[...]
    ge = gather_all(s.ENC, NE)
    ga.far()
    w_kv[4]()
    w_qo[4]()

    def split(dst, h0, value, rows):
        for h in range(Hl):
            dst[h0 + h, rows, :hd] = value[:, h * hd : (h + 1) * hd]

    def project_one(k, _):
        i = order(k)
        w = block(i, N)
        f = s.FIRST[w, :]
        for q in range(2):
            y = mm(f, s.W2[q, :, : 2 * hw]).astype(BF16)
            split(s.k3, Hl * q, y[:, :hw], w)
            split(s.v3, Hl * q, y[:, hw:], w)

        @pl.when(k < 2)
        def _():
            for q in range(2):
                split(s.q3, Hl * q, mm(f, s.W2[q, :, c_q : c_q + hw]).astype(BF16), block(i // 2, N))

        return 0

    lax.fori_loop(0, 4, project_one, 0)

    def turn(dst, src):
        def one(h, _):
            dst[h] = src[h, :, :hd].T
            return 0

        lax.fori_loop(0, H2, one, 0)

    turn(s.t3, s.v3)
    s.WO[...] = s.W2[:, :, c_o : c_o + hw]

    def after_first(u):
        @pl.when(u == 0)
        def _():
            w_c[3]()
            w_f[1]()
            ge.side()
            ge.forward()

    fwd_attention(s.q3, s.k3, s.t3, s.out_t, s.lse, H2, query_block, lambda I: I + 1, s.tiles, after_first)
    s.MIX[...] = s.out_t[...].T.astype(BF16)

    def out_proj(mix, weight):
        def fn(u):
            w = block(u, N)
            return mm(mix[w, :hw], weight[0], NT) + mm(mix[w, hw:], weight[1], NT)

        return fn

    end = scatter_chip(out_proj(s.MIX, s.WO), s.s0, s.i0, s.res)
    end()

    def norm_two(w, _):
        v = s.XN[w, :].astype(F32) + s.res[w, :]
        s.MID[w, :] = v
        norm_rows(v, 1, s.inv2, w, s.SECOND, rows_in(u_own, w))
        return 0

    second_go, second_ready = gather_chip(s.SECOND)
    for k in range(2):
        chunks(N, norm_two, 0, k)
        second_go(k)
    ge.far()
    w_c[4]()
    s.WCO[...] = s.W2[:, :, c_co : c_co + hw]

    def project_enc(i, _):
        w = block(i, N)
        e = s.ENC[w, :]
        for q in range(2):
            y = mm(e, s.W2[q, :, c_ckv : c_ckv + 2 * hw]).astype(BF16)
            split(s.ck3, Hl * q, y[:, :hw], w)
            split(s.cv3, Hl * q, y[:, hw:], w)
        return 0

    lax.fori_loop(0, NK // N, project_enc, 0)
    turn(s.ct3, s.cv3)
    second_ready()

    def project_two(u, _):
        w = block(u, N)
        t = s.SECOND[w, :]
        for q in range(2):
            split(s.cq3, Hl * q, mm(t, s.W2[q, :, c_cq : c_cq + hw]).astype(BF16), w)
        return 0

    lax.fori_loop(0, 2, project_two, 0)
    wait_o()
    own_pos = lax.broadcasted_iota(jnp.int32, (N, 128), 0) + own * N
    s.ok[...] = (own_pos.astype(F32) < length).astype(F32)

    def mask_rows(w, _):
        s.GF[rows_in(own, w), :] = (s.ON[w, :].astype(F32) * s.ok[w, :1]).astype(BF16)
        return 0

    chunks(N, mask_rows)
    gg = gather_all(s.GF, N)

    def after_cross(u):
        @pl.when(u == 0)
        def _():
            w_f[2]()

    fwd_attention(
        s.cq3, s.ck3, s.ct3, s.out_t2, s.lse2, H2, query_block, lambda I: NK // TILE, None, after_cross
    )
    s.MIX2[...] = s.out_t2[...].T.astype(BF16)
    scatter_chip(out_proj(s.MIX2, s.WCO), s.s0, s.i1, s.res)()

    def norm_three(w, _):
        v = s.MID[w, :] + s.res[w, :]
        s.LAT[w, :] = v
        norm_rows(v, 2, s.inv3, w, s.THIRD, rows_in(own, w))
        return 0

    gt = gather(s.THIRD, N)
    for k in range(2):
        chunks(N, norm_three, 0, k)
        gt.start(k)
    gg.side()
    gg.forward()
    gg.far()
    w_f[3]()
    root = 0.7978845608028654
    SUB = 128

    def feed(i):
        def sub(u, _):
            w = pl.ds(pl.multiple_of(i * N + u * SUB, SUB), SUB)
            t = s.THIRD[w, :]
            gate = mm(t, s.WF[:, :FFL])
            up = mm(t, s.WF[:, FFL : 2 * FFL])
            dh = mm(s.GF[w, :], s.WF[:, 2 * FFL :])
            sq = gate * gate
            th = jnp.tanh(root * gate * (1.0 + 0.044715 * sq))
            half = 0.5 * (1.0 + th)
            act = gate * half
            slope = half + 0.5 * gate * (1.0 - th * th) * root * (1.0 + 3 * 0.044715 * sq)
            s.HID[w, :] = (act * up).astype(BF16)
            s.DGU[w, :FFL] = (dh * up * slope).astype(BF16)
            s.DGU[w, FFL:] = (dh * act).astype(BF16)
            return 0

        lax.fori_loop(0, N // SUB, sub, 0)

    each_block(gt, feed)
    end = scatter(
        lambda i: mm(s.DGU[block(i, N), :], s.WF[:, : 2 * FFL], NT), (s.s0, s.s1, s.zs, s.a0, s.a1, s.az), s.res
    )

    def weight_grad(put, parts):
        def step(q, _):
            m = pl.ds(pl.multiple_of(q * 256, 256), 256)
            total = None
            for left, right in parts:
                y = mm(left(m), right, TN)
                total = y if total is None else total + y
            put(m, total.astype(BF16))
            return 0

        lax.fori_loop(0, D // 256, step, 0)

    def put_f(col, n):
        def put(m, v):
            s.dWF[m, col : col + n] = v

        return put

    def put_slots(col, n):
        def put(m, v):
            for q in range(2):
                s.dW2[q, m, col : col + n] = v[:, q * n : (q + 1) * n]

        return put

    weight_grad(put_f(2 * FFL, FFL), [(lambda m: s.GF[:, m], s.HID[...])])
    weight_grad(put_f(0, 2 * FFL), [(lambda m: s.THIRD[:, m], s.DGU[...])])
    half_f = 3 * FFL // 2
    grad_f = collect(
        (s.dWF, None, pl.ds(0, half_f)), (s.dWF, None, pl.ds(half_f, half_f)), (s.ra1, s.rb1, s.ra2, s.rb2), ff_home
    )
    def back_three(w, acc):
        back, part_gain = norm_back_rows(s.res[w, :], s.LAT[w, :], 2, s.inv3[w, :1])
        d = s.GF[rows_in(own, w), :].astype(F32) + back
        s.GR[w, :] = d
        s.DL[rows_in(u_own, w), :] = d.astype(BF16)
        return acc + part_gain

    dl_go, dl_ready = gather_chip(s.DL)
    gain_three = zero_gain
    for k in range(2):
        end(k)
        gain_three = chunks(N, back_three, gain_three, k)
        dl_go(k)
    end_out = scatter(
        lambda i: mm(s.HID[block(i, N), :], s.WF[:, 2 * FFL :], NT), (s.s0, s.s1, s.zs, s.b0, s.b1, s.bz), s.res
    )

    turn(s.ct3, s.ck3)

    def back_heads(src, weight, out_t):
        def body(u, _):
            w = block(u, N)
            for q in range(2):
                y = mm(src[w, :], weight[q]).astype(BF16)
                split(s.do3, Hl * q, y, w)
                yt = y.astype(F32).T
                for h in range(Hl):
                    g_h = Hl * q + h
                    both = yt[h * hd : (h + 1) * hd, :] * out_t[g_h * hd : (g_h + 1) * hd, w]
                    s.delta[g_h : g_h + 1, w] = jnp.sum(both, axis=0, keepdims=True)
            return 0

        lax.fori_loop(0, 2, body, 0)

    dl_ready()
    back_heads(s.DL, s.WCO, s.out_t2)

    def put_cross(J):
        w = tile_rows(J)
        for h in range(H2):
            q, hh = h // Hl, h % Hl
            at = 2 * hw * q + hh * hd
            s.DGU[w, at : at + hd] = s.dk[h, :, :hd].astype(BF16)
            s.DGU[w, at + hw : at + hw + hd] = s.dv[h].astype(BF16)

    def cross_between(J):
        @pl.when(J == 0)
        def _():
            grad_f[0]()

    bwd_attention(
        s.cq3, s.ck3, s.cv3, s.ct3, s.do3, s.lse2, s.delta, s.out_t2, s.dk, s.dv, put_cross, H2, query_block,
        lambda J: 0, NK // TILE, None, None, cross_between,
    )
    s.DQ[...] = s.out_t2[...].T.astype(BF16)

    def query_grad(col):
        def fn(u):
            w = block(u, N)
            return mm(s.DQ[w, :hw], s.W2[0, :, col : col + hw], NT) + mm(s.DQ[w, hw:], s.W2[1, :, col : col + hw], NT)

        return fn

    def put_out(w, _):
        s.ON[w, :] = (s.LAT[w, :] + s.res[w, :]).astype(BF16)
        return 0

    end_out()
    chunks(N, put_out)
    wait_lo = swap(s.ON, s.lo)
    end = scatter_chip(query_grad(c_cq), s.s0, s.i2, s.res)

    def kv_grad(n, col):
        def fn(i):
            w = block(i, n)
            return (
                mm(s.DGU[w, : 2 * hw], s.W2[0, :, col : col + 2 * hw], NT)
                + mm(s.DGU[w, 2 * hw : 4 * hw], s.W2[1, :, col : col + 2 * hw], NT)
            )

        return fn

    weight_grad(put_slots(c_cq, hw), [(lambda m: s.SECOND[:, m], s.DQ[...])])
    weight_grad(put_slots(c_co, hw), [(lambda m: s.DL[:, m], s.MIX2[...])])
    weight_grad(put_slots(c_ckv, 2 * hw), [(lambda m: s.ENC[:, m], s.DGU[:NK, : 4 * hw])])
    grad_f[1]()
    C4 = pl.ds(4 * hw, 4 * hw)
    grad_c = collect((s.dW2, 0, C4), (s.dW2, 1, C4), (s.qa1, s.qb1, s.qa2, s.qb2), attn_home(4 * hw, 4 * hw, s.pair1))
    end()

    def back_two(w, acc):
        back, part_gain = norm_back_rows(s.res[w, :], s.MID[w, :], 1, s.inv2[w, :1])
        d = s.GR[w, :] + back
        s.GR[w, :] = d
        s.DM[rows_in(u_own, w), :] = d.astype(BF16)
        return acc + part_gain

    dm_go, dm_ready = gather_chip(s.DM)
    gain_two = zero_gain
    for k in range(2):
        gain_two = chunks(N, back_two, gain_two, k)
        dm_go(k)
    end_enc = scatter(kv_grad(NE, c_ckv), (s.e0, s.e1, s.es, s.f0, s.f1, s.fz), s.rese)
    end_enc()
    s.EN[...] = s.rese[...].astype(BF16)
    wait_eo = swap(s.EN, s.eg)
    turn(s.t3, s.k3)

    dm_ready()
    back_heads(s.DM, s.WO, s.out_t)
    weight_grad(put_slots(c_o, hw), [(lambda m: s.DM[:, m], s.MIX[...])])
    s.dtile[...] = jnp.zeros_like(s.dtile)

    def self_between(J):
        @pl.when(J == 0)
        def _():
            grad_c[0]()

    bwd_attention(
        s.q3, s.k3, s.v3, s.t3, s.do3, s.lse, s.delta, s.out_t, s.dk, s.dv, put_cross, H2, query_block,
        lambda J: jnp.where(J <= lo_block, 0, 1), hi_block + 1, s.tiles, s.dtile, self_between,
    )

    def clear(J, _):
        s.DGU[tile_rows(J), :] = jnp.zeros((TILE, s.DGU.shape[1]), BF16)
        return 0

    lax.fori_loop(hi_block + 1, 4, clear, 0)
    s.DQ[...] = s.out_t[...].T.astype(BF16)
    own_part = query_grad(c_q)
    other_part = kv_grad(N, 0)

    def scatter_first(bufs, res):
        s0, s1, zs, r0, r1, rz = bufs
        s0[...] = other_part(order(3)).astype(BF16)
        d0 = remote(s0, r0, sibling)
        d0.start()
        res[...] = other_part(order(2))
        d0.wait_recv()
        zs[...] = (res[...] + r0[...].astype(F32)).astype(BF16)
        n = res.shape[0] // 2
        parts = [pl.ds(k * n, n) for k in range(2)]
        dz = [remote(zs.at[w, :], rz.at[w, :], across) for w in parts]
        for copy in dz:
            copy.start()
        s1[...] = (other_part(3 - own) + own_part(1 - u_own)).astype(BF16)
        d1 = remote(s1, r1, sibling)
        d1.start()
        res[...] = other_part(own) + own_part(u_own)

        def finish(k=None):
            for q in (0, 1) if k is None else (k,):
                if q == 0:
                    d1.wait_recv()
                w = parts[q]
                dz[q].wait_recv()
                res[w, :] += r1[w, :].astype(F32) + rz[w, :].astype(F32)
                if q == 1:
                    for copy in (d0, d1, *dz):
                        copy.wait_send()

        steps = chain(lambda: finish(0), lambda: finish(1))
        return lambda k=None: [step() for step in (steps if k is None else steps[k : k + 1])]

    KV, QO = pl.ds(0, 2 * hw), pl.ds(2 * hw, 2 * hw)
    bufs = (s.ra1, s.rb1, s.ra2, s.rb2)
    cut = lambda k: tuple(x.at[..., pl.ds(k * 2 * hw, 2 * hw)] for x in bufs)
    grad_c[1]()
    weight_grad(put_slots(0, 2 * hw), [(lambda m: s.FIRST[:, m], s.DGU[:, : 4 * hw])])
    grad_kv = collect((s.dW2, 0, KV), (s.dW2, 1, KV), cut(0), attn_home(0, 2 * hw, s.pair2))
    weight_grad(
        put_slots(c_q, hw),
        [
            (lambda m: s.FIRST[tile_rows(lo_block), m], s.DQ[:N, :]),
            (lambda m: s.FIRST[tile_rows(hi_block), m], s.DQ[N:, :]),
        ],
    )
    grad_qo = collect((s.dW2, 0, QO), (s.dW2, 1, QO), cut(1), attn_home(2 * hw, 2 * hw, s.pair3))
    end = scatter_first((s.s0, s.s1, s.zs, s.a0, s.a1, s.az), s.res)
    grad_c[2]()
    grad_kv[0]()
    s.small[...] = jnp.zeros_like(s.small)
    flip = (key_at + query_at == TILE - 1).astype(BF16)
    blank = jnp.zeros((TILE, TILE), F32)
    head_row = lax.broadcasted_iota(jnp.int32, (16, span), 0)
    gap = lax.broadcasted_iota(jnp.int32, (1, span), 1)
    near_back = jnp.where(gap >= TILE - 1, pltpu.roll(near, TILE - 1, 1), -1)
    next_back = jnp.where(gap < span - 1, pltpu.roll(near, span - 1, 1), -1)
    for k, row in enumerate((near_back, next_back)):

        def line_up(h, diag):
            full = s.dtile[h, k]
            high = full.astype(BF16)
            rest = full - high.astype(F32)
            mid = rest.astype(BF16)
            turned = mm(flip, high) + mm(flip, mid) + mm(flip, (rest - mid.astype(F32)).astype(BF16))
            lined = pltpu.roll(jnp.concatenate([turned, blank], axis=1), 0, 1, stride=1, stride_axis=0)
            return jnp.where(head_row == H2 * c + h, jnp.sum(lined, axis=0, keepdims=True), diag)

        diag = lax.fori_loop(0, H2, line_up, jnp.zeros((16, span), F32))
        s.small[:16, :NB] += lax.dot_general(
            diag, onehot(row), NT, precision=lax.Precision.HIGHEST, preferred_element_type=F32
        )
    far_row = lax.broadcasted_iota(jnp.int32, (16, 1), 0)

    def far_total(h, acc):
        total = jnp.sum(jnp.sum(s.dtile[h, 2], axis=0, keepdims=True), axis=1, keepdims=True)
        return jnp.where(far_row == H2 * c + h, total, acc)

    far_sum = lax.fori_loop(0, H2, far_total, jnp.zeros((16, 1), F32))
    is_last = (lax.broadcasted_iota(jnp.int32, (1, NB), 1) == buckets[:, -1:]).astype(F32)
    s.small[:16, :NB] += far_sum * is_last

    def put_rows(buf, at, row):
        for k in range(D // 128):
            buf[at + k : at + k + 1, :] = row[:, 128 * k : 128 * (k + 1)]

    put_rows(s.small, 16, gain_two)
    put_rows(s.small, 24, gain_three)
    sum_small = all_sum(s.small, s.small1, s.small2)
    sum_small[0]()
    def back_one(w, acc):
        back, part_gain = norm_back_rows(s.res[w, :], s.XN[w, :].astype(F32), 0, s.inv1[w, :1])
        s.i0[w, :] = (s.GR[w, :] + back).astype(BF16)
        return acc + part_gain

    swap_dg = swap_halves(s.i0, s.dg)
    wait_dg = [pair[1] for pair in swap_dg]
    gain_one = zero_gain
    for k in range(2):
        end(k)
        gain_one = chunks(N, back_one, gain_one, k)
        swap_dg[k][0]()
        if k == 0:
            grad_qo[0]()
    s.late[...] = jnp.zeros_like(s.late)
    put_rows(s.late, 0, gain_one)
    sum_late = all_sum(s.late, s.late1, s.late2)
    sum_late[0]()
    grad_kv[1]()
    sum_small[1]()
    grad_qo[1]()
    sum_late[1]()
    grad_kv[2]()
    sum_small[2]()
    grad_qo[2]()
    sum_late[2]()
    s.sm[...] = jnp.zeros_like(s.sm)
    for k in range(D // 128):
        w = slice(128 * k, 128 * (k + 1))
        s.sm[0:1, w] = s.late[k : k + 1, :]
        s.sm[1:2, w] = s.small[16 + k : 17 + k, :]
        s.sm[2:3, w] = s.small[24 + k : 25 + k, :]
    s.sm[:, D:] = s.small[:16, :]
    wait_lo()
    wait_eo()
    grad_f[2]()
    grad_c[3]()
    grad_kv[3]()
    for wait in wait_dg:
        wait()
    grad_qo[3]()
    for copy in unsent:
        copy.wait_send()
    assert counter[0] <= part, counter[0]


def layer_call(pieces, x, enc, og, gains, rel_bias, seq_lengths, rel_buckets, dims):
    D, Hl, hd, FFL, N, NE, g, part = dims
    hw = Hl * hd
    H2, NC, NQ, NK = 2 * Hl, 2 * N, 4 * N, 4 * NE
    ra = D // 8
    vm, any_ = pl.BlockSpec(memory_space=pltpu.VMEM), pl.BlockSpec(memory_space=pl.ANY)
    sm_ = pl.BlockSpec(memory_space=pltpu.SMEM)
    piece_names = ("p_sk", "p_sv", "p_sq", "p_so", "p_ck", "p_cv", "p_cq", "p_co", "p_gate", "p_up", "p_down")
    ins = dict({k: any_ for k in piece_names}, x=any_, enc=any_, og=any_, gains=vm, rel_bias=vm, seq_lengths=sm_, rel_buckets=vm)
    outs = dict(
        lo=((N, D), BF16, any_), dg=((N, D), BF16, any_), eg=((NE, D), BF16, any_),
        gz2=((2, ra, 8 * hw), BF16, any_), gzf=((2, ra, 3 * FFL), BF16, any_), sm=((16, D + 128), F32, vm),
    )
    sc = {}

    def add(dtype, **shapes):
        for name, shape in shapes.items():
            sc[name] = pltpu.VMEM(shape, dtype)

    add(BF16, wpack=(ra, 8 * hw + 3 * FFL), raw=(6, ra, hw), raw_t=(2, hw, ra))
    add(BF16, pair1=(D // 4, 4 * hw), pair2=(D // 4, 2 * hw), pair3=(D // 4, 2 * hw))
    add(BF16, W2=(2, D, 8 * hw), dW2=(2, D, 8 * hw), WF=(D, 3 * FFL), dWF=(D, 3 * FFL), WO=(2, D, hw), WCO=(2, D, hw))
    for k in "rq":
        add(BF16, **{k + "a1": (D // 2, 4 * hw), k + "b1": (2, D // 4, 4 * hw), k + "a2": (D // 4, 4 * hw), k + "b2": (D // 4, 4 * hw)})
    add(BF16, FIRST=(NQ, D), THIRD=(NQ, D), GF=(NQ, D), SECOND=(NC, D), DL=(NC, D), DM=(NC, D), ENC=(NK, D))
    add(BF16, **{k: (N, D) for k in ("s0", "s1", "zs", "a0", "a1", "az", "b0", "b1", "bz", "i0", "i1", "i2", "XN", "ON")})
    add(BF16, **{k: (NE, D) for k in ("e0", "e1", "es", "f0", "f1", "fz", "EN")})
    add(F32, **{k: (N, D) for k in ("MID", "LAT", "GR", "res")}, rese=(NE, D))
    add(F32, inv1=(N, 128), inv2=(N, 128), inv3=(N, 128), ok=(N, 128))
    add(BF16, q3=(H2, NC, 128), k3=(H2, NQ, 128), v3=(H2, NQ, hd), cq3=(H2, NC, hd), ck3=(H2, NK, hd), cv3=(H2, NK, hd))
    add(BF16, do3=(H2, NC, hd), t3=(H2, hd, NQ), ct3=(H2, hd, NK))
    add(F32, out_t=(2 * hw, NC), out_t2=(2 * hw, NC), lse=(8, NC), lse2=(8, NC), delta=(8, NC))
    add(F32, dk=(H2, TILE, 128), dv=(H2, TILE, hd))
    add(BF16, MIX=(NC, 2 * hw), MIX2=(NC, 2 * hw), HID=(NQ, FFL), DGU=(NQ, 2 * FFL), DQ=(NC, 2 * hw))
    add(BF16, tiles=(H2, 3, TILE, TILE))
    add(F32, dtile=(H2, 3, TILE, TILE), vecs=(24, 2 * TILE))
    add(F32, tab=(4, 8, 128), len_out=(8, 128), len_in=(8, 128), len_row=(8, 128))
    add(F32, small=(32, 128), small1=(8, 32, 128), small2=(4, 32, 128))
    add(F32, late=(8, 128), late1=(8, 8, 128), late2=(4, 8, 128))
    names = list(ins) + list(outs) + list(sc) + ["sems"]
    return pl.pallas_call(
        functools.partial(layer_kernel, dims, names),
        out_shape=[jax.ShapeDtypeStruct(o[0], o[1]) for o in outs.values()],
        in_specs=list(ins.values()),
        out_specs=[o[2] for o in outs.values()],
        scratch_shapes=list(sc.values()) + [pltpu.SemaphoreType.DMA((part,))],
        compiler_params=pltpu.CompilerParams(collective_id=0, has_side_effects=True, vmem_limit_bytes=67043328),
        name="layer",
    )(*pieces, x, enc, og, gains, rel_bias, seq_lengths, rel_buckets)


def finish_kernel(dims, lo, dg, eg, gz2, gzf, sm, *outs):
    D, Hl, hd, FFL, N, NE, g, part = dims
    hw = Hl * hd
    o_lo, o_dg, o_eg, o_gains, o_bias, sq, sk, sv, so, cq, ck, cv, co, gg, gu, gd = outs
    o_lo[...] = lo[...]
    o_dg[...] = dg[...].astype(F32)
    o_eg[...] = eg[...].astype(F32)
    o_gains[...] = sm[:3, :D]
    o_bias[...] = sm[: 4 * Hl, D : D + NB]

    def total(col, n):
        w = pl.ds(col, n)
        return gz2[0, :, w].astype(F32) + gz2[1, :, w].astype(F32)

    for base, parts in ((0, (sk, sv, sq, so)), (4 * hw, (ck, cv, cq, co))):
        y = total(base, 4 * hw)
        for k, out in enumerate(parts):
            v = y[:, k * hw : (k + 1) * hw]
            out[...] = v if k < 3 else v.T
    f = gzf[0].astype(F32) + gzf[1].astype(F32)
    gg[...] = f[:, :FFL]
    gu[...] = f[:, FFL : 2 * FFL]
    gd[...] = f[:, 2 * FFL :]


def finish_call(dims, lo, dg, eg, gz2, gzf, sm):
    D, Hl, hd, FFL, N, NE, g, part = dims
    hw, ra = Hl * hd, D // 8
    vm = pl.BlockSpec(memory_space=pltpu.VMEM)
    shapes = [((N, D), BF16), ((N, D), F32), ((NE, D), F32), ((3, D), F32), ((4 * Hl, NB), F32)]
    shapes += [((ra, hw), F32)] * 3 + [((hw, ra), F32)] + [((ra, hw), F32)] * 3 + [((hw, ra), F32)]
    shapes += [((ra, FFL), F32)] * 3
    return pl.pallas_call(
        functools.partial(finish_kernel, dims),
        out_shape=[jax.ShapeDtypeStruct(*v) for v in shapes],
        in_specs=[vm] * 6,
        out_specs=[vm] * len(shapes),
        name="finish",
    )(lo, dg, eg, gz2, gzf, sm)


def exchange(value, step, size):
    return lax.ppermute(value, "dp", [(i, i ^ step) for i in range(size)])


def per_device(
    decoder_in, encoder_out, seq_lengths, rel_buckets, norm_gains, rel_bias,
    self_query, self_key, self_value, self_out, cross_query, cross_key, cross_value, cross_out,
    gate_weight, up_weight, down_weight, out_grad,
):
    width = decoder_in.shape[1]
    heads, w, f = rel_bias.shape[1], self_query.shape[1], gate_weight.shape[1]
    size = lax.axis_size("dp")
    g = size // 8
    rows, erows = decoder_in.shape[0], encoder_out.shape[0]
    pieces = (
        self_key, self_value, self_query, self_out, cross_key, cross_value, cross_query, cross_out,
        gate_weight, up_weight, down_weight.T,
    )
    if g > 1:
        wpack = jnp.concatenate([x.T if k in (3, 7) else x for k, x in enumerate(pieces)], axis=1)
        step = 1
        while step < g:
            other = exchange(wpack, step, size)
            upper = (lax.axis_index("dp") // step) % 2
            wpack = jnp.where(upper == 1, jnp.concatenate([other, wpack], 0), jnp.concatenate([wpack, other], 0))
            step *= 2
        cols = [wpack[:, k * w : (k + 1) * w] for k in range(8)]
        cols[3], cols[7] = cols[3].T, cols[7].T
        pieces = (*cols, *(wpack[:, 8 * w + k * f : 8 * w + (k + 1) * f] for k in range(3)))
    dims = (width, heads, w // heads, f, rows, erows, g, 480)
    lo, dg, eg, gz2, gzf, sm = layer_call(
        pieces, decoder_in, encoder_out, out_grad, norm_gains, rel_bias.T, seq_lengths, rel_buckets.reshape(1, -1), dims
    )
    if g == 1:
        outs = list(finish_call(dims, lo, dg, eg, gz2, gzf, sm))
        outs[4], outs[15] = outs[4].T, outs[15].T
        return tuple(outs)
    gw = jnp.concatenate([jnp.sum(gz2.astype(F32), axis=0), jnp.sum(gzf.astype(F32), axis=0)], axis=1)
    step = g // 2
    while step >= 1:
        upper = (lax.axis_index("dp") // step) % 2
        n = gw.shape[0] // 2
        keep = jnp.where(upper == 1, gw[n:], gw[:n])
        give = jnp.where(upper == 1, gw[:n], gw[n:])
        gw = keep + exchange(give, step, size)
        sm = sm + exchange(sm, step, size)
        step //= 2
    col = lambda k: gw[:, k * w : (k + 1) * w]
    return (
        lo, dg.astype(F32), eg.astype(F32), sm[:3, :width], sm[: 4 * heads, width : width + NB].T,
        col(2), col(0), col(1), col(3).T, col(6), col(4), col(5), col(7).T,
        gw[:, 8 * w : 8 * w + f], gw[:, 8 * w + f : 8 * w + 2 * f], gw[:, 8 * w + 2 * f :].T,
    )


def solution(mesh):
    return jax.shard_map(
        per_device,
        mesh=mesh,
        in_specs=(
            P(("dp", "mp"), None),
            P(("dp", "mp"), None),
            P("dp"),
            P(),
            P(),
            P(None, "mp"),
            P("dp", "mp"),
            P("dp", "mp"),
            P("dp", "mp"),
            P("mp", "dp"),
            P("dp", "mp"),
            P("dp", "mp"),
            P("dp", "mp"),
            P("mp", "dp"),
            P("dp", "mp"),
            P("dp", "mp"),
            P("mp", "dp"),
            P(("dp", "mp"), None),
        ),
        out_specs=(
            P(("dp", "mp"), None),
            P(("dp", "mp"), None),
            P(("dp", "mp"), None),
            P(),
            P(),
            P("dp", "mp"),
            P("dp", "mp"),
            P("dp", "mp"),
            P("mp", "dp"),
            P("dp", "mp"),
            P("dp", "mp"),
            P("dp", "mp"),
            P("mp", "dp"),
            P("dp", "mp"),
            P("dp", "mp"),
            P("mp", "dp"),
        ),
        check_vma=False,
    )
```

```python
import functools
import types

import jax
import jax.numpy as jnp
from jax import lax
from jax.experimental import pallas as pl
from jax.experimental.pallas import tpu as pltpu
from jax.sharding import PartitionSpec as P

NB = 32
EPS = 1e-06
F32 = jnp.float32
BF16 = jnp.bfloat16
NEG = -1e30
TILE = 256
NN = (((1,), (0,)), ((), ()))
NT = (((1,), (1,)), ((), ()))
TN = (((0,), (0,)), ((), ()))
MESH_ID = pl.DeviceIdType.MESH


def mm(a, b, dims=NN):
    return lax.dot_general(a, b, dims, preferred_element_type=F32)


def tile_rows(i):
    return pl.ds(pl.multiple_of(i * TILE, TILE), TILE)


def fwd_attention(q3, k3, vt3, out_t, lse, heads, query_block, key_blocks, tiles, between):
    hd = vt3.shape[1]

    def qblock(u, _):
        ri = tile_rows(u)
        I = query_block(u)

        def kblock(J, carry):
            rj = tile_rows(J)
            new = []
            for h in range(heads):
                m, l, acc = carry[h]
                s = mm(k3[h, rj, :], q3[h, ri, :], NT)
                if tiles is not None:
                    s = s + tiles[h, jnp.minimum(I - J, 2)].astype(F32)
                m2 = jnp.maximum(m, jnp.max(s, axis=0, keepdims=True))
                a = jnp.exp(m - m2)
                p = jnp.exp(s - m2)
                l2 = l * a + jnp.sum(p, axis=0, keepdims=True)
                new.append((m2, l2, acc * a + mm(vt3[h, :, rj], p.astype(BF16))))
            between(u, J)
            return tuple(new)

        init = tuple(
            (jnp.full((1, TILE), NEG, F32), jnp.zeros((1, TILE), F32), jnp.zeros((hd, TILE), F32)) for _ in range(heads)
        )
        res = lax.fori_loop(0, key_blocks(I), kblock, init)
        for h in range(heads):
            m, l, acc = res[h]
            out_t[h * hd : (h + 1) * hd, ri] = acc / l
            lse[h : h + 1, ri] = m + jnp.log(l)
        return 0

    lax.fori_loop(0, 2, qblock, 0)


def bwd_attention(
    q3, k3, v3, kt3, do3, lse, delta, dqt, dk, dv, put, heads, query_block, first_query, key_end, tiles, dtile, between
):
    hd = kt3.shape[1]
    dqt[...] = jnp.zeros_like(dqt)

    def kblock(J, _):
        rj = tile_rows(J)
        dk[...] = jnp.zeros_like(dk)
        dv[...] = jnp.zeros_like(dv)

        def qblock(u, _):
            ri = tile_rows(u)
            apart = query_block(u) - J
            for h in range(heads):
                s = mm(k3[h, rj, :], q3[h, ri, :], NT)
                if tiles is not None:
                    s = s + tiles[h, jnp.minimum(apart, 2)].astype(F32)
                p = jnp.exp(s - lse[h : h + 1, ri])
                dp = mm(v3[h, rj, :], do3[h, ri, :], NT)
                ds = (p * (dp - delta[h : h + 1, ri])).astype(BF16)
                dv[h] += mm(p.astype(BF16), do3[h, ri, :])
                dk[h, :, : q3.shape[2]] += mm(ds, q3[h, ri, :])
                dqt[h * hd : (h + 1) * hd, ri] += mm(kt3[h, :, rj], ds)
                if tiles is not None:
                    dtile[h, jnp.minimum(apart, 2)] += ds.astype(F32)
            return 0

        lax.fori_loop(first_query(J), 2, qblock, 0)
        put(J)
        between(J)
        return 0

    lax.fori_loop(0, key_end, kblock, 0)


def layer_kernel(dims, names, *refs):
    D, Hl, hd, FFL, N, NE, g, part = dims
    s = types.SimpleNamespace(**dict(zip(names, refs)))
    hw = Hl * hd
    H2 = 2 * Hl
    NC, NQ, NK = 2 * N, 4 * N, 4 * NE
    dp, z = lax.axis_index("dp"), lax.axis_index("mp")
    a, low = dp // g, dp % g
    c, r = a % 2, a // 2
    p, zb = z // 2, z % 2
    j = 2 * c + zb
    rx, ry, rd = r + 1 - 2 * (r % 2), (r + 2) % 4, 3 - r
    z1, z2 = z + 1 - 2 * zb, (z + 2) % 4
    stay, moved = c == p, c != p
    own = jnp.where(stay, z, 3 - z)
    beyond = jnp.where(stay, z1, 3 - z1)
    u_own = own // 2
    lo_block = jnp.minimum(own, 3 - own)
    hi_block = 3 - lo_block

    def device(r_, c_, z_):
        return {"dp": (2 * r_ + c_) * g + low, "mp": z_}

    sibling, across = device(r, 1 - c, z), device(r, c, z1)
    home = device(r, p, 3 - z)
    x_chip, y_chip = device(rx, c, z), device(ry, c, z)
    counter = [0]

    def slots(k):
        counter[0] += k
        return counter[0] - k

    def remote(src, dst, dev, send=None, recv=None):
        send = slots(1) if send is None else send
        recv = slots(1) if recv is None else recv
        return pltpu.make_async_remote_copy(
            src_ref=src, dst_ref=dst, send_sem=s.sems.at[send], recv_sem=s.sems.at[recv],
            device_id=dev, device_id_type=MESH_ID,
        )

    def local(src, dst, sem=None):
        return pltpu.make_async_copy(src, dst, s.sems.at[slots(1) if sem is None else sem])

    def either(cond, yes, no):
        @pl.when(cond)
        def _():
            yes()

        @pl.when(jnp.logical_not(cond))
        def _():
            no()

    unsent = []

    def chain(*steps):
        return steps

    def go(copy):
        copy.start()
        unsent.append(copy)
        return copy

    def block(i, n):
        return pl.ds(pl.multiple_of(i * n, n), n)

    def order(k):
        first = jnp.where(k < 2, own, beyond)
        return jnp.where(k % 2 == 0, first, 3 - first)

    def query_block(u):
        return jnp.where(u == 0, lo_block, hi_block)

    pieces = (s.p_sk, s.p_sv, s.p_sq, s.p_so, s.p_ck, s.p_cv, s.p_cq, s.p_co)
    loads = []
    for k, piece in enumerate(pieces):
        loads.append(local(piece, s.raw_t.at[k // 4] if k % 4 == 3 else s.raw.at[k - k // 4]))
    for k, piece in enumerate((s.p_gate, s.p_up, s.p_down)):
        loads.append(local(piece, s.wpack.at[:, pl.ds(8 * hw + k * FFL, FFL)]))
    for copy in loads:
        copy.start()

    barrier = pltpu.get_barrier_semaphore()
    peers = [device(r, (c + dc) % 2, (z + dz) % 4) for dz in range(4) for dc in range(2) if dz or dc] + [x_chip, y_chip, device(rd, c, z)]
    for peer in peers:
        pl.semaphore_signal(barrier, inc=1, device_id=peer, device_id_type=MESH_ID)
    for copy in loads:
        copy.wait()
    for k in range(8):
        piece = s.raw_t[k // 4].T if k % 4 == 3 else s.raw[k - k // 4]
        s.wpack[:, k * hw : (k + 1) * hw] = piece
    pl.semaphore_wait(barrier, len(peers))

    def swap_halves(src, dst):
        n = src.shape[0] // 2
        return [swap_of(src.at[pl.ds(k * n, n), :], dst.at[pl.ds(k * n, n), :]) for k in range(2)]

    def swap(src, dst):
        start, wait = swap_of(src, dst)
        start()
        return wait

    def swap_of(src, dst):
        far, near = remote(src, dst, home), local(src, dst)
        return chain(lambda: either(moved, far.start, near.start), lambda: either(moved, far.wait, near.wait))

    rows_a = D // 8
    chip = 2 * rows_a

    def spread(A, B):
        def at(ref, w):
            buf, slot, cols = ref
            return buf.at[w, cols] if slot is None else buf.at[slot, w, cols]

        def hop(ref, w, dev):
            return remote(at(ref, w), at(ref, w), dev)

        first = [hop(A, block(r, chip), x_chip), hop(B, block(r, chip), y_chip)]
        last = [hop(A, block(r // 2, 2 * chip), y_chip)] + [hop(B, block(q, chip), x_chip) for q in (r, ry)]

        def first_hop():
            go(first[0])
            go(first[1])

        def second_hop():
            first[0].wait_recv()
            go(last[0])
            first[1].wait_recv()
            go(last[1])
            go(last[2])

        def finish():
            for copy in last:
                copy.wait_recv()

        return first_hop, second_hop, finish

    def attn_weights(col, wide):
        C = pl.ds(col, wide)
        src = s.wpack.at[:, C]
        base = slots(4)
        dst = s.W2.at[zb, block(a, rows_a), C]
        out = [remote(src, dst, device(r, p, z_), None, base + 2 * zb + c) for z_ in (z2, z1)]
        near = local(src, dst)
        beside = remote(src, dst, sibling, None, base + 2 * zb + c)
        at = [s.W2.at[zb, block(2 * r + c_, rows_a), C] for c_ in range(2)]
        pass_on = [remote(at[c_], at[c_], across, None, base + 2 * zb + c_) for c_ in range(2)]
        here = [remote(src, at[0], sibling, 0, base + 2 * zb + c_) for c_ in range(2)]
        there = [remote(src, at[0], sibling, 0, base + 2 * (1 - zb) + c_) for c_ in range(2)]
        first_hop, second_hop, finish = spread((s.W2, 0, C), (s.W2, 1, C))

        def start():
            for copy in out:
                go(copy)
            either(stay, near.start, beside.start)

        def relay():
            def forward():
                beside.wait_send()
                for c_ in range(2):
                    here[c_].wait_recv()
                    pass_on[c_].start()

            def settle():
                near.wait()
                remote_side.wait_recv()

            either(moved, forward, settle)

        remote_side = remote(src, at[0], sibling, 0, base + 2 * zb + 1 - c)

        def first():
            for c_ in range(2):
                there[c_].wait_recv()
            pl.when(moved)(lambda: [copy.wait_send() for copy in pass_on] and None)
            first_hop()

        return chain(start, relay, first, second_hop, finish)

    def ff_weights(col, wide):
        src = s.wpack.at[:, pl.ds(col, wide)]
        dst = s.WF.at[block(a, rows_a), :]
        near, beside = local(src, dst), remote(src, dst, sibling)
        base = slots(2)
        out = remote(src, dst, device(r, p, z2), None, base + c)
        got = [remote(src, dst, sibling, 0, base + k) for k in range(2)]
        half = wide // 2
        first_hop, second_hop, finish = spread((s.WF, None, pl.ds(0, half)), (s.WF, None, pl.ds(half, half)))

        def start():
            go(out)
            either(stay, near.start, beside.start)

        def first():
            @pl.when(stay)
            def _():
                near.wait()
                beside.wait_recv()

            @pl.when(moved)
            def _():
                beside.wait_send()
                for copy in got:
                    copy.wait_recv()

            first_hop()

        return chain(start, first, second_hop, finish)

    def collect(A, B, bufs, send_home):
        ra1, rb1, ra2, rb2 = bufs

        def at(ref, w):
            buf, slot, cols = ref
            return buf.at[w, cols] if slot is None else buf.at[slot, w, cols]

        one = [
            go(remote(at(A, block(ry // 2, 2 * chip)), ra1, y_chip)),
            go(remote(at(B, block(rx, chip)), rb1.at[0], x_chip)),
            go(remote(at(B, block(rd, chip)), rb1.at[1], x_chip)),
        ]
        two = [remote(at(A, block(rx, chip)), ra2, x_chip), remote(at(B, block(ry, chip)), rb2, y_chip)]
        home_steps = send_home()

        def add(dst, src):
            n = 96
            for q in range(src.shape[0] // n):
                w = pl.ds(q * n, n)
                dst[w, :] = (dst[w, :].astype(F32) + src[w, :].astype(F32)).astype(BF16)

        def second():
            one[0].wait_recv()
            add(at(A, block(r // 2, 2 * chip)), ra1)
            go(two[0])
            one[2].wait_recv()
            add(at(B, block(ry, chip)), rb1.at[1])
            go(two[1])
            one[1].wait_recv()
            add(at(B, block(r, chip)), rb1.at[0])

        def third():
            two[0].wait_recv()
            add(at(A, block(r, chip)), ra2)
            two[1].wait_recv()
            add(at(B, block(r, chip)), rb2)
            home_steps[0]()

        return chain(second, third, *home_steps[1:])

    def to_home(grad, out):
        recv, near_recv, near_sem = slots(1), slots(1), slots(1)
        beside = remote(grad(2 * r + 1 - c), out(0), sibling, None, near_recv)
        near = local(grad(a), out(0), near_sem)
        far = [remote(grad(2 * r + k), out(1), device(r, k, z2), None, recv) for k in range(2)]

        def send():
            @pl.when(stay)
            def _():
                beside.start()
                near.start()

            @pl.when(moved)
            def _():
                for copy in far:
                    copy.start()

        def finish():
            @pl.when(stay)
            def _():
                beside.wait_send()
                near.wait()

            @pl.when(moved)
            def _():
                beside.wait_recv()
                for copy in far:
                    copy.wait_send()

            far[0].wait_recv()

        return send, finish

    def attn_home(col, wide, buf):
        C = pl.ds(col, wide)

        def build():
            pair = remote(s.dW2.at[1 - zb, block(r, chip), C], buf, across)
            send, finish = to_home(
                lambda i: s.dW2.at[zb, block(i, rows_a), C], lambda k: s.gz2.at[k, :, C]
            )

            def add_pair():
                pair.wait()
                for q in range(2):
                    w = pl.ds(q * rows_a, rows_a)
                    at = s.dW2.at[zb, block(2 * r + q, rows_a), C]
                    at[...] = (at[...].astype(F32) + buf[w, :].astype(F32)).astype(BF16)
                send()

            return pair.start, add_pair, finish

        return build

    def ff_home():
        return to_home(lambda i: s.dWF.at[block(i, rows_a), :], lambda k: s.gzf.at[k])

    def all_sum(buf, in1, in2):
        base1, base2 = slots(8), slots(4)
        me = 4 * c + z
        one, two = [], []
        for dz in range(4):
            for dc in range(2):
                if dz or dc:
                    c_, z_ = (c + dc) % 2, (z + dz) % 4
                    one.append((remote(in1.at[me], in1.at[me], device(r, c_, z_), None, base1 + me), base1 + 4 * c_ + z_))
        for dr in range(1, 4):
            r_ = (r + dr) % 4
            two.append((remote(in2.at[r], in2.at[r], device(r_, c, z), None, base2 + r), base2 + r_))

        def waits(copies, ref):
            for copy, recv in copies:
                copy.wait_send()
                remote(ref, ref, sibling, 0, recv).wait_recv()

        def start():
            in1[me] = buf[...]
            for copy, _ in one:
                copy.start()

        def middle():
            waits(one, in1.at[0])
            in2[r] = jnp.sum(in1[...], axis=0)
            for copy, _ in two:
                copy.start()

        def finish():
            waits(two, in2.at[0])
            buf[...] = jnp.sum(in2[...], axis=0)

        return chain(start, middle, finish)

    def gather(buf, n):
        half = n // 2
        copies = []
        for k in range(2):
            mine = buf.at[block(2 * own + k, half), :]
            there = buf.at[block(2 * beyond + k, half), :]
            copies.append((remote(mine, mine, across), remote(mine, mine, sibling), remote(there, there, sibling)))

        def start(k):
            copies[k][0].start()
            copies[k][1].start()

        def side():
            for copy in copies:
                copy[1].wait_recv()

        def forward():
            for copy in copies:
                copy[0].wait_recv()
                copy[2].start()

        def far():
            for copy in copies:
                copy[2].wait_recv()
                for one in copy:
                    one.wait_send()

        first, second, side, forward, far = chain(lambda: start(0), lambda: start(1), side, forward, far)
        return types.SimpleNamespace(start=lambda k: (first, second)[k](), side=side, forward=forward, far=far)

    def gather_all(buf, n):
        h = gather(buf, n)
        h.start(0)
        h.start(1)
        return h

    def each_block(h, body):
        h.side()
        lax.fori_loop(0, 2, lambda k, _: (body(order(k)), 0)[1], 0)
        h.forward()
        h.far()
        lax.fori_loop(2, 4, lambda k, _: (body(order(k)), 0)[1], 0)

    def gather_chip(buf):
        copies = []
        for k in range(2):
            mine = buf.at[block(2 * u_own + k, N // 2), :]
            copies.append(remote(mine, mine, sibling))

        def ready():
            for copy in copies:
                copy.wait_recv()

        first, second, ready = chain(lambda: go(copies[0]), lambda: go(copies[1]), ready)
        return (lambda k: (first, second)[k]()), ready

    def scatter(fn, bufs, res):
        s0, s1, zs, r0, r1, rz = bufs
        s0[...] = fn(order(3)).astype(BF16)
        d0 = remote(s0, r0, sibling)
        d0.start()
        res[...] = fn(order(2))
        d0.wait_recv()
        zs[...] = (res[...] + r0[...].astype(F32)).astype(BF16)
        n = res.shape[0] // 2
        parts = [pl.ds(k * n, n) for k in range(2)]
        dz = [remote(zs.at[w, :], rz.at[w, :], across) for w in parts]
        for copy in dz:
            copy.start()
        s1[...] = fn(order(1)).astype(BF16)
        d1 = remote(s1, r1, sibling)
        d1.start()
        res[...] = fn(order(0))

        def finish(k=None):
            for q in (0, 1) if k is None else (k,):
                if q == 0:
                    d1.wait_recv()
                w = parts[q]
                dz[q].wait_recv()
                res[w, :] += r1[w, :].astype(F32) + rz[w, :].astype(F32)
                if q == 1:
                    for copy in (d0, d1, *dz):
                        copy.wait_send()

        steps = chain(lambda: finish(0), lambda: finish(1))
        return lambda k=None: [step() for step in (steps if k is None else steps[k : k + 1])]

    def scatter_chip(fn, s0, r0, res):
        s0[...] = fn(1 - u_own).astype(BF16)
        d0 = remote(s0, r0, sibling)
        d0.start()
        res[...] = fn(u_own)

        def finish():
            d0.wait()
            res[...] += r0[...].astype(F32)

        return chain(finish)[0]

    CH = 64

    def chunks(n, body, init=0, half=None):
        lo, hi = (0, n // CH) if half is None else (half * n // (2 * CH), (half + 1) * n // (2 * CH))
        return lax.fori_loop(lo, hi, lambda i, v: body(pl.ds(pl.multiple_of(i * CH, CH), CH), v), init)

    gains = [s.gains[k : k + 1, :].astype(F32) for k in range(3)]

    def norm_rows(v, which, inv_ref, w, dst, dst_at):
        inv = lax.rsqrt(jnp.sum(v * v, axis=1, keepdims=True) / D + EPS)
        inv_ref[w, :] = jnp.broadcast_to(inv, (CH, 128))
        dst[dst_at, :] = (v * inv * gains[which]).astype(BF16)

    def rows_in(i, w):
        return pl.ds(pl.multiple_of(i * N + w.start, CH), CH)

    def norm_back_rows(d, v, which, inv):
        scaled = d * gains[which]
        dotted = jnp.sum(scaled * v, axis=1, keepdims=True)
        back = inv * scaled - v * (inv * inv * inv * dotted / D)
        return back, jnp.sum(d * v * inv, axis=0, keepdims=True)

    zero_gain = jnp.zeros((1, D), F32)
    o_ff = 8 * hw
    c_q, c_o, c_ckv, c_cq, c_co = 2 * hw, 3 * hw, 4 * hw, 6 * hw, 7 * hw

    w_kv = attn_weights(0, 2 * hw)
    w_qo = attn_weights(2 * hw, 2 * hw)
    swap_x = swap_halves(s.x, s.XN)
    w_kv[0]()
    w_qo[0]()
    for k in range(2):
        swap_x[k][0]()
    s.tab[z] = jnp.zeros_like(s.tab[z])
    s.tab[z, :Hl, :NB] = s.rel_bias[...].astype(F32)
    tab_base = slots(4)
    tab_out = [
        remote(s.tab.at[z], s.tab.at[z], device(r, c, (z + dz) % 4), None, tab_base + z) for dz in range(1, 4)
    ]
    for copy in tab_out:
        go(copy)
    s.len_out[...] = jnp.full(s.len_out.shape, s.seq_lengths[0], jnp.int32).astype(F32)
    lens = go(remote(s.len_out, s.len_in, sibling))
    lens.wait_recv()
    s.len_row[...] = jnp.where(stay, s.len_out[...], s.len_in[...])
    for dz in range(1, 4):
        other = s.tab.at[(z + dz) % 4]
        remote(other, other, sibling, 0, tab_base + (z + dz) % 4).wait_recv()
    span = 2 * TILE
    ids = lax.broadcasted_iota(jnp.int32, (NB, span), 0)
    buckets = s.rel_buckets[...]
    last = jnp.broadcast_to(buckets[:, -1:], (1, span))
    near = buckets[:, :span]
    after = jnp.concatenate([buckets[:, TILE:span], buckets[:, :TILE]], axis=1)

    def onehot(row):
        return (ids == row).astype(F32)

    key_at = lax.broadcasted_iota(jnp.int32, (TILE, TILE), 0)
    query_at = lax.broadcasted_iota(jnp.int32, (TILE, TILE), 1)
    w_kv[1]()
    for q in range(2):
        table = s.tab[2 * c + q, :, :NB]
        for k, row in enumerate((near, after, last)):
            s.vecs[8 * k : 8 * k + 8, :] = mm(table, onehot(row))

        def build(h, _):
            for k in range(3):
                wide = jnp.broadcast_to(s.vecs[pl.ds(8 * k + h, 1), :], (TILE, span))
                tile = pltpu.roll(wide, 0, 1, stride=1, stride_axis=0)[:, :TILE]
                s.tiles[Hl * q + h, k] = (jnp.where(query_at >= key_at, tile, NEG) if k == 0 else tile).astype(BF16)
            return 0

        lax.fori_loop(0, Hl, build, 0)
    w_qo[1]()
    length = s.len_row[0:1, :]
    lane = lax.broadcasted_iota(jnp.int32, (TILE, 128), 1)

    def extra_lane(i, _):
        w = tile_rows(i)
        at = lax.broadcasted_iota(jnp.int32, (TILE, 128), 0) + i * TILE
        mask = jnp.where((lane == hd) & (at.astype(F32) >= length), NEG, 0.0).astype(BF16)
        for h in range(H2):
            s.k3[h, w, :] = mask

        @pl.when(i < 2)
        def _():
            for h in range(H2):
                s.q3[h, w, :] = jnp.where(lane == hd, 1.0, 0.0).astype(BF16)

        return 0

    lax.fori_loop(0, 4, extra_lane, 0)
    ga = gather(s.FIRST, N)
    w_kv[2]()

    def norm_one(w, _):
        norm_rows(s.XN[w, :].astype(F32), 0, s.inv1, w, s.FIRST, rows_in(own, w))
        return 0

    for k in range(2):
        swap_x[k][1]()
        chunks(N, norm_one, 0, k)
        ga.start(k)
        if k == 0:
            w_qo[2]()
    w_kv[3]()
    w_ca = attn_weights(4 * hw, 2 * hw)
    w_cb = attn_weights(6 * hw, 2 * hw)
    w_f = ff_weights(o_ff, 3 * FFL)
    w_ca[0]()
    w_cb[0]()
    w_qo[3]()
    w_ca[1]()
    wait_e = swap(s.enc, s.EN)
    w_cb[1]()
    ga.side()
    ga.forward()
    w_f[0]()
    w_ca[2]()
    ga.far()
    wait_o = swap(s.og, s.ON)
    wait_e()
    s.ENC[block(own, NE), :] = s.EN[...]
    ge = gather_all(s.ENC, NE)
    w_kv[4]()
    w_qo[4]()

    def split(dst, h0, value, rows):
        for h in range(Hl):
            dst[h0 + h, rows, :hd] = value[:, h * hd : (h + 1) * hd]

    def project_one(k, _):
        i = order(k)
        w = block(i, N)
        f = s.FIRST[w, :]
        for q in range(2):
            y = mm(f, s.W2[q, :, : 2 * hw]).astype(BF16)
            split(s.k3, Hl * q, y[:, :hw], w)
            split(s.v3, Hl * q, y[:, hw:], w)

        @pl.when(k < 2)
        def _():
            for q in range(2):
                split(s.q3, Hl * q, mm(f, s.W2[q, :, c_q : c_q + hw]).astype(BF16), block(i // 2, N))

        return 0

    lax.fori_loop(0, 4, project_one, 0)
    w_cb[2]()
    w_ca[3]()

    def turn(dst, src):
        def one(h, _):
            dst[h] = src[h, :, :hd].T
            return 0

        lax.fori_loop(0, H2, one, 0)

    turn(s.t3, s.v3)
    s.WO[...] = s.W2[:, :, c_o : c_o + hw]

    def after_first(u, J):
        @pl.when(jnp.logical_and(u == 1, J == 0))
        def _():
            ge.side()
            ge.forward()
            w_cb[3]()
            w_f[1]()

    fwd_attention(s.q3, s.k3, s.t3, s.out_t, s.lse, H2, query_block, lambda I: I + 1, s.tiles, after_first)
    s.MIX[...] = s.out_t[...].T.astype(BF16)

    def out_proj(mix, weight):
        def fn(u):
            w = block(u, N)
            return mm(mix[w, :hw], weight[0], NT) + mm(mix[w, hw:], weight[1], NT)

        return fn

    end = scatter_chip(out_proj(s.MIX, s.WO), s.s0, s.i0, s.res)
    end()

    def norm_two(w, _):
        v = s.XN[w, :].astype(F32) + s.res[w, :]
        s.MID[w, :] = v
        norm_rows(v, 1, s.inv2, w, s.SECOND, rows_in(u_own, w))
        return 0

    second_go, second_ready = gather_chip(s.SECOND)
    for k in range(2):
        chunks(N, norm_two, 0, k)
        second_go(k)
    wait_o()
    own_pos = lax.broadcasted_iota(jnp.int32, (N, 128), 0) + own * N
    s.ok[...] = (own_pos.astype(F32) < length).astype(F32)

    def mask_rows(w, _):
        s.GF[rows_in(own, w), :] = (s.ON[w, :].astype(F32) * s.ok[w, :1]).astype(BF16)
        return 0

    chunks(N, mask_rows)
    gg = gather_all(s.GF, N)
    ge.far()
    w_ca[4]()

    def project_enc(i, _):
        w = block(i, N)
        e = s.ENC[w, :]
        for q in range(2):
            y = mm(e, s.W2[q, :, c_ckv : c_ckv + 2 * hw]).astype(BF16)
            split(s.ck3, Hl * q, y[:, :hw], w)
            split(s.cv3, Hl * q, y[:, hw:], w)
        return 0

    lax.fori_loop(0, NK // N, project_enc, 0)
    turn(s.ct3, s.cv3)
    w_cb[4]()
    s.WCO[...] = s.W2[:, :, c_co : c_co + hw]
    second_ready()

    def project_two(u, _):
        w = block(u, N)
        t = s.SECOND[w, :]
        for q in range(2):
            split(s.cq3, Hl * q, mm(t, s.W2[q, :, c_cq : c_cq + hw]).astype(BF16), w)
        return 0

    lax.fori_loop(0, 2, project_two, 0)
    def after_cross(u, J):
        @pl.when(jnp.logical_and(u == 0, J == 0))
        def _():
            w_f[2]()

    fwd_attention(
        s.cq3, s.ck3, s.ct3, s.out_t2, s.lse2, H2, query_block, lambda I: NK // TILE, None, after_cross
    )
    s.MIX2[...] = s.out_t2[...].T.astype(BF16)
    scatter_chip(out_proj(s.MIX2, s.WCO), s.s0, s.i1, s.res)()

    def norm_three(w, _):
        v = s.MID[w, :] + s.res[w, :]
        s.LAT[w, :] = v
        norm_rows(v, 2, s.inv3, w, s.THIRD, rows_in(own, w))
        return 0

    gt = gather(s.THIRD, N)
    for k in range(2):
        chunks(N, norm_three, 0, k)
        gt.start(k)
    gg.side()
    gg.forward()
    gg.far()
    w_f[3]()
    root = 0.7978845608028654
    SUB = 128

    def feed(i):
        def sub(u, _):
            w = pl.ds(pl.multiple_of(i * N + u * SUB, SUB), SUB)
            t = s.THIRD[w, :]
            gate = mm(t, s.WF[:, :FFL])
            up = mm(t, s.WF[:, FFL : 2 * FFL])
            dh = mm(s.GF[w, :], s.WF[:, 2 * FFL :])
            sq = gate * gate
            th = jnp.tanh(root * gate * (1.0 + 0.044715 * sq))
            half = 0.5 * (1.0 + th)
            act = gate * half
            slope = half + 0.5 * gate * (1.0 - th * th) * root * (1.0 + 3 * 0.044715 * sq)
            s.HID[w, :] = (act * up).astype(BF16)
            s.DGU[w, :FFL] = (dh * up * slope).astype(BF16)
            s.DGU[w, FFL:] = (dh * act).astype(BF16)
            return 0

        lax.fori_loop(0, N // SUB, sub, 0)

    each_block(gt, feed)
    end = scatter(
        lambda i: mm(s.DGU[block(i, N), :], s.WF[:, : 2 * FFL], NT), (s.s0, s.s1, s.zs, s.a0, s.a1, s.az), s.res
    )

    def weight_grad(put, parts):
        def step(q, _):
            m = pl.ds(pl.multiple_of(q * 256, 256), 256)
            total = None
            for left, right in parts:
                y = mm(left(m), right, TN)
                total = y if total is None else total + y
            put(m, total.astype(BF16))
            return 0

        lax.fori_loop(0, D // 256, step, 0)

    def put_f(col, n):
        def put(m, v):
            s.dWF[m, col : col + n] = v

        return put

    def put_slots(col, n):
        def put(m, v):
            for q in range(2):
                s.dW2[q, m, col : col + n] = v[:, q * n : (q + 1) * n]

        return put

    weight_grad(put_f(2 * FFL, FFL), [(lambda m: s.GF[:, m], s.HID[...])])
    weight_grad(put_f(0, 2 * FFL), [(lambda m: s.THIRD[:, m], s.DGU[...])])
    half_f = 3 * FFL // 2
    grad_f = collect(
        (s.dWF, None, pl.ds(0, half_f)), (s.dWF, None, pl.ds(half_f, half_f)), (s.ra1, s.rb1, s.ra2, s.rb2), ff_home
    )
    turn(s.ct3, s.ck3)
    turn(s.t3, s.k3)
    s.dtile[...] = jnp.zeros_like(s.dtile)

    def back_three(w, acc):
        back, part_gain = norm_back_rows(s.res[w, :], s.LAT[w, :], 2, s.inv3[w, :1])
        d = s.GF[rows_in(own, w), :].astype(F32) + back
        s.GR[w, :] = d
        s.DL[rows_in(u_own, w), :] = d.astype(BF16)
        return acc + part_gain

    dl_go, dl_ready = gather_chip(s.DL)
    gain_three = zero_gain
    for k in range(2):
        end(k)
        gain_three = chunks(N, back_three, gain_three, k)
        dl_go(k)
    end_out = scatter(
        lambda i: mm(s.HID[block(i, N), :], s.WF[:, 2 * FFL :], NT), (s.s0, s.s1, s.zs, s.b0, s.b1, s.bz), s.res
    )


    def back_heads(src, weight, out_t):
        def body(u, _):
            w = block(u, N)
            for q in range(2):
                y = mm(src[w, :], weight[q]).astype(BF16)
                split(s.do3, Hl * q, y, w)
                yt = y.astype(F32).T
                for h in range(Hl):
                    g_h = Hl * q + h
                    both = yt[h * hd : (h + 1) * hd, :] * out_t[g_h * hd : (g_h + 1) * hd, w]
                    s.delta[g_h : g_h + 1, w] = jnp.sum(both, axis=0, keepdims=True)
            return 0

        lax.fori_loop(0, 2, body, 0)

    dl_ready()
    back_heads(s.DL, s.WCO, s.out_t2)

    def put_cross(J):
        w = tile_rows(J)
        for h in range(H2):
            q, hh = h // Hl, h % Hl
            at = 2 * hw * q + hh * hd
            s.DGU[w, at : at + hd] = s.dk[h, :, :hd].astype(BF16)
            s.DGU[w, at + hw : at + hw + hd] = s.dv[h].astype(BF16)

    def cross_between(J):
        @pl.when(J == 0)
        def _():
            grad_f[0]()

    bwd_attention(
        s.cq3, s.ck3, s.cv3, s.ct3, s.do3, s.lse2, s.delta, s.out_t2, s.dk, s.dv, put_cross, H2, query_block,
        lambda J: 0, NK // TILE, None, None, cross_between,
    )
    s.DQ[...] = s.out_t2[...].T.astype(BF16)

    def query_grad(col):
        def fn(u):
            w = block(u, N)
            return mm(s.DQ[w, :hw], s.W2[0, :, col : col + hw], NT) + mm(s.DQ[w, hw:], s.W2[1, :, col : col + hw], NT)

        return fn

    def put_out(w, _):
        s.ON[w, :] = (s.LAT[w, :] + s.res[w, :]).astype(BF16)
        return 0

    end_out()
    chunks(N, put_out)
    wait_lo = swap(s.ON, s.lo)
    end = scatter_chip(query_grad(c_cq), s.s0, s.i2, s.res)

    def kv_grad(n, col):
        def fn(i):
            w = block(i, n)
            return (
                mm(s.DGU[w, : 2 * hw], s.W2[0, :, col : col + 2 * hw], NT)
                + mm(s.DGU[w, 2 * hw : 4 * hw], s.W2[1, :, col : col + 2 * hw], NT)
            )

        return fn

    weight_grad(put_slots(c_cq, hw), [(lambda m: s.SECOND[:, m], s.DQ[...])])
    weight_grad(put_slots(c_co, hw), [(lambda m: s.DL[:, m], s.MIX2[...])])
    weight_grad(put_slots(c_ckv, 2 * hw), [(lambda m: s.ENC[:, m], s.DGU[:NK, : 4 * hw])])
    grad_f[1]()
    C4 = pl.ds(4 * hw, 4 * hw)
    grad_c = collect((s.dW2, 0, C4), (s.dW2, 1, C4), (s.qa1, s.qb1, s.qa2, s.qb2), attn_home(4 * hw, 4 * hw, s.pair1))
    end()

    def back_two(w, acc):
        back, part_gain = norm_back_rows(s.res[w, :], s.MID[w, :], 1, s.inv2[w, :1])
        d = s.GR[w, :] + back
        s.GR[w, :] = d
        s.DM[rows_in(u_own, w), :] = d.astype(BF16)
        return acc + part_gain

    dm_go, dm_ready = gather_chip(s.DM)
    gain_two = zero_gain
    for k in range(2):
        gain_two = chunks(N, back_two, gain_two, k)
        dm_go(k)
    end_enc = scatter(kv_grad(NE, c_ckv), (s.e0, s.e1, s.es, s.f0, s.f1, s.fz), s.rese)
    end_enc()
    s.EN[...] = s.rese[...].astype(BF16)
    wait_eo = swap(s.EN, s.eg)

    dm_ready()
    back_heads(s.DM, s.WO, s.out_t)
    weight_grad(put_slots(c_o, hw), [(lambda m: s.DM[:, m], s.MIX[...])])

    def self_between(J):
        @pl.when(J == 0)
        def _():
            grad_c[0]()

    bwd_attention(
        s.q3, s.k3, s.v3, s.t3, s.do3, s.lse, s.delta, s.out_t, s.dk, s.dv, put_cross, H2, query_block,
        lambda J: jnp.where(J <= lo_block, 0, 1), hi_block + 1, s.tiles, s.dtile, self_between,
    )

    def clear(J, _):
        s.DGU[tile_rows(J), :] = jnp.zeros((TILE, s.DGU.shape[1]), BF16)
        return 0

    lax.fori_loop(hi_block + 1, 4, clear, 0)
    s.DQ[...] = s.out_t[...].T.astype(BF16)
    own_part = query_grad(c_q)
    other_part = kv_grad(N, 0)

    def scatter_first(bufs, res):
        s0, s1, zs, r0, r1, rz = bufs
        s0[...] = other_part(order(3)).astype(BF16)
        d0 = remote(s0, r0, sibling)
        d0.start()
        res[...] = other_part(order(2))
        d0.wait_recv()
        zs[...] = (res[...] + r0[...].astype(F32)).astype(BF16)
        n = res.shape[0] // 2
        parts = [pl.ds(k * n, n) for k in range(2)]
        dz = [remote(zs.at[w, :], rz.at[w, :], across) for w in parts]
        for copy in dz:
            copy.start()
        s1[...] = (other_part(3 - own) + own_part(1 - u_own)).astype(BF16)
        d1 = remote(s1, r1, sibling)
        d1.start()
        res[...] = other_part(own) + own_part(u_own)

        def finish(k=None):
            for q in (0, 1) if k is None else (k,):
                if q == 0:
                    d1.wait_recv()
                w = parts[q]
                dz[q].wait_recv()
                res[w, :] += r1[w, :].astype(F32) + rz[w, :].astype(F32)
                if q == 1:
                    for copy in (d0, d1, *dz):
                        copy.wait_send()

        steps = chain(lambda: finish(0), lambda: finish(1))
        return lambda k=None: [step() for step in (steps if k is None else steps[k : k + 1])]

    KV, QO = pl.ds(0, 2 * hw), pl.ds(2 * hw, 2 * hw)
    bufs = (s.ra1, s.rb1, s.ra2, s.rb2)
    cut = lambda k: tuple(x.at[..., pl.ds(k * 2 * hw, 2 * hw)] for x in bufs)
    grad_c[1]()
    weight_grad(put_slots(0, 2 * hw), [(lambda m: s.FIRST[:, m], s.DGU[:, : 4 * hw])])
    grad_kv = collect((s.dW2, 0, KV), (s.dW2, 1, KV), cut(0), attn_home(0, 2 * hw, s.pair2))
    weight_grad(
        put_slots(c_q, hw),
        [
            (lambda m: s.FIRST[tile_rows(lo_block), m], s.DQ[:N, :]),
            (lambda m: s.FIRST[tile_rows(hi_block), m], s.DQ[N:, :]),
        ],
    )
    grad_qo = collect((s.dW2, 0, QO), (s.dW2, 1, QO), cut(1), attn_home(2 * hw, 2 * hw, s.pair3))
    end = scatter_first((s.s0, s.s1, s.zs, s.a0, s.a1, s.az), s.res)
    grad_c[2]()
    grad_kv[0]()
    s.small[...] = jnp.zeros_like(s.small)
    flip = (key_at + query_at == TILE - 1).astype(BF16)
    blank = jnp.zeros((TILE, TILE), F32)
    head_row = lax.broadcasted_iota(jnp.int32, (16, span), 0)
    gap = lax.broadcasted_iota(jnp.int32, (1, span), 1)
    near_back = jnp.where(gap >= TILE - 1, pltpu.roll(near, TILE - 1, 1), -1)
    next_back = jnp.where(gap < span - 1, pltpu.roll(near, span - 1, 1), -1)
    for k, row in enumerate((near_back, next_back)):

        def line_up(h, diag):
            full = s.dtile[h, k]
            high = full.astype(BF16)
            rest = full - high.astype(F32)
            mid = rest.astype(BF16)
            turned = mm(flip, high) + mm(flip, mid) + mm(flip, (rest - mid.astype(F32)).astype(BF16))
            lined = pltpu.roll(jnp.concatenate([turned, blank], axis=1), 0, 1, stride=1, stride_axis=0)
            return jnp.where(head_row == H2 * c + h, jnp.sum(lined, axis=0, keepdims=True), diag)

        diag = lax.fori_loop(0, H2, line_up, jnp.zeros((16, span), F32))
        s.small[:16, :NB] += lax.dot_general(
            diag, onehot(row), NT, precision=lax.Precision.HIGHEST, preferred_element_type=F32
        )
    far_row = lax.broadcasted_iota(jnp.int32, (16, 1), 0)

    def far_total(h, acc):
        total = jnp.sum(jnp.sum(s.dtile[h, 2], axis=0, keepdims=True), axis=1, keepdims=True)
        return jnp.where(far_row == H2 * c + h, total, acc)

    far_sum = lax.fori_loop(0, H2, far_total, jnp.zeros((16, 1), F32))
    is_last = (lax.broadcasted_iota(jnp.int32, (1, NB), 1) == buckets[:, -1:]).astype(F32)
    s.small[:16, :NB] += far_sum * is_last

    def put_rows(buf, at, row):
        for k in range(D // 128):
            buf[at + k : at + k + 1, :] = row[:, 128 * k : 128 * (k + 1)]

    put_rows(s.small, 16, gain_two)
    put_rows(s.small, 24, gain_three)
    sum_small = all_sum(s.small, s.small1, s.small2)
    sum_small[0]()
    def back_one(w, acc):
        back, part_gain = norm_back_rows(s.res[w, :], s.XN[w, :].astype(F32), 0, s.inv1[w, :1])
        s.i0[w, :] = (s.GR[w, :] + back).astype(BF16)
        return acc + part_gain

    swap_dg = swap_halves(s.i0, s.dg)
    wait_dg = [pair[1] for pair in swap_dg]
    gain_one = zero_gain
    for k in range(2):
        end(k)
        gain_one = chunks(N, back_one, gain_one, k)
        swap_dg[k][0]()
    grad_qo[0]()
    s.late[...] = jnp.zeros_like(s.late)
    put_rows(s.late, 0, gain_one)
    sum_late = all_sum(s.late, s.late1, s.late2)
    sum_late[0]()
    grad_kv[1]()
    sum_small[1]()
    grad_qo[1]()
    sum_late[1]()
    grad_kv[2]()
    sum_small[2]()
    grad_qo[2]()
    sum_late[2]()
    s.sm[...] = jnp.zeros_like(s.sm)
    for k in range(D // 128):
        w = slice(128 * k, 128 * (k + 1))
        s.sm[0:1, w] = s.late[k : k + 1, :]
        s.sm[1:2, w] = s.small[16 + k : 17 + k, :]
        s.sm[2:3, w] = s.small[24 + k : 25 + k, :]
    s.sm[:, D:] = s.small[:16, :]
    wait_lo()
    wait_eo()
    grad_f[2]()
    grad_c[3]()
    grad_kv[3]()
    for wait in wait_dg:
        wait()
    grad_qo[3]()
    for copy in unsent:
        copy.wait_send()
    assert counter[0] <= part, counter[0]


def layer_call(pieces, x, enc, og, gains, rel_bias, seq_lengths, rel_buckets, dims):
    D, Hl, hd, FFL, N, NE, g, part = dims
    hw = Hl * hd
    H2, NC, NQ, NK = 2 * Hl, 2 * N, 4 * N, 4 * NE
    ra = D // 8
    vm, any_ = pl.BlockSpec(memory_space=pltpu.VMEM), pl.BlockSpec(memory_space=pl.ANY)
    sm_ = pl.BlockSpec(memory_space=pltpu.SMEM)
    piece_names = ("p_sk", "p_sv", "p_sq", "p_so", "p_ck", "p_cv", "p_cq", "p_co", "p_gate", "p_up", "p_down")
    ins = dict({k: any_ for k in piece_names}, x=any_, enc=any_, og=any_, gains=vm, rel_bias=vm, seq_lengths=sm_, rel_buckets=vm)
    outs = dict(
        lo=((N, D), BF16, any_), dg=((N, D), BF16, any_), eg=((NE, D), BF16, any_),
        gz2=((2, ra, 8 * hw), BF16, any_), gzf=((2, ra, 3 * FFL), BF16, any_), sm=((16, D + 128), F32, vm),
    )
    sc = {}

    def add(dtype, **shapes):
        for name, shape in shapes.items():
            sc[name] = pltpu.VMEM(shape, dtype)

    add(BF16, wpack=(ra, 8 * hw + 3 * FFL), raw=(6, ra, hw), raw_t=(2, hw, ra))
    add(BF16, pair1=(D // 4, 4 * hw), pair2=(D // 4, 2 * hw), pair3=(D // 4, 2 * hw))
    add(BF16, W2=(2, D, 8 * hw), dW2=(2, D, 8 * hw), WF=(D, 3 * FFL), dWF=(D, 3 * FFL), WO=(2, D, hw), WCO=(2, D, hw))
    for k in "rq":
        add(BF16, **{k + "a1": (D // 2, 4 * hw), k + "b1": (2, D // 4, 4 * hw), k + "a2": (D // 4, 4 * hw), k + "b2": (D // 4, 4 * hw)})
    add(BF16, FIRST=(NQ, D), THIRD=(NQ, D), GF=(NQ, D), SECOND=(NC, D), DL=(NC, D), DM=(NC, D), ENC=(NK, D))
    add(BF16, **{k: (N, D) for k in ("s0", "s1", "zs", "a0", "a1", "az", "b0", "b1", "bz", "i0", "i1", "i2", "XN", "ON")})
    add(BF16, **{k: (NE, D) for k in ("e0", "e1", "es", "f0", "f1", "fz", "EN")})
    add(F32, **{k: (N, D) for k in ("MID", "LAT", "GR", "res")}, rese=(NE, D))
    add(F32, inv1=(N, 128), inv2=(N, 128), inv3=(N, 128), ok=(N, 128))
    add(BF16, q3=(H2, NC, 128), k3=(H2, NQ, 128), v3=(H2, NQ, hd), cq3=(H2, NC, hd), ck3=(H2, NK, hd), cv3=(H2, NK, hd))
    add(BF16, do3=(H2, NC, hd), t3=(H2, hd, NQ), ct3=(H2, hd, NK))
    add(F32, out_t=(2 * hw, NC), out_t2=(2 * hw, NC), lse=(8, NC), lse2=(8, NC), delta=(8, NC))
    add(F32, dk=(H2, TILE, 128), dv=(H2, TILE, hd))
    add(BF16, MIX=(NC, 2 * hw), MIX2=(NC, 2 * hw), HID=(NQ, FFL), DGU=(NQ, 2 * FFL), DQ=(NC, 2 * hw))
    add(BF16, tiles=(H2, 3, TILE, TILE))
    add(F32, dtile=(H2, 3, TILE, TILE), vecs=(24, 2 * TILE))
    add(F32, tab=(4, 8, 128), len_out=(8, 128), len_in=(8, 128), len_row=(8, 128))
    add(F32, small=(32, 128), small1=(8, 32, 128), small2=(4, 32, 128))
    add(F32, late=(8, 128), late1=(8, 8, 128), late2=(4, 8, 128))
    names = list(ins) + list(outs) + list(sc) + ["sems"]
    return pl.pallas_call(
        functools.partial(layer_kernel, dims, names),
        out_shape=[jax.ShapeDtypeStruct(o[0], o[1]) for o in outs.values()],
        in_specs=list(ins.values()),
        out_specs=[o[2] for o in outs.values()],
        scratch_shapes=list(sc.values()) + [pltpu.SemaphoreType.DMA((part,))],
        compiler_params=pltpu.CompilerParams(collective_id=0, has_side_effects=True, vmem_limit_bytes=67043328),
        name="layer",
    )(*pieces, x, enc, og, gains, rel_bias, seq_lengths, rel_buckets)


def finish_kernel(dims, lo, dg, eg, gz2, gzf, sm, *outs):
    D, Hl, hd, FFL, N, NE, g, part = dims
    hw = Hl * hd
    o_lo, o_dg, o_eg, o_gains, o_bias, sq, sk, sv, so, cq, ck, cv, co, gg, gu, gd = outs
    o_lo[...] = lo[...]
    o_dg[...] = dg[...].astype(F32)
    o_eg[...] = eg[...].astype(F32)
    o_gains[...] = sm[:3, :D]
    o_bias[...] = sm[: 4 * Hl, D : D + NB]

    def total(col, n):
        w = pl.ds(col, n)
        return gz2[0, :, w].astype(F32) + gz2[1, :, w].astype(F32)

    for base, parts in ((0, (sk, sv, sq, so)), (4 * hw, (ck, cv, cq, co))):
        y = total(base, 4 * hw)
        for k, out in enumerate(parts):
            v = y[:, k * hw : (k + 1) * hw]
            out[...] = v if k < 3 else v.T
    f = gzf[0].astype(F32) + gzf[1].astype(F32)
    gg[...] = f[:, :FFL]
    gu[...] = f[:, FFL : 2 * FFL]
    gd[...] = f[:, 2 * FFL :]


def finish_call(dims, lo, dg, eg, gz2, gzf, sm):
    D, Hl, hd, FFL, N, NE, g, part = dims
    hw, ra = Hl * hd, D // 8
    vm = pl.BlockSpec(memory_space=pltpu.VMEM)
    shapes = [((N, D), BF16), ((N, D), F32), ((NE, D), F32), ((3, D), F32), ((4 * Hl, NB), F32)]
    shapes += [((ra, hw), F32)] * 3 + [((hw, ra), F32)] + [((ra, hw), F32)] * 3 + [((hw, ra), F32)]
    shapes += [((ra, FFL), F32)] * 3
    return pl.pallas_call(
        functools.partial(finish_kernel, dims),
        out_shape=[jax.ShapeDtypeStruct(*v) for v in shapes],
        in_specs=[vm] * 6,
        out_specs=[vm] * len(shapes),
        name="finish",
    )(lo, dg, eg, gz2, gzf, sm)


def exchange(value, step, size):
    return lax.ppermute(value, "dp", [(i, i ^ step) for i in range(size)])


def per_device(
    decoder_in, encoder_out, seq_lengths, rel_buckets, norm_gains, rel_bias,
    self_query, self_key, self_value, self_out, cross_query, cross_key, cross_value, cross_out,
    gate_weight, up_weight, down_weight, out_grad,
):
    width = decoder_in.shape[1]
    heads, w, f = rel_bias.shape[1], self_query.shape[1], gate_weight.shape[1]
    size = lax.axis_size("dp")
    g = size // 8
    rows, erows = decoder_in.shape[0], encoder_out.shape[0]
    pieces = (
        self_key, self_value, self_query, self_out, cross_key, cross_value, cross_query, cross_out,
        gate_weight, up_weight, down_weight.T,
    )
    if g > 1:
        wpack = jnp.concatenate([x.T if k in (3, 7) else x for k, x in enumerate(pieces)], axis=1)
        step = 1
        while step < g:
            other = exchange(wpack, step, size)
            upper = (lax.axis_index("dp") // step) % 2
            wpack = jnp.where(upper == 1, jnp.concatenate([other, wpack], 0), jnp.concatenate([wpack, other], 0))
            step *= 2
        cols = [wpack[:, k * w : (k + 1) * w] for k in range(8)]
        cols[3], cols[7] = cols[3].T, cols[7].T
        pieces = (*cols, *(wpack[:, 8 * w + k * f : 8 * w + (k + 1) * f] for k in range(3)))
    dims = (width, heads, w // heads, f, rows, erows, g, 480)
    lo, dg, eg, gz2, gzf, sm = layer_call(
        pieces, decoder_in, encoder_out, out_grad, norm_gains, rel_bias.T, seq_lengths, rel_buckets.reshape(1, -1), dims
    )
    if g == 1:
        outs = list(finish_call(dims, lo, dg, eg, gz2, gzf, sm))
        outs[4], outs[15] = outs[4].T, outs[15].T
        return tuple(outs)
    gw = jnp.concatenate([jnp.sum(gz2.astype(F32), axis=0), jnp.sum(gzf.astype(F32), axis=0)], axis=1)
    step = g // 2
    while step >= 1:
        upper = (lax.axis_index("dp") // step) % 2
        n = gw.shape[0] // 2
        keep = jnp.where(upper == 1, gw[n:], gw[:n])
        give = jnp.where(upper == 1, gw[:n], gw[n:])
        gw = keep + exchange(give, step, size)
        sm = sm + exchange(sm, step, size)
        step //= 2
    col = lambda k: gw[:, k * w : (k + 1) * w]
    return (
        lo, dg.astype(F32), eg.astype(F32), sm[:3, :width], sm[: 4 * heads, width : width + NB].T,
        col(2), col(0), col(1), col(3).T, col(6), col(4), col(5), col(7).T,
        gw[:, 8 * w : 8 * w + f], gw[:, 8 * w + f : 8 * w + 2 * f], gw[:, 8 * w + 2 * f :].T,
    )


def solution(mesh):
    return jax.shard_map(
        per_device,
        mesh=mesh,
        in_specs=(
            P(("dp", "mp"), None),
            P(("dp", "mp"), None),
            P("dp"),
            P(),
            P(),
            P(None, "mp"),
            P("dp", "mp"),
            P("dp", "mp"),
            P("dp", "mp"),
            P("mp", "dp"),
            P("dp", "mp"),
            P("dp", "mp"),
            P("dp", "mp"),
            P("mp", "dp"),
            P("dp", "mp"),
            P("dp", "mp"),
            P("mp", "dp"),
            P(("dp", "mp"), None),
        ),
        out_specs=(
            P(("dp", "mp"), None),
            P(("dp", "mp"), None),
            P(("dp", "mp"), None),
            P(),
            P(),
            P("dp", "mp"),
            P("dp", "mp"),
            P("dp", "mp"),
            P("mp", "dp"),
            P("dp", "mp"),
            P("dp", "mp"),
            P("dp", "mp"),
            P("mp", "dp"),
            P("dp", "mp"),
            P("dp", "mp"),
            P("mp", "dp"),
        ),
        check_vma=False,
    )
```

```python
import functools
import types

import jax
import jax.numpy as jnp
from jax import lax
from jax.experimental import pallas as pl
from jax.experimental.pallas import tpu as pltpu
from jax.sharding import PartitionSpec as P

NB = 32
EPS = 1e-06
F32 = jnp.float32
BF16 = jnp.bfloat16
NEG = -1e30
TILE = 256
NN = (((1,), (0,)), ((), ()))
NT = (((1,), (1,)), ((), ()))
TN = (((0,), (0,)), ((), ()))
MESH_ID = pl.DeviceIdType.MESH


def mm(a, b, dims=NN):
    return lax.dot_general(a, b, dims, preferred_element_type=F32)


def tile_rows(i):
    return pl.ds(pl.multiple_of(i * TILE, TILE), TILE)


def fwd_attention(q3, k3, vt3, out_t, lse, heads, query_block, key_blocks, tiles, between):
    hd = vt3.shape[1]

    def qblock(u, _):
        ri = tile_rows(u)
        I = query_block(u)

        def kblock(J, carry):
            rj = tile_rows(J)
            new = []
            for h in range(heads):
                m, l, acc = carry[h]
                s = mm(k3[h, rj, :], q3[h, ri, :], NT)
                if tiles is not None:
                    s = s + tiles[h, jnp.minimum(I - J, 2)].astype(F32)
                m2 = jnp.maximum(m, jnp.max(s, axis=0, keepdims=True))
                a = jnp.exp(m - m2)
                p = jnp.exp(s - m2)
                l2 = l * a + jnp.sum(p, axis=0, keepdims=True)
                new.append((m2, l2, acc * a + mm(vt3[h, :, rj], p.astype(BF16))))
            between(u, J)
            return tuple(new)

        init = tuple(
            (jnp.full((1, TILE), NEG, F32), jnp.zeros((1, TILE), F32), jnp.zeros((hd, TILE), F32)) for _ in range(heads)
        )
        res = lax.fori_loop(0, key_blocks(I), kblock, init)
        for h in range(heads):
            m, l, acc = res[h]
            out_t[h * hd : (h + 1) * hd, ri] = acc / l
            lse[h : h + 1, ri] = m + jnp.log(l)
        return 0

    lax.fori_loop(0, 2, qblock, 0)


def bwd_attention(
    q3, k3, v3, kt3, do3, lse, delta, dqt, dk, dv, put, heads, query_block, first_query, key_end, tiles, dtile, between
):
    hd = kt3.shape[1]
    dqt[...] = jnp.zeros_like(dqt)

    def kblock(J, _):
        rj = tile_rows(J)
        dk[...] = jnp.zeros_like(dk)
        dv[...] = jnp.zeros_like(dv)

        def qblock(u, _):
            ri = tile_rows(u)
            apart = query_block(u) - J
            for h in range(heads):
                s = mm(k3[h, rj, :], q3[h, ri, :], NT)
                if tiles is not None:
                    s = s + tiles[h, jnp.minimum(apart, 2)].astype(F32)
                p = jnp.exp(s - lse[h : h + 1, ri])
                dp = mm(v3[h, rj, :], do3[h, ri, :], NT)
                ds = (p * (dp - delta[h : h + 1, ri])).astype(BF16)
                dv[h] += mm(p.astype(BF16), do3[h, ri, :])
                dk[h, :, : q3.shape[2]] += mm(ds, q3[h, ri, :])
                dqt[h * hd : (h + 1) * hd, ri] += mm(kt3[h, :, rj], ds)
                if tiles is not None:
                    dtile[h, jnp.minimum(apart, 2)] += ds.astype(F32)
            return 0

        lax.fori_loop(first_query(J), 2, qblock, 0)
        put(J)
        between(J)
        return 0

    lax.fori_loop(0, key_end, kblock, 0)


def layer_kernel(dims, names, *refs):
    D, Hl, hd, FFL, N, NE, g, part = dims
    s = types.SimpleNamespace(**dict(zip(names, refs)))
    hw = Hl * hd
    H2 = 2 * Hl
    NC, NQ, NK = 2 * N, 4 * N, 4 * NE
    dp, z = lax.axis_index("dp"), lax.axis_index("mp")
    a, low = dp // g, dp % g
    c, r = a % 2, a // 2
    p, zb = z // 2, z % 2
    j = 2 * c + zb
    rx, ry, rd = r + 1 - 2 * (r % 2), (r + 2) % 4, 3 - r
    z1, z2 = z + 1 - 2 * zb, (z + 2) % 4
    stay, moved = c == p, c != p
    own = jnp.where(stay, z, 3 - z)
    beyond = jnp.where(stay, z1, 3 - z1)
    u_own = own // 2
    lo_block = jnp.minimum(own, 3 - own)
    hi_block = 3 - lo_block

    def device(r_, c_, z_):
        return {"dp": (2 * r_ + c_) * g + low, "mp": z_}

    sibling, across = device(r, 1 - c, z), device(r, c, z1)
    home = device(r, p, 3 - z)
    x_chip, y_chip = device(rx, c, z), device(ry, c, z)
    counter = [0]

    def slots(k):
        counter[0] += k
        return counter[0] - k

    def remote(src, dst, dev, send=None, recv=None):
        send = slots(1) if send is None else send
        recv = slots(1) if recv is None else recv
        return pltpu.make_async_remote_copy(
            src_ref=src, dst_ref=dst, send_sem=s.sems.at[send], recv_sem=s.sems.at[recv],
            device_id=dev, device_id_type=MESH_ID,
        )

    def local(src, dst, sem=None):
        return pltpu.make_async_copy(src, dst, s.sems.at[slots(1) if sem is None else sem])

    def either(cond, yes, no):
        @pl.when(cond)
        def _():
            yes()

        @pl.when(jnp.logical_not(cond))
        def _():
            no()

    unsent = []

    def chain(*steps):
        return steps

    def go(copy):
        copy.start()
        unsent.append(copy)
        return copy

    def block(i, n):
        return pl.ds(pl.multiple_of(i * n, n), n)

    def order(k):
        first = jnp.where(k < 2, own, beyond)
        return jnp.where(k % 2 == 0, first, 3 - first)

    def query_block(u):
        return jnp.where(u == 0, lo_block, hi_block)

    pieces = (s.p_sk, s.p_sv, s.p_sq, s.p_so, s.p_ck, s.p_cv, s.p_cq, s.p_co)
    loads = []
    for k, piece in enumerate(pieces):
        loads.append(local(piece, s.raw_t.at[k // 4] if k % 4 == 3 else s.raw.at[k - k // 4]))
    for k, piece in enumerate((s.p_gate, s.p_up, s.p_down)):
        loads.append(local(piece, s.wpack.at[:, pl.ds(8 * hw + k * FFL, FFL)]))
    for copy in loads:
        copy.start()

    barrier = pltpu.get_barrier_semaphore()
    peers = [device(r, (c + dc) % 2, (z + dz) % 4) for dz in range(4) for dc in range(2) if dz or dc] + [x_chip, y_chip, device(rd, c, z)]
    for peer in peers:
        pl.semaphore_signal(barrier, inc=1, device_id=peer, device_id_type=MESH_ID)
    for copy in loads:
        copy.wait()
    for k in range(8):
        piece = s.raw_t[k // 4].T if k % 4 == 3 else s.raw[k - k // 4]
        s.wpack[:, k * hw : (k + 1) * hw] = piece
    pl.semaphore_wait(barrier, len(peers))

    def swap_halves(src, dst):
        n = src.shape[0] // 2
        return [swap_of(src.at[pl.ds(k * n, n), :], dst.at[pl.ds(k * n, n), :]) for k in range(2)]

    def swap(src, dst):
        start, wait = swap_of(src, dst)
        start()
        return wait

    def swap_of(src, dst):
        far, near = remote(src, dst, home), local(src, dst)
        return chain(lambda: either(moved, far.start, near.start), lambda: either(moved, far.wait, near.wait))

    rows_a = D // 8
    chip = 2 * rows_a

    def spread(A, B):
        def at(ref, w):
            buf, slot, cols = ref
            return buf.at[w, cols] if slot is None else buf.at[slot, w, cols]

        def hop(ref, w, dev):
            return remote(at(ref, w), at(ref, w), dev)

        first = [hop(A, block(r, chip), x_chip), hop(B, block(r, chip), y_chip)]
        last = [hop(A, block(r // 2, 2 * chip), y_chip)] + [hop(B, block(q, chip), x_chip) for q in (r, ry)]

        def first_hop():
            go(first[0])
            go(first[1])

        def second_hop():
            first[0].wait_recv()
            go(last[0])
            first[1].wait_recv()
            go(last[1])
            go(last[2])

        def finish():
            for copy in last:
                copy.wait_recv()

        return first_hop, second_hop, finish

    def attn_weights(col, wide):
        C = pl.ds(col, wide)
        src = s.wpack.at[:, C]
        base = slots(4)
        dst = s.W2.at[zb, block(a, rows_a), C]
        out = [remote(src, dst, device(r, p, z_), None, base + 2 * zb + c) for z_ in (z2, z1)]
        near = local(src, dst)
        beside = remote(src, dst, sibling, None, base + 2 * zb + c)
        at = [s.W2.at[zb, block(2 * r + c_, rows_a), C] for c_ in range(2)]
        pass_on = [remote(at[c_], at[c_], across, None, base + 2 * zb + c_) for c_ in range(2)]
        here = [remote(src, at[0], sibling, 0, base + 2 * zb + c_) for c_ in range(2)]
        there = [remote(src, at[0], sibling, 0, base + 2 * (1 - zb) + c_) for c_ in range(2)]
        first_hop, second_hop, finish = spread((s.W2, 0, C), (s.W2, 1, C))

        def start():
            for copy in out:
                go(copy)
            either(stay, near.start, beside.start)

        def relay():
            def forward():
                beside.wait_send()
                for c_ in range(2):
                    here[c_].wait_recv()
                    pass_on[c_].start()

            def settle():
                near.wait()
                remote_side.wait_recv()

            either(moved, forward, settle)

        remote_side = remote(src, at[0], sibling, 0, base + 2 * zb + 1 - c)

        def first():
            for c_ in range(2):
                there[c_].wait_recv()
            pl.when(moved)(lambda: [copy.wait_send() for copy in pass_on] and None)
            first_hop()

        return chain(start, relay, first, second_hop, finish)

    def ff_weights(col, wide):
        src = s.wpack.at[:, pl.ds(col, wide)]
        dst = s.WF.at[block(a, rows_a), :]
        near, beside = local(src, dst), remote(src, dst, sibling)
        base = slots(2)
        out = remote(src, dst, device(r, p, z2), None, base + c)
        got = [remote(src, dst, sibling, 0, base + k) for k in range(2)]
        half = wide // 2
        first_hop, second_hop, finish = spread((s.WF, None, pl.ds(0, half)), (s.WF, None, pl.ds(half, half)))

        def start():
            go(out)
            either(stay, near.start, beside.start)

        def first():
            @pl.when(stay)
            def _():
                near.wait()
                beside.wait_recv()

            @pl.when(moved)
            def _():
                beside.wait_send()
                for copy in got:
                    copy.wait_recv()

            first_hop()

        return chain(start, first, second_hop, finish)

    def collect(A, B, bufs, send_home):
        ra1, rb1, ra2, rb2 = bufs

        def at(ref, w):
            buf, slot, cols = ref
            return buf.at[w, cols] if slot is None else buf.at[slot, w, cols]

        one = [
            go(remote(at(A, block(ry // 2, 2 * chip)), ra1, y_chip)),
            go(remote(at(B, block(rx, chip)), rb1.at[0], x_chip)),
            go(remote(at(B, block(rd, chip)), rb1.at[1], x_chip)),
        ]
        two = [remote(at(A, block(rx, chip)), ra2, x_chip), remote(at(B, block(ry, chip)), rb2, y_chip)]
        home_steps = send_home()

        def add(dst, src):
            n = 96
            for q in range(src.shape[0] // n):
                w = pl.ds(q * n, n)
                dst[w, :] = (dst[w, :].astype(F32) + src[w, :].astype(F32)).astype(BF16)

        def second():
            one[0].wait_recv()
            add(at(A, block(r // 2, 2 * chip)), ra1)
            go(two[0])
            one[2].wait_recv()
            add(at(B, block(ry, chip)), rb1.at[1])
            go(two[1])
            one[1].wait_recv()
            add(at(B, block(r, chip)), rb1.at[0])

        def third():
            two[0].wait_recv()
            add(at(A, block(r, chip)), ra2)
            two[1].wait_recv()
            add(at(B, block(r, chip)), rb2)
            home_steps[0]()

        return chain(second, third, *home_steps[1:])

    def to_home(grad, out):
        recv, near_recv, near_sem = slots(1), slots(1), slots(1)
        beside = remote(grad(2 * r + 1 - c), out(0), sibling, None, near_recv)
        near = local(grad(a), out(0), near_sem)
        far = [remote(grad(2 * r + k), out(1), device(r, k, z2), None, recv) for k in range(2)]

        def send():
            @pl.when(stay)
            def _():
                beside.start()
                near.start()

            @pl.when(moved)
            def _():
                for copy in far:
                    copy.start()

        def finish():
            @pl.when(stay)
            def _():
                beside.wait_send()
                near.wait()

            @pl.when(moved)
            def _():
                beside.wait_recv()
                for copy in far:
                    copy.wait_send()

            far[0].wait_recv()

        return send, finish

    def attn_home(col, wide, buf):
        C = pl.ds(col, wide)

        def build():
            pair = remote(s.dW2.at[1 - zb, block(r, chip), C], buf, across)
            send, finish = to_home(
                lambda i: s.dW2.at[zb, block(i, rows_a), C], lambda k: s.gz2.at[k, :, C]
            )

            def add_pair():
                pair.wait()
                for q in range(2):
                    w = pl.ds(q * rows_a, rows_a)
                    at = s.dW2.at[zb, block(2 * r + q, rows_a), C]
                    at[...] = (at[...].astype(F32) + buf[w, :].astype(F32)).astype(BF16)
                send()

            return pair.start, add_pair, finish

        return build

    def ff_home():
        return to_home(lambda i: s.dWF.at[block(i, rows_a), :], lambda k: s.gzf.at[k])

    def all_sum(buf, in1, in2):
        base1, base2 = slots(8), slots(4)
        me = 4 * c + z
        one, two = [], []
        for dz in range(4):
            for dc in range(2):
                if dz or dc:
                    c_, z_ = (c + dc) % 2, (z + dz) % 4
                    one.append((remote(in1.at[me], in1.at[me], device(r, c_, z_), None, base1 + me), base1 + 4 * c_ + z_))
        for dr in range(1, 4):
            r_ = (r + dr) % 4
            two.append((remote(in2.at[r], in2.at[r], device(r_, c, z), None, base2 + r), base2 + r_))

        def waits(copies, ref):
            for copy, recv in copies:
                copy.wait_send()
                remote(ref, ref, sibling, 0, recv).wait_recv()

        def start():
            in1[me] = buf[...]
            for copy, _ in one:
                copy.start()

        def middle():
            waits(one, in1.at[0])
            in2[r] = jnp.sum(in1[...], axis=0)
            for copy, _ in two:
                copy.start()

        def finish():
            waits(two, in2.at[0])
            buf[...] = jnp.sum(in2[...], axis=0)

        return chain(start, middle, finish)

    def gather(buf, n):
        half = n // 2
        copies = []
        for k in range(2):
            mine = buf.at[block(2 * own + k, half), :]
            there = buf.at[block(2 * beyond + k, half), :]
            copies.append((remote(mine, mine, across), remote(mine, mine, sibling), remote(there, there, sibling)))

        def start(k):
            copies[k][0].start()
            copies[k][1].start()

        def side():
            for copy in copies:
                copy[1].wait_recv()

        def forward():
            for copy in copies:
                copy[0].wait_recv()
                copy[2].start()

        def far():
            for copy in copies:
                copy[2].wait_recv()
                for one in copy:
                    one.wait_send()

        first, second, side, forward, far = chain(lambda: start(0), lambda: start(1), side, forward, far)
        return types.SimpleNamespace(start=lambda k: (first, second)[k](), side=side, forward=forward, far=far)

    def gather_all(buf, n):
        h = gather(buf, n)
        h.start(0)
        h.start(1)
        return h

    def each_block(h, body):
        h.side()
        lax.fori_loop(0, 2, lambda k, _: (body(order(k)), 0)[1], 0)
        h.forward()
        h.far()
        lax.fori_loop(2, 4, lambda k, _: (body(order(k)), 0)[1], 0)

    def gather_chip(buf):
        copies = []
        for k in range(2):
            mine = buf.at[block(2 * u_own + k, N // 2), :]
            copies.append(remote(mine, mine, sibling))

        def ready():
            for copy in copies:
                copy.wait_recv()

        first, second, ready = chain(lambda: go(copies[0]), lambda: go(copies[1]), ready)
        return (lambda k: (first, second)[k]()), ready

    def scatter(fn, bufs, res):
        s0, s1, zs, r0, r1, rz = bufs
        s0[...] = fn(order(3)).astype(BF16)
        d0 = remote(s0, r0, sibling)
        d0.start()
        res[...] = fn(order(2))
        d0.wait_recv()
        zs[...] = (res[...] + r0[...].astype(F32)).astype(BF16)
        n = res.shape[0] // 2
        parts = [pl.ds(k * n, n) for k in range(2)]
        dz = [remote(zs.at[w, :], rz.at[w, :], across) for w in parts]
        for copy in dz:
            copy.start()
        s1[...] = fn(order(1)).astype(BF16)
        d1 = remote(s1, r1, sibling)
        d1.start()
        res[...] = fn(order(0))

        def finish(k=None):
            for q in (0, 1) if k is None else (k,):
                if q == 0:
                    d1.wait_recv()
                w = parts[q]
                dz[q].wait_recv()
                res[w, :] += r1[w, :].astype(F32) + rz[w, :].astype(F32)
                if q == 1:
                    for copy in (d0, d1, *dz):
                        copy.wait_send()

        steps = chain(lambda: finish(0), lambda: finish(1))
        return lambda k=None: [step() for step in (steps if k is None else steps[k : k + 1])]

    def scatter_chip(fn, s0, r0, res):
        s0[...] = fn(1 - u_own).astype(BF16)
        d0 = remote(s0, r0, sibling)
        d0.start()
        res[...] = fn(u_own)

        def finish():
            d0.wait()
            res[...] += r0[...].astype(F32)

        return chain(finish)[0]

    CH = 64

    def chunks(n, body, init=0, half=None):
        lo, hi = (0, n // CH) if half is None else (half * n // (2 * CH), (half + 1) * n // (2 * CH))
        return lax.fori_loop(lo, hi, lambda i, v: body(pl.ds(pl.multiple_of(i * CH, CH), CH), v), init)

    gains = [s.gains[k : k + 1, :].astype(F32) for k in range(3)]

    def norm_rows(v, which, inv_ref, w, dst, dst_at):
        inv = lax.rsqrt(jnp.sum(v * v, axis=1, keepdims=True) / D + EPS)
        inv_ref[w, :] = jnp.broadcast_to(inv, (CH, 128))
        dst[dst_at, :] = (v * inv * gains[which]).astype(BF16)

    def rows_in(i, w):
        return pl.ds(pl.multiple_of(i * N + w.start, CH), CH)

    def norm_back_rows(d, v, which, inv):
        scaled = d * gains[which]
        dotted = jnp.sum(scaled * v, axis=1, keepdims=True)
        back = inv * scaled - v * (inv * inv * inv * dotted / D)
        return back, jnp.sum(d * v * inv, axis=0, keepdims=True)

    zero_gain = jnp.zeros((1, D), F32)
    o_ff = 8 * hw
    c_q, c_o, c_ckv, c_cq, c_co = 2 * hw, 3 * hw, 4 * hw, 6 * hw, 7 * hw

    w_kv = attn_weights(0, 2 * hw)
    w_qo = attn_weights(2 * hw, 2 * hw)
    swap_x = swap_halves(s.x, s.XN)
    w_kv[0]()
    w_qo[0]()
    for k in range(2):
        swap_x[k][0]()
    s.tab[z] = jnp.zeros_like(s.tab[z])
    s.tab[z, :Hl, :NB] = s.rel_bias[...].astype(F32)
    tab_base = slots(4)
    tab_out = [
        remote(s.tab.at[z], s.tab.at[z], device(r, c, (z + dz) % 4), None, tab_base + z) for dz in range(1, 4)
    ]
    for copy in tab_out:
        go(copy)
    s.len_out[...] = jnp.full(s.len_out.shape, s.seq_lengths[0], jnp.int32).astype(F32)
    lens = go(remote(s.len_out, s.len_in, sibling))
    lens.wait_recv()
    s.len_row[...] = jnp.where(stay, s.len_out[...], s.len_in[...])
    for dz in range(1, 4):
        other = s.tab.at[(z + dz) % 4]
        remote(other, other, sibling, 0, tab_base + (z + dz) % 4).wait_recv()
    span = 2 * TILE
    ids = lax.broadcasted_iota(jnp.int32, (NB, span), 0)
    buckets = s.rel_buckets[...]
    last = jnp.broadcast_to(buckets[:, -1:], (1, span))
    near = buckets[:, :span]
    after = jnp.concatenate([buckets[:, TILE:span], buckets[:, :TILE]], axis=1)

    def onehot(row):
        return (ids == row).astype(F32)

    key_at = lax.broadcasted_iota(jnp.int32, (TILE, TILE), 0)
    query_at = lax.broadcasted_iota(jnp.int32, (TILE, TILE), 1)
    w_kv[1]()
    for q in range(2):
        table = s.tab[2 * c + q, :, :NB]
        for k, row in enumerate((near, after, last)):
            s.vecs[8 * k : 8 * k + 8, :] = mm(table, onehot(row))

        def build(h, _):
            for k in range(3):
                wide = jnp.broadcast_to(s.vecs[pl.ds(8 * k + h, 1), :], (TILE, span))
                tile = pltpu.roll(wide, 0, 1, stride=1, stride_axis=0)[:, :TILE]
                s.tiles[Hl * q + h, k] = (jnp.where(query_at >= key_at, tile, NEG) if k == 0 else tile).astype(BF16)
            return 0

        lax.fori_loop(0, Hl, build, 0)
    w_qo[1]()
    length = s.len_row[0:1, :]
    lane = lax.broadcasted_iota(jnp.int32, (TILE, 128), 1)

    def extra_lane(i, _):
        w = tile_rows(i)
        at = lax.broadcasted_iota(jnp.int32, (TILE, 128), 0) + i * TILE
        mask = jnp.where((lane == hd) & (at.astype(F32) >= length), NEG, 0.0).astype(BF16)
        for h in range(H2):
            s.k3[h, w, :] = mask

        @pl.when(i < 2)
        def _():
            for h in range(H2):
                s.q3[h, w, :] = jnp.where(lane == hd, 1.0, 0.0).astype(BF16)

        return 0

    lax.fori_loop(0, 4, extra_lane, 0)
    ga = gather(s.FIRST, N)
    w_kv[2]()

    def norm_one(w, _):
        norm_rows(s.XN[w, :].astype(F32), 0, s.inv1, w, s.FIRST, rows_in(own, w))
        return 0

    for k in range(2):
        swap_x[k][1]()
        chunks(N, norm_one, 0, k)
        ga.start(k)
        if k == 0:
            w_qo[2]()
    w_kv[3]()
    w_ca = attn_weights(4 * hw, 2 * hw)
    w_cb = attn_weights(6 * hw, 2 * hw)
    w_f = ff_weights(o_ff, 3 * FFL)
    w_ca[0]()
    w_cb[0]()
    w_qo[3]()
    w_ca[1]()
    wait_e = swap(s.enc, s.EN)
    w_cb[1]()
    ga.side()
    ga.forward()
    w_f[0]()
    w_ca[2]()
    ga.far()
    wait_o = swap(s.og, s.ON)
    wait_e()
    s.ENC[block(own, NE), :] = s.EN[...]
    ge = gather_all(s.ENC, NE)
    w_kv[4]()
    w_qo[4]()

    def split(dst, h0, value, rows):
        for h in range(Hl):
            dst[h0 + h, rows, :hd] = value[:, h * hd : (h + 1) * hd]

    def project_one(k, _):
        i = order(k)
        w = block(i, N)
        f = s.FIRST[w, :]
        for q in range(2):
            y = mm(f, s.W2[q, :, : 2 * hw]).astype(BF16)
            split(s.k3, Hl * q, y[:, :hw], w)
            split(s.v3, Hl * q, y[:, hw:], w)

        @pl.when(k < 2)
        def _():
            for q in range(2):
                split(s.q3, Hl * q, mm(f, s.W2[q, :, c_q : c_q + hw]).astype(BF16), block(i // 2, N))

        return 0

    lax.fori_loop(0, 4, project_one, 0)
    w_cb[2]()
    w_ca[3]()

    def turn(dst, src):
        def one(h, _):
            dst[h] = src[h, :, :hd].T
            return 0

        lax.fori_loop(0, H2, one, 0)

    turn(s.t3, s.v3)
    s.WO[...] = s.W2[:, :, c_o : c_o + hw]

    def after_first(u, J):
        @pl.when(jnp.logical_and(u == 1, J == 0))
        def _():
            ge.side()
            ge.forward()
            w_cb[3]()
            w_f[1]()

    fwd_attention(s.q3, s.k3, s.t3, s.out_t, s.lse, H2, query_block, lambda I: I + 1, s.tiles, after_first)
    s.MIX[...] = s.out_t[...].T.astype(BF16)

    def out_proj(mix, weight):
        def fn(u):
            w = block(u, N)
            return mm(mix[w, :hw], weight[0], NT) + mm(mix[w, hw:], weight[1], NT)

        return fn

    end = scatter_chip(out_proj(s.MIX, s.WO), s.s0, s.i0, s.res)
    end()

    def norm_two(w, _):
        v = s.XN[w, :].astype(F32) + s.res[w, :]
        s.MID[w, :] = v
        norm_rows(v, 1, s.inv2, w, s.SECOND, rows_in(u_own, w))
        return 0

    second_go, second_ready = gather_chip(s.SECOND)
    for k in range(2):
        chunks(N, norm_two, 0, k)
        second_go(k)
    wait_o()
    own_pos = lax.broadcasted_iota(jnp.int32, (N, 128), 0) + own * N
    s.ok[...] = (own_pos.astype(F32) < length).astype(F32)

    def mask_rows(w, _):
        s.GF[rows_in(own, w), :] = (s.ON[w, :].astype(F32) * s.ok[w, :1]).astype(BF16)
        return 0

    chunks(N, mask_rows)
    gg = gather_all(s.GF, N)
    ge.far()
    w_ca[4]()

    def project_enc(i, _):
        w = block(i, N)
        e = s.ENC[w, :]
        for q in range(2):
            y = mm(e, s.W2[q, :, c_ckv : c_ckv + 2 * hw]).astype(BF16)
            split(s.ck3, Hl * q, y[:, :hw], w)
            split(s.cv3, Hl * q, y[:, hw:], w)
        return 0

    lax.fori_loop(0, NK // N, project_enc, 0)
    turn(s.ct3, s.cv3)
    w_cb[4]()
    s.WCO[...] = s.W2[:, :, c_co : c_co + hw]
    second_ready()

    def project_two(u, _):
        w = block(u, N)
        t = s.SECOND[w, :]
        for q in range(2):
            split(s.cq3, Hl * q, mm(t, s.W2[q, :, c_cq : c_cq + hw]).astype(BF16), w)
        return 0

    lax.fori_loop(0, 2, project_two, 0)
    def after_cross(u, J):
        @pl.when(jnp.logical_and(u == 0, J == 0))
        def _():
            w_f[2]()

    fwd_attention(
        s.cq3, s.ck3, s.ct3, s.out_t2, s.lse2, H2, query_block, lambda I: NK // TILE, None, after_cross
    )
    s.MIX2[...] = s.out_t2[...].T.astype(BF16)
    scatter_chip(out_proj(s.MIX2, s.WCO), s.s0, s.i1, s.res)()

    def norm_three(w, _):
        v = s.MID[w, :] + s.res[w, :]
        s.LAT[w, :] = v
        norm_rows(v, 2, s.inv3, w, s.THIRD, rows_in(own, w))
        return 0

    gt = gather(s.THIRD, N)
    for k in range(2):
        chunks(N, norm_three, 0, k)
        gt.start(k)
    gg.side()
    gg.forward()
    gg.far()
    w_f[3]()
    root = 0.7978845608028654
    SUB = 128

    def feed(i):
        def sub(u, _):
            w = pl.ds(pl.multiple_of(i * N + u * SUB, SUB), SUB)
            t = s.THIRD[w, :]
            gate = mm(t, s.WF[:, :FFL])
            up = mm(t, s.WF[:, FFL : 2 * FFL])
            dh = mm(s.GF[w, :], s.WF[:, 2 * FFL :])
            sq = gate * gate
            th = jnp.tanh(root * gate * (1.0 + 0.044715 * sq))
            half = 0.5 * (1.0 + th)
            act = gate * half
            slope = half + 0.5 * gate * (1.0 - th * th) * root * (1.0 + 3 * 0.044715 * sq)
            s.HID[w, :] = (act * up).astype(BF16)
            s.DGU[w, :FFL] = (dh * up * slope).astype(BF16)
            s.DGU[w, FFL:] = (dh * act).astype(BF16)
            return 0

        lax.fori_loop(0, N // SUB, sub, 0)

    each_block(gt, feed)
    end = scatter(
        lambda i: mm(s.DGU[block(i, N), :], s.WF[:, : 2 * FFL], NT), (s.s0, s.s1, s.zs, s.a0, s.a1, s.az), s.res
    )

    def weight_grad(put, parts):
        def step(q, _):
            m = pl.ds(pl.multiple_of(q * 256, 256), 256)
            total = None
            for left, right in parts:
                y = mm(left(m), right, TN)
                total = y if total is None else total + y
            put(m, total.astype(BF16))
            return 0

        lax.fori_loop(0, D // 256, step, 0)

    def put_f(col, n):
        def put(m, v):
            s.dWF[m, col : col + n] = v

        return put

    def put_slots(col, n):
        def put(m, v):
            for q in range(2):
                s.dW2[q, m, col : col + n] = v[:, q * n : (q + 1) * n]

        return put

    weight_grad(put_f(2 * FFL, FFL), [(lambda m: s.GF[:, m], s.HID[...])])
    weight_grad(put_f(0, 2 * FFL), [(lambda m: s.THIRD[:, m], s.DGU[...])])
    half_f = 3 * FFL // 2
    grad_f = collect(
        (s.dWF, None, pl.ds(0, half_f)), (s.dWF, None, pl.ds(half_f, half_f)), (s.ra1, s.rb1, s.ra2, s.rb2), ff_home
    )
    turn(s.ct3, s.ck3)
    turn(s.t3, s.k3)
    s.dtile[...] = jnp.zeros_like(s.dtile)

    def back_three(w, acc):
        back, part_gain = norm_back_rows(s.res[w, :], s.LAT[w, :], 2, s.inv3[w, :1])
        d = s.GF[rows_in(own, w), :].astype(F32) + back
        s.GR[w, :] = d
        s.DL[rows_in(u_own, w), :] = d.astype(BF16)
        return acc + part_gain

    dl_go, dl_ready = gather_chip(s.DL)
    gain_three = zero_gain
    for k in range(2):
        end(k)
        gain_three = chunks(N, back_three, gain_three, k)
        dl_go(k)
    end_out = scatter(
        lambda i: mm(s.HID[block(i, N), :], s.WF[:, 2 * FFL :], NT), (s.s0, s.s1, s.zs, s.b0, s.b1, s.bz), s.res
    )


    def back_heads(src, weight, out_t):
        def body(u, _):
            w = block(u, N)
            for q in range(2):
                y = mm(src[w, :], weight[q]).astype(BF16)
                split(s.do3, Hl * q, y, w)
                yt = y.astype(F32).T
                for h in range(Hl):
                    g_h = Hl * q + h
                    both = yt[h * hd : (h + 1) * hd, :] * out_t[g_h * hd : (g_h + 1) * hd, w]
                    s.delta[g_h : g_h + 1, w] = jnp.sum(both, axis=0, keepdims=True)
            return 0

        lax.fori_loop(0, 2, body, 0)

    dl_ready()
    back_heads(s.DL, s.WCO, s.out_t2)

    def put_cross(J):
        w = tile_rows(J)
        for h in range(H2):
            q, hh = h // Hl, h % Hl
            at = 2 * hw * q + hh * hd
            s.DGU[w, at : at + hd] = s.dk[h, :, :hd].astype(BF16)
            s.DGU[w, at + hw : at + hw + hd] = s.dv[h].astype(BF16)

    def cross_between(J):
        @pl.when(J == 0)
        def _():
            grad_f[0]()

    bwd_attention(
        s.cq3, s.ck3, s.cv3, s.ct3, s.do3, s.lse2, s.delta, s.out_t2, s.dk, s.dv, put_cross, H2, query_block,
        lambda J: 0, NK // TILE, None, None, cross_between,
    )
    s.DQ[...] = s.out_t2[...].T.astype(BF16)

    def query_grad(col):
        def fn(u):
            w = block(u, N)
            return mm(s.DQ[w, :hw], s.W2[0, :, col : col + hw], NT) + mm(s.DQ[w, hw:], s.W2[1, :, col : col + hw], NT)

        return fn

    def put_out(w, _):
        s.ON[w, :] = (s.LAT[w, :] + s.res[w, :]).astype(BF16)
        return 0

    end_out()
    chunks(N, put_out)
    wait_lo = swap(s.ON, s.lo)
    end = scatter_chip(query_grad(c_cq), s.s0, s.i2, s.res)

    def kv_grad(n, col):
        def fn(i):
            w = block(i, n)
            return (
                mm(s.DGU[w, : 2 * hw], s.W2[0, :, col : col + 2 * hw], NT)
                + mm(s.DGU[w, 2 * hw : 4 * hw], s.W2[1, :, col : col + 2 * hw], NT)
            )

        return fn

    weight_grad(put_slots(c_cq, hw), [(lambda m: s.SECOND[:, m], s.DQ[...])])
    weight_grad(put_slots(c_co, hw), [(lambda m: s.DL[:, m], s.MIX2[...])])
    weight_grad(put_slots(c_ckv, 2 * hw), [(lambda m: s.ENC[:, m], s.DGU[:NK, : 4 * hw])])
    grad_f[1]()
    C4 = pl.ds(4 * hw, 4 * hw)
    grad_c = collect((s.dW2, 0, C4), (s.dW2, 1, C4), (s.qa1, s.qb1, s.qa2, s.qb2), attn_home(4 * hw, 4 * hw, s.pair1))
    end()

    def back_two(w, acc):
        back, part_gain = norm_back_rows(s.res[w, :], s.MID[w, :], 1, s.inv2[w, :1])
        d = s.GR[w, :] + back
        s.GR[w, :] = d
        s.DM[rows_in(u_own, w), :] = d.astype(BF16)
        return acc + part_gain

    dm_go, dm_ready = gather_chip(s.DM)
    gain_two = zero_gain
    for k in range(2):
        gain_two = chunks(N, back_two, gain_two, k)
        dm_go(k)
    end_enc = scatter(kv_grad(NE, c_ckv), (s.e0, s.e1, s.es, s.f0, s.f1, s.fz), s.rese)
    end_enc()
    s.EN[...] = s.rese[...].astype(BF16)
    wait_eo = swap(s.EN, s.eg)

    dm_ready()
    back_heads(s.DM, s.WO, s.out_t)
    weight_grad(put_slots(c_o, hw), [(lambda m: s.DM[:, m], s.MIX[...])])

    def self_between(J):
        @pl.when(J == 0)
        def _():
            grad_c[0]()

    bwd_attention(
        s.q3, s.k3, s.v3, s.t3, s.do3, s.lse, s.delta, s.out_t, s.dk, s.dv, put_cross, H2, query_block,
        lambda J: jnp.where(J <= lo_block, 0, 1), hi_block + 1, s.tiles, s.dtile, self_between,
    )

    def clear(J, _):
        s.DGU[tile_rows(J), :] = jnp.zeros((TILE, s.DGU.shape[1]), BF16)
        return 0

    lax.fori_loop(hi_block + 1, 4, clear, 0)
    s.DQ[...] = s.out_t[...].T.astype(BF16)
    own_part = query_grad(c_q)
    other_part = kv_grad(N, 0)

    def scatter_first(bufs, res, filler):
        s0, s1, zs, r0, r1, rz = bufs
        s0[...] = other_part(order(3)).astype(BF16)
        d0 = remote(s0, r0, sibling)
        d0.start()
        res[...] = other_part(order(2))
        d0.wait_recv()
        zs[...] = (res[...] + r0[...].astype(F32)).astype(BF16)
        n = res.shape[0] // 2
        parts = [pl.ds(k * n, n) for k in range(2)]
        dz = [remote(zs.at[w, :], rz.at[w, :], across) for w in parts]
        for copy in dz:
            copy.start()
        filler()
        s1[...] = (other_part(3 - own) + own_part(1 - u_own)).astype(BF16)
        d1 = remote(s1, r1, sibling)
        d1.start()
        res[...] = other_part(own) + own_part(u_own)

        def finish(k=None):
            for q in (0, 1) if k is None else (k,):
                if q == 0:
                    d1.wait_recv()
                w = parts[q]
                dz[q].wait_recv()
                res[w, :] += r1[w, :].astype(F32) + rz[w, :].astype(F32)
                if q == 1:
                    for copy in (d0, d1, *dz):
                        copy.wait_send()

        steps = chain(lambda: finish(0), lambda: finish(1))
        return lambda k=None: [step() for step in (steps if k is None else steps[k : k + 1])]

    KV, QO = pl.ds(0, 2 * hw), pl.ds(2 * hw, 2 * hw)
    bufs = (s.ra1, s.rb1, s.ra2, s.rb2)
    cut = lambda k: tuple(x.at[..., pl.ds(k * 2 * hw, 2 * hw)] for x in bufs)
    grad_c[1]()
    weight_grad(put_slots(0, 2 * hw), [(lambda m: s.FIRST[:, m], s.DGU[:, : 4 * hw])])
    grad_kv = collect((s.dW2, 0, KV), (s.dW2, 1, KV), cut(0), attn_home(0, 2 * hw, s.pair2))
    query_part = []

    def query_grads():
        weight_grad(
            put_slots(c_q, hw),
            [
                (lambda m: s.FIRST[tile_rows(lo_block), m], s.DQ[:N, :]),
                (lambda m: s.FIRST[tile_rows(hi_block), m], s.DQ[N:, :]),
            ],
        )
        query_part.append(collect((s.dW2, 0, QO), (s.dW2, 1, QO), cut(1), attn_home(2 * hw, 2 * hw, s.pair3)))

    end = scatter_first((s.s0, s.s1, s.zs, s.a0, s.a1, s.az), s.res, query_grads)
    grad_qo = query_part[0]
    grad_c[2]()
    grad_kv[0]()
    s.small[...] = jnp.zeros_like(s.small)
    flip = (key_at + query_at == TILE - 1).astype(BF16)
    blank = jnp.zeros((TILE, TILE), F32)
    head_row = lax.broadcasted_iota(jnp.int32, (16, span), 0)
    gap = lax.broadcasted_iota(jnp.int32, (1, span), 1)
    near_back = jnp.where(gap >= TILE - 1, pltpu.roll(near, TILE - 1, 1), -1)
    next_back = jnp.where(gap < span - 1, pltpu.roll(near, span - 1, 1), -1)
    for k, row in enumerate((near_back, next_back)):

        def line_up(h, diag):
            full = s.dtile[h, k]
            high = full.astype(BF16)
            rest = full - high.astype(F32)
            mid = rest.astype(BF16)
            turned = mm(flip, high) + mm(flip, mid) + mm(flip, (rest - mid.astype(F32)).astype(BF16))
            lined = pltpu.roll(jnp.concatenate([turned, blank], axis=1), 0, 1, stride=1, stride_axis=0)
            return jnp.where(head_row == H2 * c + h, jnp.sum(lined, axis=0, keepdims=True), diag)

        diag = lax.fori_loop(0, H2, line_up, jnp.zeros((16, span), F32))
        s.small[:16, :NB] += lax.dot_general(
            diag, onehot(row), NT, precision=lax.Precision.HIGHEST, preferred_element_type=F32
        )
    far_row = lax.broadcasted_iota(jnp.int32, (16, 1), 0)

    def far_total(h, acc):
        total = jnp.sum(jnp.sum(s.dtile[h, 2], axis=0, keepdims=True), axis=1, keepdims=True)
        return jnp.where(far_row == H2 * c + h, total, acc)

    far_sum = lax.fori_loop(0, H2, far_total, jnp.zeros((16, 1), F32))
    is_last = (lax.broadcasted_iota(jnp.int32, (1, NB), 1) == buckets[:, -1:]).astype(F32)
    s.small[:16, :NB] += far_sum * is_last

    def put_rows(buf, at, row):
        for k in range(D // 128):
            buf[at + k : at + k + 1, :] = row[:, 128 * k : 128 * (k + 1)]

    put_rows(s.small, 16, gain_two)
    put_rows(s.small, 24, gain_three)
    sum_small = all_sum(s.small, s.small1, s.small2)
    sum_small[0]()
    def back_one(w, acc):
        back, part_gain = norm_back_rows(s.res[w, :], s.XN[w, :].astype(F32), 0, s.inv1[w, :1])
        s.i0[w, :] = (s.GR[w, :] + back).astype(BF16)
        return acc + part_gain

    swap_dg = swap_halves(s.i0, s.dg)
    wait_dg = [pair[1] for pair in swap_dg]
    gain_one = zero_gain
    for k in range(2):
        end(k)
        gain_one = chunks(N, back_one, gain_one, k)
        swap_dg[k][0]()
    grad_qo[0]()
    s.late[...] = jnp.zeros_like(s.late)
    put_rows(s.late, 0, gain_one)
    sum_late = all_sum(s.late, s.late1, s.late2)
    sum_late[0]()
    grad_kv[1]()
    sum_small[1]()
    grad_qo[1]()
    sum_late[1]()
    grad_kv[2]()
    sum_small[2]()
    grad_qo[2]()
    sum_late[2]()
    s.sm[...] = jnp.zeros_like(s.sm)
    for k in range(D // 128):
        w = slice(128 * k, 128 * (k + 1))
        s.sm[0:1, w] = s.late[k : k + 1, :]
        s.sm[1:2, w] = s.small[16 + k : 17 + k, :]
        s.sm[2:3, w] = s.small[24 + k : 25 + k, :]
    s.sm[:, D:] = s.small[:16, :]
    wait_lo()
    wait_eo()
    grad_f[2]()
    grad_c[3]()
    grad_kv[3]()
    for wait in wait_dg:
        wait()
    grad_qo[3]()
    for copy in unsent:
        copy.wait_send()
    assert counter[0] <= part, counter[0]


def layer_call(pieces, x, enc, og, gains, rel_bias, seq_lengths, rel_buckets, dims):
    D, Hl, hd, FFL, N, NE, g, part = dims
    hw = Hl * hd
    H2, NC, NQ, NK = 2 * Hl, 2 * N, 4 * N, 4 * NE
    ra = D // 8
    vm, any_ = pl.BlockSpec(memory_space=pltpu.VMEM), pl.BlockSpec(memory_space=pl.ANY)
    sm_ = pl.BlockSpec(memory_space=pltpu.SMEM)
    piece_names = ("p_sk", "p_sv", "p_sq", "p_so", "p_ck", "p_cv", "p_cq", "p_co", "p_gate", "p_up", "p_down")
    ins = dict({k: any_ for k in piece_names}, x=any_, enc=any_, og=any_, gains=vm, rel_bias=vm, seq_lengths=sm_, rel_buckets=vm)
    outs = dict(
        lo=((N, D), BF16, any_), dg=((N, D), BF16, any_), eg=((NE, D), BF16, any_),
        gz2=((2, ra, 8 * hw), BF16, any_), gzf=((2, ra, 3 * FFL), BF16, any_), sm=((16, D + 128), F32, vm),
    )
    sc = {}

    def add(dtype, **shapes):
        for name, shape in shapes.items():
            sc[name] = pltpu.VMEM(shape, dtype)

    add(BF16, wpack=(ra, 8 * hw + 3 * FFL), raw=(6, ra, hw), raw_t=(2, hw, ra))
    add(BF16, pair1=(D // 4, 4 * hw), pair2=(D // 4, 2 * hw), pair3=(D // 4, 2 * hw))
    add(BF16, W2=(2, D, 8 * hw), dW2=(2, D, 8 * hw), WF=(D, 3 * FFL), dWF=(D, 3 * FFL), WO=(2, D, hw), WCO=(2, D, hw))
    for k in "rq":
        add(BF16, **{k + "a1": (D // 2, 4 * hw), k + "b1": (2, D // 4, 4 * hw), k + "a2": (D // 4, 4 * hw), k + "b2": (D // 4, 4 * hw)})
    add(BF16, FIRST=(NQ, D), THIRD=(NQ, D), GF=(NQ, D), SECOND=(NC, D), DL=(NC, D), DM=(NC, D), ENC=(NK, D))
    add(BF16, **{k: (N, D) for k in ("s0", "s1", "zs", "a0", "a1", "az", "b0", "b1", "bz", "i0", "i1", "i2", "XN", "ON")})
    add(BF16, **{k: (NE, D) for k in ("e0", "e1", "es", "f0", "f1", "fz", "EN")})
    add(F32, **{k: (N, D) for k in ("MID", "LAT", "GR", "res")}, rese=(NE, D))
    add(F32, inv1=(N, 128), inv2=(N, 128), inv3=(N, 128), ok=(N, 128))
    add(BF16, q3=(H2, NC, 128), k3=(H2, NQ, 128), v3=(H2, NQ, hd), cq3=(H2, NC, hd), ck3=(H2, NK, hd), cv3=(H2, NK, hd))
    add(BF16, do3=(H2, NC, hd), t3=(H2, hd, NQ), ct3=(H2, hd, NK))
    add(F32, out_t=(2 * hw, NC), out_t2=(2 * hw, NC), lse=(8, NC), lse2=(8, NC), delta=(8, NC))
    add(F32, dk=(H2, TILE, 128), dv=(H2, TILE, hd))
    add(BF16, MIX=(NC, 2 * hw), MIX2=(NC, 2 * hw), HID=(NQ, FFL), DGU=(NQ, 2 * FFL), DQ=(NC, 2 * hw))
    add(BF16, tiles=(H2, 3, TILE, TILE))
    add(F32, dtile=(H2, 3, TILE, TILE), vecs=(24, 2 * TILE))
    add(F32, tab=(4, 8, 128), len_out=(8, 128), len_in=(8, 128), len_row=(8, 128))
    add(F32, small=(32, 128), small1=(8, 32, 128), small2=(4, 32, 128))
    add(F32, late=(8, 128), late1=(8, 8, 128), late2=(4, 8, 128))
    names = list(ins) + list(outs) + list(sc) + ["sems"]
    return pl.pallas_call(
        functools.partial(layer_kernel, dims, names),
        out_shape=[jax.ShapeDtypeStruct(o[0], o[1]) for o in outs.values()],
        in_specs=list(ins.values()),
        out_specs=[o[2] for o in outs.values()],
        scratch_shapes=list(sc.values()) + [pltpu.SemaphoreType.DMA((part,))],
        compiler_params=pltpu.CompilerParams(collective_id=0, has_side_effects=True, vmem_limit_bytes=67043328),
        name="layer",
    )(*pieces, x, enc, og, gains, rel_bias, seq_lengths, rel_buckets)


def finish_kernel(dims, lo, dg, eg, gz2, gzf, sm, *outs):
    D, Hl, hd, FFL, N, NE, g, part = dims
    hw = Hl * hd
    o_lo, o_dg, o_eg, o_gains, o_bias, sq, sk, sv, so, cq, ck, cv, co, gg, gu, gd = outs
    o_lo[...] = lo[...]
    o_dg[...] = dg[...].astype(F32)
    o_eg[...] = eg[...].astype(F32)
    o_gains[...] = sm[:3, :D]
    o_bias[...] = sm[: 4 * Hl, D : D + NB]

    def total(col, n):
        w = pl.ds(col, n)
        return gz2[0, :, w].astype(F32) + gz2[1, :, w].astype(F32)

    for base, parts in ((0, (sk, sv, sq, so)), (4 * hw, (ck, cv, cq, co))):
        y = total(base, 4 * hw)
        for k, out in enumerate(parts):
            v = y[:, k * hw : (k + 1) * hw]
            out[...] = v if k < 3 else v.T
    f = gzf[0].astype(F32) + gzf[1].astype(F32)
    gg[...] = f[:, :FFL]
    gu[...] = f[:, FFL : 2 * FFL]
    gd[...] = f[:, 2 * FFL :]


def finish_call(dims, lo, dg, eg, gz2, gzf, sm):
    D, Hl, hd, FFL, N, NE, g, part = dims
    hw, ra = Hl * hd, D // 8
    vm = pl.BlockSpec(memory_space=pltpu.VMEM)
    shapes = [((N, D), BF16), ((N, D), F32), ((NE, D), F32), ((3, D), F32), ((4 * Hl, NB), F32)]
    shapes += [((ra, hw), F32)] * 3 + [((hw, ra), F32)] + [((ra, hw), F32)] * 3 + [((hw, ra), F32)]
    shapes += [((ra, FFL), F32)] * 3
    return pl.pallas_call(
        functools.partial(finish_kernel, dims),
        out_shape=[jax.ShapeDtypeStruct(*v) for v in shapes],
        in_specs=[vm] * 6,
        out_specs=[vm] * len(shapes),
        name="finish",
    )(lo, dg, eg, gz2, gzf, sm)


def exchange(value, step, size):
    return lax.ppermute(value, "dp", [(i, i ^ step) for i in range(size)])


def per_device(
    decoder_in, encoder_out, seq_lengths, rel_buckets, norm_gains, rel_bias,
    self_query, self_key, self_value, self_out, cross_query, cross_key, cross_value, cross_out,
    gate_weight, up_weight, down_weight, out_grad,
):
    width = decoder_in.shape[1]
    heads, w, f = rel_bias.shape[1], self_query.shape[1], gate_weight.shape[1]
    size = lax.axis_size("dp")
    g = size // 8
    rows, erows = decoder_in.shape[0], encoder_out.shape[0]
    pieces = (
        self_key, self_value, self_query, self_out, cross_key, cross_value, cross_query, cross_out,
        gate_weight, up_weight, down_weight.T,
    )
    if g > 1:
        wpack = jnp.concatenate([x.T if k in (3, 7) else x for k, x in enumerate(pieces)], axis=1)
        step = 1
        while step < g:
            other = exchange(wpack, step, size)
            upper = (lax.axis_index("dp") // step) % 2
            wpack = jnp.where(upper == 1, jnp.concatenate([other, wpack], 0), jnp.concatenate([wpack, other], 0))
            step *= 2
        cols = [wpack[:, k * w : (k + 1) * w] for k in range(8)]
        cols[3], cols[7] = cols[3].T, cols[7].T
        pieces = (*cols, *(wpack[:, 8 * w + k * f : 8 * w + (k + 1) * f] for k in range(3)))
    dims = (width, heads, w // heads, f, rows, erows, g, 480)
    lo, dg, eg, gz2, gzf, sm = layer_call(
        pieces, decoder_in, encoder_out, out_grad, norm_gains, rel_bias.T, seq_lengths, rel_buckets.reshape(1, -1), dims
    )
    if g == 1:
        outs = list(finish_call(dims, lo, dg, eg, gz2, gzf, sm))
        outs[4], outs[15] = outs[4].T, outs[15].T
        return tuple(outs)
    gw = jnp.concatenate([jnp.sum(gz2.astype(F32), axis=0), jnp.sum(gzf.astype(F32), axis=0)], axis=1)
    step = g // 2
    while step >= 1:
        upper = (lax.axis_index("dp") // step) % 2
        n = gw.shape[0] // 2
        keep = jnp.where(upper == 1, gw[n:], gw[:n])
        give = jnp.where(upper == 1, gw[:n], gw[n:])
        gw = keep + exchange(give, step, size)
        sm = sm + exchange(sm, step, size)
        step //= 2
    col = lambda k: gw[:, k * w : (k + 1) * w]
    return (
        lo, dg.astype(F32), eg.astype(F32), sm[:3, :width], sm[: 4 * heads, width : width + NB].T,
        col(2), col(0), col(1), col(3).T, col(6), col(4), col(5), col(7).T,
        gw[:, 8 * w : 8 * w + f], gw[:, 8 * w + f : 8 * w + 2 * f], gw[:, 8 * w + 2 * f :].T,
    )


def solution(mesh):
    return jax.shard_map(
        per_device,
        mesh=mesh,
        in_specs=(
            P(("dp", "mp"), None),
            P(("dp", "mp"), None),
            P("dp"),
            P(),
            P(),
            P(None, "mp"),
            P("dp", "mp"),
            P("dp", "mp"),
            P("dp", "mp"),
            P("mp", "dp"),
            P("dp", "mp"),
            P("dp", "mp"),
            P("dp", "mp"),
            P("mp", "dp"),
            P("dp", "mp"),
            P("dp", "mp"),
            P("mp", "dp"),
            P(("dp", "mp"), None),
        ),
        out_specs=(
            P(("dp", "mp"), None),
            P(("dp", "mp"), None),
            P(("dp", "mp"), None),
            P(),
            P(),
            P("dp", "mp"),
            P("dp", "mp"),
            P("dp", "mp"),
            P("mp", "dp"),
            P("dp", "mp"),
            P("dp", "mp"),
            P("dp", "mp"),
            P("mp", "dp"),
            P("dp", "mp"),
            P("dp", "mp"),
            P("mp", "dp"),
        ),
        check_vma=False,
    )
```

```python
import functools
import types

import jax
import jax.numpy as jnp
from jax import lax
from jax.experimental import pallas as pl
from jax.experimental.pallas import tpu as pltpu
from jax.sharding import PartitionSpec as P

NB = 32
EPS = 1e-06
F32 = jnp.float32
BF16 = jnp.bfloat16
NEG = -1e30
TILE = 256
NN = (((1,), (0,)), ((), ()))
NT = (((1,), (1,)), ((), ()))
TN = (((0,), (0,)), ((), ()))
MESH_ID = pl.DeviceIdType.MESH


def mm(a, b, dims=NN):
    return lax.dot_general(a, b, dims, preferred_element_type=F32)


def tile_rows(i):
    return pl.ds(pl.multiple_of(i * TILE, TILE), TILE)


def fwd_attention(q3, k3, vt3, out_t, lse, heads, query_block, key_blocks, tiles, between):
    hd = vt3.shape[1]

    def qblock(u, _):
        ri = tile_rows(u)
        I = query_block(u)

        def kblock(J, carry):
            rj = tile_rows(J)
            new = []
            for h in range(heads):
                m, l, acc = carry[h]
                s = mm(k3[h, rj, :], q3[h, ri, :], NT)
                if tiles is not None:
                    s = s + tiles[h, jnp.minimum(I - J, 2)].astype(F32)
                m2 = jnp.maximum(m, jnp.max(s, axis=0, keepdims=True))
                a = jnp.exp(m - m2)
                p = jnp.exp(s - m2)
                l2 = l * a + jnp.sum(p, axis=0, keepdims=True)
                new.append((m2, l2, acc * a + mm(vt3[h, :, rj], p.astype(BF16))))
            between(u, J)
            return tuple(new)

        init = tuple(
            (jnp.full((1, TILE), NEG, F32), jnp.zeros((1, TILE), F32), jnp.zeros((hd, TILE), F32)) for _ in range(heads)
        )
        res = lax.fori_loop(0, key_blocks(I), kblock, init)
        for h in range(heads):
            m, l, acc = res[h]
            out_t[h * hd : (h + 1) * hd, ri] = acc / l
            lse[h : h + 1, ri] = m + jnp.log(l)
        return 0

    lax.fori_loop(0, 2, qblock, 0)


def bwd_attention(
    q3, k3, v3, kt3, do3, lse, delta, dqt, dk, dv, put, heads, query_block, first_query, key_end, tiles, dtile, between
):
    hd = kt3.shape[1]
    dqt[...] = jnp.zeros_like(dqt)

    def kblock(J, _):
        rj = tile_rows(J)
        dk[...] = jnp.zeros_like(dk)
        dv[...] = jnp.zeros_like(dv)

        def qblock(u, _):
            ri = tile_rows(u)
            apart = query_block(u) - J
            for h in range(heads):
                s = mm(k3[h, rj, :], q3[h, ri, :], NT)
                if tiles is not None:
                    s = s + tiles[h, jnp.minimum(apart, 2)].astype(F32)
                p = jnp.exp(s - lse[h : h + 1, ri])
                dp = mm(v3[h, rj, :], do3[h, ri, :], NT)
                ds = (p * (dp - delta[h : h + 1, ri])).astype(BF16)
                dv[h] += mm(p.astype(BF16), do3[h, ri, :])
                dk[h, :, : q3.shape[2]] += mm(ds, q3[h, ri, :])
                dqt[h * hd : (h + 1) * hd, ri] += mm(kt3[h, :, rj], ds)
                if tiles is not None:
                    dtile[h, jnp.minimum(apart, 2)] += ds.astype(F32)
            return 0

        lax.fori_loop(first_query(J), 2, qblock, 0)
        put(J)
        between(J)
        return 0

    lax.fori_loop(0, key_end, kblock, 0)


def layer_kernel(dims, names, *refs):
    D, Hl, hd, FFL, N, NE, g, part = dims
    s = types.SimpleNamespace(**dict(zip(names, refs)))
    hw = Hl * hd
    H2 = 2 * Hl
    NC, NQ, NK = 2 * N, 4 * N, 4 * NE
    dp, z = lax.axis_index("dp"), lax.axis_index("mp")
    a, low = dp // g, dp % g
    c, r = a % 2, a // 2
    p, zb = z // 2, z % 2
    j = 2 * c + zb
    rx, ry, rd = r + 1 - 2 * (r % 2), (r + 2) % 4, 3 - r
    z1, z2 = z + 1 - 2 * zb, (z + 2) % 4
    stay, moved = c == p, c != p
    own = jnp.where(stay, z, 3 - z)
    beyond = jnp.where(stay, z1, 3 - z1)
    u_own = own // 2
    lo_block = jnp.minimum(own, 3 - own)
    hi_block = 3 - lo_block

    def device(r_, c_, z_):
        return {"dp": (2 * r_ + c_) * g + low, "mp": z_}

    sibling, across = device(r, 1 - c, z), device(r, c, z1)
    home = device(r, p, 3 - z)
    x_chip, y_chip = device(rx, c, z), device(ry, c, z)
    counter = [0]

    def slots(k):
        counter[0] += k
        return counter[0] - k

    def remote(src, dst, dev, send=None, recv=None):
        send = slots(1) if send is None else send
        recv = slots(1) if recv is None else recv
        return pltpu.make_async_remote_copy(
            src_ref=src, dst_ref=dst, send_sem=s.sems.at[send], recv_sem=s.sems.at[recv],
            device_id=dev, device_id_type=MESH_ID,
        )

    def local(src, dst, sem=None):
        return pltpu.make_async_copy(src, dst, s.sems.at[slots(1) if sem is None else sem])

    def either(cond, yes, no):
        @pl.when(cond)
        def _():
            yes()

        @pl.when(jnp.logical_not(cond))
        def _():
            no()

    unsent = []

    def chain(*steps):
        return steps

    def go(copy):
        copy.start()
        unsent.append(copy)
        return copy

    def block(i, n):
        return pl.ds(pl.multiple_of(i * n, n), n)

    def order(k):
        first = jnp.where(k < 2, own, beyond)
        return jnp.where(k % 2 == 0, first, 3 - first)

    def query_block(u):
        return jnp.where(u == 0, lo_block, hi_block)

    pieces = (s.p_sk, s.p_sv, s.p_sq, s.p_so, s.p_ck, s.p_cv, s.p_cq, s.p_co)
    loads = []
    for k, piece in enumerate(pieces):
        loads.append(local(piece, s.raw_t.at[k // 4] if k % 4 == 3 else s.raw.at[k - k // 4]))
    for k, piece in enumerate((s.p_gate, s.p_up, s.p_down)):
        loads.append(local(piece, s.wpack.at[:, pl.ds(8 * hw + k * FFL, FFL)]))
    for copy in loads:
        copy.start()

    barrier = pltpu.get_barrier_semaphore()
    peers = [device(r, (c + dc) % 2, (z + dz) % 4) for dz in range(4) for dc in range(2) if dz or dc] + [x_chip, y_chip, device(rd, c, z)]
    for peer in peers:
        pl.semaphore_signal(barrier, inc=1, device_id=peer, device_id_type=MESH_ID)
    for copy in loads:
        copy.wait()
    for k in range(8):
        piece = s.raw_t[k // 4].T if k % 4 == 3 else s.raw[k - k // 4]
        s.wpack[:, k * hw : (k + 1) * hw] = piece
    pl.semaphore_wait(barrier, len(peers))

    def swap_halves(src, dst):
        n = src.shape[0] // 2
        return [swap_of(src.at[pl.ds(k * n, n), :], dst.at[pl.ds(k * n, n), :]) for k in range(2)]

    def swap(src, dst):
        start, wait = swap_of(src, dst)
        start()
        return wait

    def swap_of(src, dst):
        far, near = remote(src, dst, home), local(src, dst)
        return chain(lambda: either(moved, far.start, near.start), lambda: either(moved, far.wait, near.wait))

    rows_a = D // 8
    chip = 2 * rows_a

    def spread(A, B):
        def at(ref, w):
            buf, slot, cols = ref
            return buf.at[w, cols] if slot is None else buf.at[slot, w, cols]

        def hop(ref, w, dev):
            return remote(at(ref, w), at(ref, w), dev)

        first = [hop(A, block(r, chip), x_chip), hop(B, block(r, chip), y_chip)]
        last = [hop(A, block(r // 2, 2 * chip), y_chip)] + [hop(B, block(q, chip), x_chip) for q in (r, ry)]

        def first_hop():
            go(first[0])
            go(first[1])

        def second_hop():
            first[0].wait_recv()
            go(last[0])
            first[1].wait_recv()
            go(last[1])
            go(last[2])

        def finish():
            for copy in last:
                copy.wait_recv()

        return first_hop, second_hop, finish

    def attn_weights(col, wide):
        C = pl.ds(col, wide)
        src = s.wpack.at[:, C]
        base = slots(4)
        dst = s.W2.at[zb, block(a, rows_a), C]
        out = [remote(src, dst, device(r, p, z_), None, base + 2 * zb + c) for z_ in (z2, z1)]
        near = local(src, dst)
        beside = remote(src, dst, sibling, None, base + 2 * zb + c)
        at = [s.W2.at[zb, block(2 * r + c_, rows_a), C] for c_ in range(2)]
        pass_on = [remote(at[c_], at[c_], across, None, base + 2 * zb + c_) for c_ in range(2)]
        here = [remote(src, at[0], sibling, 0, base + 2 * zb + c_) for c_ in range(2)]
        there = [remote(src, at[0], sibling, 0, base + 2 * (1 - zb) + c_) for c_ in range(2)]
        first_hop, second_hop, finish = spread((s.W2, 0, C), (s.W2, 1, C))

        def start():
            for copy in out:
                go(copy)
            either(stay, near.start, beside.start)

        def relay():
            def forward():
                beside.wait_send()
                for c_ in range(2):
                    here[c_].wait_recv()
                    pass_on[c_].start()

            def settle():
                near.wait()
                remote_side.wait_recv()

            either(moved, forward, settle)

        remote_side = remote(src, at[0], sibling, 0, base + 2 * zb + 1 - c)

        def first():
            for c_ in range(2):
                there[c_].wait_recv()
            pl.when(moved)(lambda: [copy.wait_send() for copy in pass_on] and None)
            first_hop()

        return chain(start, relay, first, second_hop, finish)

    def ff_weights(col, wide):
        src = s.wpack.at[:, pl.ds(col, wide)]
        dst = s.WF.at[block(a, rows_a), :]
        near, beside = local(src, dst), remote(src, dst, sibling)
        base = slots(2)
        out = remote(src, dst, device(r, p, z2), None, base + c)
        got = [remote(src, dst, sibling, 0, base + k) for k in range(2)]
        half = wide // 2
        first_hop, second_hop, finish = spread((s.WF, None, pl.ds(0, half)), (s.WF, None, pl.ds(half, half)))

        def start():
            go(out)
            either(stay, near.start, beside.start)

        def first():
            @pl.when(stay)
            def _():
                near.wait()
                beside.wait_recv()

            @pl.when(moved)
            def _():
                beside.wait_send()
                for copy in got:
                    copy.wait_recv()

            first_hop()

        return chain(start, first, second_hop, finish)

    def collect(A, B, bufs, send_home):
        ra1, rb1, ra2, rb2 = bufs

        def at(ref, w):
            buf, slot, cols = ref
            return buf.at[w, cols] if slot is None else buf.at[slot, w, cols]

        one = [
            go(remote(at(A, block(ry // 2, 2 * chip)), ra1, y_chip)),
            go(remote(at(B, block(rx, chip)), rb1.at[0], x_chip)),
            go(remote(at(B, block(rd, chip)), rb1.at[1], x_chip)),
        ]
        two = [remote(at(A, block(rx, chip)), ra2, x_chip), remote(at(B, block(ry, chip)), rb2, y_chip)]
        home_steps = send_home()

        def add(dst, src):
            n = 96
            for q in range(src.shape[0] // n):
                w = pl.ds(q * n, n)
                dst[w, :] = (dst[w, :].astype(F32) + src[w, :].astype(F32)).astype(BF16)

        def second():
            one[0].wait_recv()
            add(at(A, block(r // 2, 2 * chip)), ra1)
            go(two[0])
            one[2].wait_recv()
            add(at(B, block(ry, chip)), rb1.at[1])
            go(two[1])
            one[1].wait_recv()
            add(at(B, block(r, chip)), rb1.at[0])

        def third():
            two[0].wait_recv()
            add(at(A, block(r, chip)), ra2)
            two[1].wait_recv()
            add(at(B, block(r, chip)), rb2)
            home_steps[0]()

        return chain(second, third, *home_steps[1:])

    def to_home(grad, out):
        recv, near_recv, near_sem = slots(1), slots(1), slots(1)
        beside = remote(grad(2 * r + 1 - c), out(0), sibling, None, near_recv)
        near = local(grad(a), out(0), near_sem)
        far = [remote(grad(2 * r + k), out(1), device(r, k, z2), None, recv) for k in range(2)]

        def send():
            @pl.when(stay)
            def _():
                beside.start()
                near.start()

            @pl.when(moved)
            def _():
                for copy in far:
                    copy.start()

        def finish():
            @pl.when(stay)
            def _():
                beside.wait_send()
                near.wait()

            @pl.when(moved)
            def _():
                beside.wait_recv()
                for copy in far:
                    copy.wait_send()

            far[0].wait_recv()

        return send, finish

    def attn_home(col, wide, buf):
        C = pl.ds(col, wide)

        def build():
            pair = remote(s.dW2.at[1 - zb, block(r, chip), C], buf, across)
            send, finish = to_home(
                lambda i: s.dW2.at[zb, block(i, rows_a), C], lambda k: s.gz2.at[k, :, C]
            )

            def add_pair():
                pair.wait()
                for q in range(2):
                    w = pl.ds(q * rows_a, rows_a)
                    at = s.dW2.at[zb, block(2 * r + q, rows_a), C]
                    at[...] = (at[...].astype(F32) + buf[w, :].astype(F32)).astype(BF16)
                send()

            return pair.start, add_pair, finish

        return build

    def ff_home():
        return to_home(lambda i: s.dWF.at[block(i, rows_a), :], lambda k: s.gzf.at[k])

    def all_sum(buf, in1, in2):
        base1, base2 = slots(8), slots(4)
        me = 4 * c + z
        one, two = [], []
        for dz in range(4):
            for dc in range(2):
                if dz or dc:
                    c_, z_ = (c + dc) % 2, (z + dz) % 4
                    one.append((remote(in1.at[me], in1.at[me], device(r, c_, z_), None, base1 + me), base1 + 4 * c_ + z_))
        for dr in range(1, 4):
            r_ = (r + dr) % 4
            two.append((remote(in2.at[r], in2.at[r], device(r_, c, z), None, base2 + r), base2 + r_))

        def waits(copies, ref):
            for copy, recv in copies:
                copy.wait_send()
                remote(ref, ref, sibling, 0, recv).wait_recv()

        def start():
            in1[me] = buf[...]
            for copy, _ in one:
                copy.start()

        def middle():
            waits(one, in1.at[0])
            in2[r] = jnp.sum(in1[...], axis=0)
            for copy, _ in two:
                copy.start()

        def finish():
            waits(two, in2.at[0])
            buf[...] = jnp.sum(in2[...], axis=0)

        return chain(start, middle, finish)

    def gather(buf, n):
        half = n // 2
        copies = []
        for k in range(2):
            mine = buf.at[block(2 * own + k, half), :]
            there = buf.at[block(2 * beyond + k, half), :]
            copies.append((remote(mine, mine, across), remote(mine, mine, sibling), remote(there, there, sibling)))

        def start(k):
            copies[k][0].start()
            copies[k][1].start()

        def side():
            for copy in copies:
                copy[1].wait_recv()

        def forward():
            for copy in copies:
                copy[0].wait_recv()
                copy[2].start()

        def far():
            for copy in copies:
                copy[2].wait_recv()
                for one in copy:
                    one.wait_send()

        first, second, side, forward, far = chain(lambda: start(0), lambda: start(1), side, forward, far)
        return types.SimpleNamespace(start=lambda k: (first, second)[k](), side=side, forward=forward, far=far)

    def gather_all(buf, n):
        h = gather(buf, n)
        h.start(0)
        h.start(1)
        return h

    def each_block(h, body):
        h.side()
        lax.fori_loop(0, 2, lambda k, _: (body(order(k)), 0)[1], 0)
        h.forward()
        h.far()
        lax.fori_loop(2, 4, lambda k, _: (body(order(k)), 0)[1], 0)

    def gather_chip(buf):
        copies = []
        for k in range(2):
            mine = buf.at[block(2 * u_own + k, N // 2), :]
            copies.append(remote(mine, mine, sibling))

        def ready():
            for copy in copies:
                copy.wait_recv()

        first, second, ready = chain(lambda: go(copies[0]), lambda: go(copies[1]), ready)
        return (lambda k: (first, second)[k]()), ready

    def scatter(fn, bufs, res):
        s0, s1, zs, r0, r1, rz = bufs
        s0[...] = fn(order(3)).astype(BF16)
        d0 = remote(s0, r0, sibling)
        d0.start()
        res[...] = fn(order(2))
        d0.wait_recv()
        zs[...] = (res[...] + r0[...].astype(F32)).astype(BF16)
        n = res.shape[0] // 2
        parts = [pl.ds(k * n, n) for k in range(2)]
        dz = [remote(zs.at[w, :], rz.at[w, :], across) for w in parts]
        for copy in dz:
            copy.start()
        s1[...] = fn(order(1)).astype(BF16)
        d1 = remote(s1, r1, sibling)
        d1.start()
        res[...] = fn(order(0))

        def finish(k=None):
            for q in (0, 1) if k is None else (k,):
                if q == 0:
                    d1.wait_recv()
                w = parts[q]
                dz[q].wait_recv()
                res[w, :] += r1[w, :].astype(F32) + rz[w, :].astype(F32)
                if q == 1:
                    for copy in (d0, d1, *dz):
                        copy.wait_send()

        steps = chain(lambda: finish(0), lambda: finish(1))
        return lambda k=None: [step() for step in (steps if k is None else steps[k : k + 1])]

    def scatter_chip(fn, s0, r0, res):
        s0[...] = fn(1 - u_own).astype(BF16)
        d0 = remote(s0, r0, sibling)
        d0.start()
        res[...] = fn(u_own)

        def finish():
            d0.wait()
            res[...] += r0[...].astype(F32)

        return chain(finish)[0]

    CH = 64

    def chunks(n, body, init=0, half=None):
        lo, hi = (0, n // CH) if half is None else (half * n // (2 * CH), (half + 1) * n // (2 * CH))
        return lax.fori_loop(lo, hi, lambda i, v: body(pl.ds(pl.multiple_of(i * CH, CH), CH), v), init)

    gains = [s.gains[k : k + 1, :].astype(F32) for k in range(3)]

    def norm_rows(v, which, inv_ref, w, dst, dst_at):
        inv = lax.rsqrt(jnp.sum(v * v, axis=1, keepdims=True) / D + EPS)
        inv_ref[w, :] = jnp.broadcast_to(inv, (CH, 128))
        dst[dst_at, :] = (v * inv * gains[which]).astype(BF16)

    def rows_in(i, w):
        return pl.ds(pl.multiple_of(i * N + w.start, CH), CH)

    def norm_back_rows(d, v, which, inv):
        scaled = d * gains[which]
        dotted = jnp.sum(scaled * v, axis=1, keepdims=True)
        back = inv * scaled - v * (inv * inv * inv * dotted / D)
        return back, jnp.sum(d * v * inv, axis=0, keepdims=True)

    zero_gain = jnp.zeros((1, D), F32)
    o_ff = 8 * hw
    c_q, c_o, c_ckv, c_cq, c_co = 2 * hw, 3 * hw, 4 * hw, 6 * hw, 7 * hw

    w_kv = attn_weights(0, 2 * hw)
    w_qo = attn_weights(2 * hw, 2 * hw)
    swap_x = swap_halves(s.x, s.XN)
    w_kv[0]()
    w_qo[0]()
    for k in range(2):
        swap_x[k][0]()
    s.tab[z] = jnp.zeros_like(s.tab[z])
    s.tab[z, :Hl, :NB] = s.rel_bias[...].astype(F32)
    tab_base = slots(4)
    tab_out = [
        remote(s.tab.at[z], s.tab.at[z], device(r, c, (z + dz) % 4), None, tab_base + z) for dz in range(1, 4)
    ]
    for copy in tab_out:
        go(copy)
    s.len_out[...] = jnp.full(s.len_out.shape, s.seq_lengths[0], jnp.int32).astype(F32)
    lens = go(remote(s.len_out, s.len_in, sibling))
    lens.wait_recv()
    s.len_row[...] = jnp.where(stay, s.len_out[...], s.len_in[...])
    for dz in range(1, 4):
        other = s.tab.at[(z + dz) % 4]
        remote(other, other, sibling, 0, tab_base + (z + dz) % 4).wait_recv()
    span = 2 * TILE
    ids = lax.broadcasted_iota(jnp.int32, (NB, span), 0)
    buckets = s.rel_buckets[...]
    last = jnp.broadcast_to(buckets[:, -1:], (1, span))
    near = buckets[:, :span]
    after = jnp.concatenate([buckets[:, TILE:span], buckets[:, :TILE]], axis=1)

    def onehot(row):
        return (ids == row).astype(F32)

    key_at = lax.broadcasted_iota(jnp.int32, (TILE, TILE), 0)
    query_at = lax.broadcasted_iota(jnp.int32, (TILE, TILE), 1)
    w_kv[1]()
    for q in range(2):
        table = s.tab[2 * c + q, :, :NB]
        for k, row in enumerate((near, after, last)):
            s.vecs[8 * k : 8 * k + 8, :] = mm(table, onehot(row))

        def build(h, _):
            for k in range(3):
                wide = jnp.broadcast_to(s.vecs[pl.ds(8 * k + h, 1), :], (TILE, span))
                tile = pltpu.roll(wide, 0, 1, stride=1, stride_axis=0)[:, :TILE]
                s.tiles[Hl * q + h, k] = (jnp.where(query_at >= key_at, tile, NEG) if k == 0 else tile).astype(BF16)
            return 0

        lax.fori_loop(0, Hl, build, 0)
    w_qo[1]()
    length = s.len_row[0:1, :]
    lane = lax.broadcasted_iota(jnp.int32, (TILE, 128), 1)

    def extra_lane(i, _):
        w = tile_rows(i)
        at = lax.broadcasted_iota(jnp.int32, (TILE, 128), 0) + i * TILE
        mask = jnp.where((lane == hd) & (at.astype(F32) >= length), NEG, 0.0).astype(BF16)
        for h in range(H2):
            s.k3[h, w, :] = mask

        @pl.when(i < 2)
        def _():
            for h in range(H2):
                s.q3[h, w, :] = jnp.where(lane == hd, 1.0, 0.0).astype(BF16)

        return 0

    lax.fori_loop(0, 4, extra_lane, 0)
    ga = gather(s.FIRST, N)
    w_kv[2]()

    def norm_one(w, _):
        norm_rows(s.XN[w, :].astype(F32), 0, s.inv1, w, s.FIRST, rows_in(own, w))
        return 0

    for k in range(2):
        swap_x[k][1]()
        chunks(N, norm_one, 0, k)
        ga.start(k)
        if k == 0:
            w_qo[2]()
    w_kv[3]()
    w_ca = attn_weights(4 * hw, 2 * hw)
    w_cb = attn_weights(6 * hw, 2 * hw)
    w_f = ff_weights(o_ff, 3 * FFL)
    w_ca[0]()
    w_cb[0]()
    w_qo[3]()
    w_ca[1]()
    wait_e = swap(s.enc, s.EN)
    w_cb[1]()
    ga.side()
    ga.forward()
    w_f[0]()
    w_ca[2]()
    ga.far()
    wait_o = swap(s.og, s.ON)
    wait_e()
    s.ENC[block(own, NE), :] = s.EN[...]
    ge = gather_all(s.ENC, NE)
    w_kv[4]()
    w_qo[4]()

    def split(dst, h0, value, rows):
        for h in range(Hl):
            dst[h0 + h, rows, :hd] = value[:, h * hd : (h + 1) * hd]

    def project_one(k, _):
        i = order(k)
        w = block(i, N)
        f = s.FIRST[w, :]
        for q in range(2):
            y = mm(f, s.W2[q, :, : 2 * hw]).astype(BF16)
            split(s.k3, Hl * q, y[:, :hw], w)
            split(s.v3, Hl * q, y[:, hw:], w)

        @pl.when(k < 2)
        def _():
            for q in range(2):
                split(s.q3, Hl * q, mm(f, s.W2[q, :, c_q : c_q + hw]).astype(BF16), block(i // 2, N))

        return 0

    lax.fori_loop(0, 4, project_one, 0)
    w_cb[2]()
    w_ca[3]()

    def turn(dst, src):
        def one(h, _):
            dst[h] = src[h, :, :hd].T
            return 0

        lax.fori_loop(0, H2, one, 0)

    turn(s.t3, s.v3)
    s.WO[...] = s.W2[:, :, c_o : c_o + hw]

    def after_first(u, J):
        @pl.when(jnp.logical_and(u == 1, J == 0))
        def _():
            ge.side()
            ge.forward()
            w_cb[3]()
            w_f[1]()

    fwd_attention(s.q3, s.k3, s.t3, s.out_t, s.lse, H2, query_block, lambda I: I + 1, s.tiles, after_first)
    s.MIX[...] = s.out_t[...].T.astype(BF16)

    def out_proj(mix, weight):
        def fn(u):
            w = block(u, N)
            return mm(mix[w, :hw], weight[0], NT) + mm(mix[w, hw:], weight[1], NT)

        return fn

    end = scatter_chip(out_proj(s.MIX, s.WO), s.s0, s.i0, s.res)
    end()

    def norm_two(w, _):
        v = s.XN[w, :].astype(F32) + s.res[w, :]
        s.MID[w, :] = v
        norm_rows(v, 1, s.inv2, w, s.SECOND, rows_in(u_own, w))
        return 0

    second_go, second_ready = gather_chip(s.SECOND)
    for k in range(2):
        chunks(N, norm_two, 0, k)
        second_go(k)
    wait_o()
    own_pos = lax.broadcasted_iota(jnp.int32, (N, 128), 0) + own * N
    s.ok[...] = (own_pos.astype(F32) < length).astype(F32)

    def mask_rows(w, _):
        s.GF[rows_in(own, w), :] = (s.ON[w, :].astype(F32) * s.ok[w, :1]).astype(BF16)
        return 0

    chunks(N, mask_rows)
    gg = gather_all(s.GF, N)
    ge.far()
    w_ca[4]()

    def project_enc(i, _):
        w = block(i, N)
        e = s.ENC[w, :]
        for q in range(2):
            y = mm(e, s.W2[q, :, c_ckv : c_ckv + 2 * hw]).astype(BF16)
            split(s.ck3, Hl * q, y[:, :hw], w)
            split(s.cv3, Hl * q, y[:, hw:], w)
        return 0

    lax.fori_loop(0, NK // N, project_enc, 0)
    turn(s.ct3, s.cv3)
    w_cb[4]()
    s.WCO[...] = s.W2[:, :, c_co : c_co + hw]
    second_ready()

    def project_two(u, _):
        w = block(u, N)
        t = s.SECOND[w, :]
        for q in range(2):
            split(s.cq3, Hl * q, mm(t, s.W2[q, :, c_cq : c_cq + hw]).astype(BF16), w)
        return 0

    lax.fori_loop(0, 2, project_two, 0)
    def after_cross(u, J):
        @pl.when(jnp.logical_and(u == 0, J == 0))
        def _():
            w_f[2]()

    fwd_attention(
        s.cq3, s.ck3, s.ct3, s.out_t2, s.lse2, H2, query_block, lambda I: NK // TILE, None, after_cross
    )
    s.MIX2[...] = s.out_t2[...].T.astype(BF16)
    scatter_chip(out_proj(s.MIX2, s.WCO), s.s0, s.i1, s.res)()

    def norm_three(w, _):
        v = s.MID[w, :] + s.res[w, :]
        s.LAT[w, :] = v
        norm_rows(v, 2, s.inv3, w, s.THIRD, rows_in(own, w))
        return 0

    gt = gather(s.THIRD, N)
    for k in range(2):
        chunks(N, norm_three, 0, k)
        gt.start(k)
    gg.side()
    gg.forward()
    gg.far()
    w_f[3]()
    root = 0.7978845608028654
    SUB = 128

    def feed(i):
        def sub(u, _):
            w = pl.ds(pl.multiple_of(i * N + u * SUB, SUB), SUB)
            t = s.THIRD[w, :]
            gate = mm(t, s.WF[:, :FFL])
            up = mm(t, s.WF[:, FFL : 2 * FFL])
            dh = mm(s.GF[w, :], s.WF[:, 2 * FFL :])
            sq = gate * gate
            th = jnp.tanh(root * gate * (1.0 + 0.044715 * sq))
            half = 0.5 * (1.0 + th)
            act = gate * half
            slope = half + 0.5 * gate * (1.0 - th * th) * root * (1.0 + 3 * 0.044715 * sq)
            s.HID[w, :] = (act * up).astype(BF16)
            s.DGU[w, :FFL] = (dh * up * slope).astype(BF16)
            s.DGU[w, FFL:] = (dh * act).astype(BF16)
            return 0

        lax.fori_loop(0, N // SUB, sub, 0)

    each_block(gt, feed)
    end = scatter(
        lambda i: mm(s.DGU[block(i, N), :], s.WF[:, : 2 * FFL], NT), (s.s0, s.s1, s.zs, s.a0, s.a1, s.az), s.res
    )

    def weight_grad(put, parts):
        def step(q, _):
            m = pl.ds(pl.multiple_of(q * 256, 256), 256)
            total = None
            for left, right in parts:
                y = mm(left(m), right, TN)
                total = y if total is None else total + y
            put(m, total.astype(BF16))
            return 0

        lax.fori_loop(0, D // 256, step, 0)

    def put_f(col, n):
        def put(m, v):
            s.dWF[m, col : col + n] = v

        return put

    def put_slots(col, n):
        def put(m, v):
            for q in range(2):
                s.dW2[q, m, col : col + n] = v[:, q * n : (q + 1) * n]

        return put

    weight_grad(put_f(2 * FFL, FFL), [(lambda m: s.GF[:, m], s.HID[...])])
    weight_grad(put_f(0, 2 * FFL), [(lambda m: s.THIRD[:, m], s.DGU[...])])
    half_f = 3 * FFL // 2
    grad_f = collect(
        (s.dWF, None, pl.ds(0, half_f)), (s.dWF, None, pl.ds(half_f, half_f)), (s.ra1, s.rb1, s.ra2, s.rb2), ff_home
    )
    turn(s.ct3, s.ck3)
    turn(s.t3, s.k3)
    s.dtile[...] = jnp.zeros_like(s.dtile)

    def back_three(w, acc):
        back, part_gain = norm_back_rows(s.res[w, :], s.LAT[w, :], 2, s.inv3[w, :1])
        d = s.GF[rows_in(own, w), :].astype(F32) + back
        s.GR[w, :] = d
        s.DL[rows_in(u_own, w), :] = d.astype(BF16)
        return acc + part_gain

    dl_go, dl_ready = gather_chip(s.DL)
    gain_three = zero_gain
    for k in range(2):
        end(k)
        gain_three = chunks(N, back_three, gain_three, k)
        dl_go(k)
    end_out = scatter(
        lambda i: mm(s.HID[block(i, N), :], s.WF[:, 2 * FFL :], NT), (s.s0, s.s1, s.zs, s.b0, s.b1, s.bz), s.res
    )


    def back_heads(src, weight, out_t):
        def body(u, _):
            w = block(u, N)
            for q in range(2):
                y = mm(src[w, :], weight[q]).astype(BF16)
                split(s.do3, Hl * q, y, w)
                yt = y.astype(F32).T
                for h in range(Hl):
                    g_h = Hl * q + h
                    both = yt[h * hd : (h + 1) * hd, :] * out_t[g_h * hd : (g_h + 1) * hd, w]
                    s.delta[g_h : g_h + 1, w] = jnp.sum(both, axis=0, keepdims=True)
            return 0

        lax.fori_loop(0, 2, body, 0)

    dl_ready()
    back_heads(s.DL, s.WCO, s.out_t2)

    def put_cross(J):
        w = tile_rows(J)
        for h in range(H2):
            q, hh = h // Hl, h % Hl
            at = 2 * hw * q + hh * hd
            s.DGU[w, at : at + hd] = s.dk[h, :, :hd].astype(BF16)
            s.DGU[w, at + hw : at + hw + hd] = s.dv[h].astype(BF16)

    def cross_between(J):
        @pl.when(J == 0)
        def _():
            grad_f[0]()

    bwd_attention(
        s.cq3, s.ck3, s.cv3, s.ct3, s.do3, s.lse2, s.delta, s.out_t2, s.dk, s.dv, put_cross, H2, query_block,
        lambda J: 0, NK // TILE, None, None, cross_between,
    )
    s.DQ[...] = s.out_t2[...].T.astype(BF16)

    def query_grad(col):
        def fn(u):
            w = block(u, N)
            return mm(s.DQ[w, :hw], s.W2[0, :, col : col + hw], NT) + mm(s.DQ[w, hw:], s.W2[1, :, col : col + hw], NT)

        return fn

    def put_out(w, _):
        s.ON[w, :] = (s.LAT[w, :] + s.res[w, :]).astype(BF16)
        return 0

    end_out()
    chunks(N, put_out)
    wait_lo = swap(s.ON, s.lo)
    end = scatter_chip(query_grad(c_cq), s.s0, s.i2, s.res)

    def kv_grad(n, col):
        def fn(i):
            w = block(i, n)
            return (
                mm(s.DGU[w, : 2 * hw], s.W2[0, :, col : col + 2 * hw], NT)
                + mm(s.DGU[w, 2 * hw : 4 * hw], s.W2[1, :, col : col + 2 * hw], NT)
            )

        return fn

    weight_grad(put_slots(c_cq, hw), [(lambda m: s.SECOND[:, m], s.DQ[...])])
    weight_grad(put_slots(c_co, hw), [(lambda m: s.DL[:, m], s.MIX2[...])])
    weight_grad(put_slots(c_ckv, 2 * hw), [(lambda m: s.ENC[:, m], s.DGU[:NK, : 4 * hw])])
    grad_f[1]()
    C4 = pl.ds(4 * hw, 4 * hw)
    grad_c = collect((s.dW2, 0, C4), (s.dW2, 1, C4), (s.qa1, s.qb1, s.qa2, s.qb2), attn_home(4 * hw, 4 * hw, s.pair1))
    end()

    def back_two(w, acc):
        back, part_gain = norm_back_rows(s.res[w, :], s.MID[w, :], 1, s.inv2[w, :1])
        d = s.GR[w, :] + back
        s.GR[w, :] = d
        s.DM[rows_in(u_own, w), :] = d.astype(BF16)
        return acc + part_gain

    dm_go, dm_ready = gather_chip(s.DM)
    gain_two = zero_gain
    for k in range(2):
        gain_two = chunks(N, back_two, gain_two, k)
        dm_go(k)
    end_enc = scatter(kv_grad(NE, c_ckv), (s.e0, s.e1, s.es, s.f0, s.f1, s.fz), s.rese)
    end_enc()
    s.EN[...] = s.rese[...].astype(BF16)
    wait_eo = swap(s.EN, s.eg)

    dm_ready()
    back_heads(s.DM, s.WO, s.out_t)
    weight_grad(put_slots(c_o, hw), [(lambda m: s.DM[:, m], s.MIX[...])])

    def self_between(J):
        @pl.when(J == 0)
        def _():
            grad_c[0]()

    bwd_attention(
        s.q3, s.k3, s.v3, s.t3, s.do3, s.lse, s.delta, s.out_t, s.dk, s.dv, put_cross, H2, query_block,
        lambda J: jnp.where(J <= lo_block, 0, 1), hi_block + 1, s.tiles, s.dtile, self_between,
    )

    def clear(J, _):
        s.DGU[tile_rows(J), :] = jnp.zeros((TILE, s.DGU.shape[1]), BF16)
        return 0

    lax.fori_loop(hi_block + 1, 4, clear, 0)
    s.DQ[...] = s.out_t[...].T.astype(BF16)
    own_part = query_grad(c_q)
    other_part = kv_grad(N, 0)

    def scatter_first(bufs, res, filler):
        s0, s1, zs, r0, r1, rz = bufs
        s0[...] = other_part(order(3)).astype(BF16)
        d0 = remote(s0, r0, sibling)
        d0.start()
        res[...] = other_part(order(2))
        d0.wait_recv()
        zs[...] = (res[...] + r0[...].astype(F32)).astype(BF16)
        n = res.shape[0] // 2
        parts = [pl.ds(k * n, n) for k in range(2)]
        dz = [remote(zs.at[w, :], rz.at[w, :], across) for w in parts]
        for copy in dz:
            copy.start()
        filler()
        s1[...] = (other_part(3 - own) + own_part(1 - u_own)).astype(BF16)
        d1 = remote(s1, r1, sibling)
        d1.start()
        res[...] = other_part(own) + own_part(u_own)

        def finish(k=None):
            for q in (0, 1) if k is None else (k,):
                if q == 0:
                    d1.wait_recv()
                w = parts[q]
                dz[q].wait_recv()
                res[w, :] += r1[w, :].astype(F32) + rz[w, :].astype(F32)
                if q == 1:
                    for copy in (d0, d1, *dz):
                        copy.wait_send()

        steps = chain(lambda: finish(0), lambda: finish(1))
        return lambda k=None: [step() for step in (steps if k is None else steps[k : k + 1])]

    KV, QO = pl.ds(0, 2 * hw), pl.ds(2 * hw, 2 * hw)
    bufs = (s.ra1, s.rb1, s.ra2, s.rb2)
    cut = lambda k: tuple(x.at[..., pl.ds(k * 2 * hw, 2 * hw)] for x in bufs)
    grad_c[1]()
    weight_grad(put_slots(0, 2 * hw), [(lambda m: s.FIRST[:, m], s.DGU[:, : 4 * hw])])
    grad_kv = collect((s.dW2, 0, KV), (s.dW2, 1, KV), cut(0), attn_home(0, 2 * hw, s.pair2))
    query_part = []

    def query_grads():
        weight_grad(
            put_slots(c_q, hw),
            [
                (lambda m: s.FIRST[tile_rows(lo_block), m], s.DQ[:N, :]),
                (lambda m: s.FIRST[tile_rows(hi_block), m], s.DQ[N:, :]),
            ],
        )
        query_part.append(collect((s.dW2, 0, QO), (s.dW2, 1, QO), cut(1), attn_home(2 * hw, 2 * hw, s.pair3)))

    end = scatter_first((s.s0, s.s1, s.zs, s.a0, s.a1, s.az), s.res, query_grads)
    grad_qo = query_part[0]
    grad_c[2]()
    grad_kv[0]()
    def back_one(w, acc):
        back, part_gain = norm_back_rows(s.res[w, :], s.XN[w, :].astype(F32), 0, s.inv1[w, :1])
        s.i0[w, :] = (s.GR[w, :] + back).astype(BF16)
        return acc + part_gain

    swap_dg = swap_halves(s.i0, s.dg)
    wait_dg = [pair[1] for pair in swap_dg]
    gain_one = zero_gain
    for k in range(2):
        end(k)
        gain_one = chunks(N, back_one, gain_one, k)
        swap_dg[k][0]()
    grad_qo[0]()
    s.small[...] = jnp.zeros_like(s.small)
    flip = (key_at + query_at == TILE - 1).astype(BF16)
    blank = jnp.zeros((TILE, TILE), F32)
    head_row = lax.broadcasted_iota(jnp.int32, (16, span), 0)
    gap = lax.broadcasted_iota(jnp.int32, (1, span), 1)
    near_back = jnp.where(gap >= TILE - 1, pltpu.roll(near, TILE - 1, 1), -1)
    next_back = jnp.where(gap < span - 1, pltpu.roll(near, span - 1, 1), -1)
    for k, row in enumerate((near_back, next_back)):

        def line_up(h, diag):
            full = s.dtile[h, k]
            high = full.astype(BF16)
            rest = full - high.astype(F32)
            mid = rest.astype(BF16)
            turned = mm(flip, high) + mm(flip, mid) + mm(flip, (rest - mid.astype(F32)).astype(BF16))
            lined = pltpu.roll(jnp.concatenate([turned, blank], axis=1), 0, 1, stride=1, stride_axis=0)
            return jnp.where(head_row == H2 * c + h, jnp.sum(lined, axis=0, keepdims=True), diag)

        diag = lax.fori_loop(0, H2, line_up, jnp.zeros((16, span), F32))
        s.small[:16, :NB] += lax.dot_general(
            diag, onehot(row), NT, precision=lax.Precision.HIGHEST, preferred_element_type=F32
        )
    far_row = lax.broadcasted_iota(jnp.int32, (16, 1), 0)

    def far_total(h, acc):
        total = jnp.sum(jnp.sum(s.dtile[h, 2], axis=0, keepdims=True), axis=1, keepdims=True)
        return jnp.where(far_row == H2 * c + h, total, acc)

    far_sum = lax.fori_loop(0, H2, far_total, jnp.zeros((16, 1), F32))
    is_last = (lax.broadcasted_iota(jnp.int32, (1, NB), 1) == buckets[:, -1:]).astype(F32)
    s.small[:16, :NB] += far_sum * is_last

    def put_rows(buf, at, row):
        for k in range(D // 128):
            buf[at + k : at + k + 1, :] = row[:, 128 * k : 128 * (k + 1)]

    put_rows(s.small, 16, gain_two)
    put_rows(s.small, 24, gain_three)
    sum_small = all_sum(s.small, s.small1, s.small2)
    sum_small[0]()
    s.late[...] = jnp.zeros_like(s.late)
    put_rows(s.late, 0, gain_one)
    sum_late = all_sum(s.late, s.late1, s.late2)
    sum_late[0]()
    grad_kv[1]()
    sum_small[1]()
    grad_qo[1]()
    sum_late[1]()
    grad_kv[2]()
    sum_small[2]()
    grad_qo[2]()
    sum_late[2]()
    s.sm[...] = jnp.zeros_like(s.sm)
    for k in range(D // 128):
        w = slice(128 * k, 128 * (k + 1))
        s.sm[0:1, w] = s.late[k : k + 1, :]
        s.sm[1:2, w] = s.small[16 + k : 17 + k, :]
        s.sm[2:3, w] = s.small[24 + k : 25 + k, :]
    s.sm[:, D:] = s.small[:16, :]
    wait_lo()
    wait_eo()
    grad_f[2]()
    grad_c[3]()
    grad_kv[3]()
    for wait in wait_dg:
        wait()
    grad_qo[3]()
    for copy in unsent:
        copy.wait_send()
    assert counter[0] <= part, counter[0]


def layer_call(pieces, x, enc, og, gains, rel_bias, seq_lengths, rel_buckets, dims):
    D, Hl, hd, FFL, N, NE, g, part = dims
    hw = Hl * hd
    H2, NC, NQ, NK = 2 * Hl, 2 * N, 4 * N, 4 * NE
    ra = D // 8
    vm, any_ = pl.BlockSpec(memory_space=pltpu.VMEM), pl.BlockSpec(memory_space=pl.ANY)
    sm_ = pl.BlockSpec(memory_space=pltpu.SMEM)
    piece_names = ("p_sk", "p_sv", "p_sq", "p_so", "p_ck", "p_cv", "p_cq", "p_co", "p_gate", "p_up", "p_down")
    ins = dict({k: any_ for k in piece_names}, x=any_, enc=any_, og=any_, gains=vm, rel_bias=vm, seq_lengths=sm_, rel_buckets=vm)
    outs = dict(
        lo=((N, D), BF16, any_), dg=((N, D), BF16, any_), eg=((NE, D), BF16, any_),
        gz2=((2, ra, 8 * hw), BF16, any_), gzf=((2, ra, 3 * FFL), BF16, any_), sm=((16, D + 128), F32, vm),
    )
    sc = {}

    def add(dtype, **shapes):
        for name, shape in shapes.items():
            sc[name] = pltpu.VMEM(shape, dtype)

    add(BF16, wpack=(ra, 8 * hw + 3 * FFL), raw=(6, ra, hw), raw_t=(2, hw, ra))
    add(BF16, pair1=(D // 4, 4 * hw), pair2=(D // 4, 2 * hw), pair3=(D // 4, 2 * hw))
    add(BF16, W2=(2, D, 8 * hw), dW2=(2, D, 8 * hw), WF=(D, 3 * FFL), dWF=(D, 3 * FFL), WO=(2, D, hw), WCO=(2, D, hw))
    for k in "rq":
        add(BF16, **{k + "a1": (D // 2, 4 * hw), k + "b1": (2, D // 4, 4 * hw), k + "a2": (D // 4, 4 * hw), k + "b2": (D // 4, 4 * hw)})
    add(BF16, FIRST=(NQ, D), THIRD=(NQ, D), GF=(NQ, D), SECOND=(NC, D), DL=(NC, D), DM=(NC, D), ENC=(NK, D))
    add(BF16, **{k: (N, D) for k in ("s0", "s1", "zs", "a0", "a1", "az", "b0", "b1", "bz", "i0", "i1", "i2", "XN", "ON")})
    add(BF16, **{k: (NE, D) for k in ("e0", "e1", "es", "f0", "f1", "fz", "EN")})
    add(F32, **{k: (N, D) for k in ("MID", "LAT", "GR", "res")}, rese=(NE, D))
    add(F32, inv1=(N, 128), inv2=(N, 128), inv3=(N, 128), ok=(N, 128))
    add(BF16, q3=(H2, NC, 128), k3=(H2, NQ, 128), v3=(H2, NQ, hd), cq3=(H2, NC, hd), ck3=(H2, NK, hd), cv3=(H2, NK, hd))
    add(BF16, do3=(H2, NC, hd), t3=(H2, hd, NQ), ct3=(H2, hd, NK))
    add(F32, out_t=(2 * hw, NC), out_t2=(2 * hw, NC), lse=(8, NC), lse2=(8, NC), delta=(8, NC))
    add(F32, dk=(H2, TILE, 128), dv=(H2, TILE, hd))
    add(BF16, MIX=(NC, 2 * hw), MIX2=(NC, 2 * hw), HID=(NQ, FFL), DGU=(NQ, 2 * FFL), DQ=(NC, 2 * hw))
    add(BF16, tiles=(H2, 3, TILE, TILE))
    add(F32, dtile=(H2, 3, TILE, TILE), vecs=(24, 2 * TILE))
    add(F32, tab=(4, 8, 128), len_out=(8, 128), len_in=(8, 128), len_row=(8, 128))
    add(F32, small=(32, 128), small1=(8, 32, 128), small2=(4, 32, 128))
    add(F32, late=(8, 128), late1=(8, 8, 128), late2=(4, 8, 128))
    names = list(ins) + list(outs) + list(sc) + ["sems"]
    return pl.pallas_call(
        functools.partial(layer_kernel, dims, names),
        out_shape=[jax.ShapeDtypeStruct(o[0], o[1]) for o in outs.values()],
        in_specs=list(ins.values()),
        out_specs=[o[2] for o in outs.values()],
        scratch_shapes=list(sc.values()) + [pltpu.SemaphoreType.DMA((part,))],
        compiler_params=pltpu.CompilerParams(collective_id=0, has_side_effects=True, vmem_limit_bytes=67043328),
        name="layer",
    )(*pieces, x, enc, og, gains, rel_bias, seq_lengths, rel_buckets)


def finish_kernel(dims, lo, dg, eg, gz2, gzf, sm, *outs):
    D, Hl, hd, FFL, N, NE, g, part = dims
    hw = Hl * hd
    o_lo, o_dg, o_eg, o_gains, o_bias, sq, sk, sv, so, cq, ck, cv, co, gg, gu, gd = outs
    o_lo[...] = lo[...]
    o_dg[...] = dg[...].astype(F32)
    o_eg[...] = eg[...].astype(F32)
    o_gains[...] = sm[:3, :D]
    o_bias[...] = sm[: 4 * Hl, D : D + NB]

    def total(col, n):
        w = pl.ds(col, n)
        return gz2[0, :, w].astype(F32) + gz2[1, :, w].astype(F32)

    for base, parts in ((0, (sk, sv, sq, so)), (4 * hw, (ck, cv, cq, co))):
        y = total(base, 4 * hw)
        for k, out in enumerate(parts):
            v = y[:, k * hw : (k + 1) * hw]
            out[...] = v if k < 3 else v.T
    f = gzf[0].astype(F32) + gzf[1].astype(F32)
    gg[...] = f[:, :FFL]
    gu[...] = f[:, FFL : 2 * FFL]
    gd[...] = f[:, 2 * FFL :]


def finish_call(dims, lo, dg, eg, gz2, gzf, sm):
    D, Hl, hd, FFL, N, NE, g, part = dims
    hw, ra = Hl * hd, D // 8
    vm = pl.BlockSpec(memory_space=pltpu.VMEM)
    shapes = [((N, D), BF16), ((N, D), F32), ((NE, D), F32), ((3, D), F32), ((4 * Hl, NB), F32)]
    shapes += [((ra, hw), F32)] * 3 + [((hw, ra), F32)] + [((ra, hw), F32)] * 3 + [((hw, ra), F32)]
    shapes += [((ra, FFL), F32)] * 3
    return pl.pallas_call(
        functools.partial(finish_kernel, dims),
        out_shape=[jax.ShapeDtypeStruct(*v) for v in shapes],
        in_specs=[vm] * 6,
        out_specs=[vm] * len(shapes),
        name="finish",
    )(lo, dg, eg, gz2, gzf, sm)


def exchange(value, step, size):
    return lax.ppermute(value, "dp", [(i, i ^ step) for i in range(size)])


def per_device(
    decoder_in, encoder_out, seq_lengths, rel_buckets, norm_gains, rel_bias,
    self_query, self_key, self_value, self_out, cross_query, cross_key, cross_value, cross_out,
    gate_weight, up_weight, down_weight, out_grad,
):
    width = decoder_in.shape[1]
    heads, w, f = rel_bias.shape[1], self_query.shape[1], gate_weight.shape[1]
    size = lax.axis_size("dp")
    g = size // 8
    rows, erows = decoder_in.shape[0], encoder_out.shape[0]
    pieces = (
        self_key, self_value, self_query, self_out, cross_key, cross_value, cross_query, cross_out,
        gate_weight, up_weight, down_weight.T,
    )
    if g > 1:
        wpack = jnp.concatenate([x.T if k in (3, 7) else x for k, x in enumerate(pieces)], axis=1)
        step = 1
        while step < g:
            other = exchange(wpack, step, size)
            upper = (lax.axis_index("dp") // step) % 2
            wpack = jnp.where(upper == 1, jnp.concatenate([other, wpack], 0), jnp.concatenate([wpack, other], 0))
            step *= 2
        cols = [wpack[:, k * w : (k + 1) * w] for k in range(8)]
        cols[3], cols[7] = cols[3].T, cols[7].T
        pieces = (*cols, *(wpack[:, 8 * w + k * f : 8 * w + (k + 1) * f] for k in range(3)))
    dims = (width, heads, w // heads, f, rows, erows, g, 480)
    lo, dg, eg, gz2, gzf, sm = layer_call(
        pieces, decoder_in, encoder_out, out_grad, norm_gains, rel_bias.T, seq_lengths, rel_buckets.reshape(1, -1), dims
    )
    if g == 1:
        outs = list(finish_call(dims, lo, dg, eg, gz2, gzf, sm))
        outs[4], outs[15] = outs[4].T, outs[15].T
        return tuple(outs)
    gw = jnp.concatenate([jnp.sum(gz2.astype(F32), axis=0), jnp.sum(gzf.astype(F32), axis=0)], axis=1)
    step = g // 2
    while step >= 1:
        upper = (lax.axis_index("dp") // step) % 2
        n = gw.shape[0] // 2
        keep = jnp.where(upper == 1, gw[n:], gw[:n])
        give = jnp.where(upper == 1, gw[:n], gw[n:])
        gw = keep + exchange(give, step, size)
        sm = sm + exchange(sm, step, size)
        step //= 2
    col = lambda k: gw[:, k * w : (k + 1) * w]
    return (
        lo, dg.astype(F32), eg.astype(F32), sm[:3, :width], sm[: 4 * heads, width : width + NB].T,
        col(2), col(0), col(1), col(3).T, col(6), col(4), col(5), col(7).T,
        gw[:, 8 * w : 8 * w + f], gw[:, 8 * w + f : 8 * w + 2 * f], gw[:, 8 * w + 2 * f :].T,
    )


def solution(mesh):
    return jax.shard_map(
        per_device,
        mesh=mesh,
        in_specs=(
            P(("dp", "mp"), None),
            P(("dp", "mp"), None),
            P("dp"),
            P(),
            P(),
            P(None, "mp"),
            P("dp", "mp"),
            P("dp", "mp"),
            P("dp", "mp"),
            P("mp", "dp"),
            P("dp", "mp"),
            P("dp", "mp"),
            P("dp", "mp"),
            P("mp", "dp"),
            P("dp", "mp"),
            P("dp", "mp"),
            P("mp", "dp"),
            P(("dp", "mp"), None),
        ),
        out_specs=(
            P(("dp", "mp"), None),
            P(("dp", "mp"), None),
            P(("dp", "mp"), None),
            P(),
            P(),
            P("dp", "mp"),
            P("dp", "mp"),
            P("dp", "mp"),
            P("mp", "dp"),
            P("dp", "mp"),
            P("dp", "mp"),
            P("dp", "mp"),
            P("mp", "dp"),
            P("dp", "mp"),
            P("dp", "mp"),
            P("mp", "dp"),
        ),
        check_vma=False,
    )
```
